32 devices in a mesh: batch: 8 (over y, x, core), mem: 4 (over z).
Axes of the slice: x: 2, y: 2, z: 4, core: 2. Of those that a mesh axis runs over, the one named last changes fastest.
Arguments:
- content_in: bfloat16 [32, 512, 768], P(('batch', 'mem')), may hold values from -6 to 6
- query_in: bfloat16 [32, 512, 768], P(('batch', 'mem')), may hold values from -6 to 6
- memory: bfloat16 [32, 384, 768], P('batch', 'mem'), may hold values from -6 to 6
- sequence_lengths: int32 [32], P(('batch', 'mem')), may hold values from 1 to 512, 12288 in all
- order_rank: int32 [32, 512], P(('batch', 'mem')), may hold values from 0 to 511, each once within a row
- segment_ids: int32 [32, 512], P(('batch', 'mem')), may hold values from 0 to 1
- w_query: bfloat16 [768, 768], replicated, may hold values from -0.21875 to 0.21875
- w_key: bfloat16 [768, 768], replicated, may hold values from -0.21875 to 0.21875
- w_value: bfloat16 [768, 768], replicated, may hold values from -0.21875 to 0.21875
- w_out: bfloat16 [768, 768], replicated, may hold values from -1.75 to 1.75
- w_rel: bfloat16 [768, 768], replicated, may hold values from -0.21875 to 0.21875
- bias_content: bfloat16 [768], replicated, may hold values from -3 to 3
- bias_position: bfloat16 [768], replicated, may hold values from -3 to 3
- bias_segment: bfloat16 [768], replicated, may hold values from -3 to 3
- segment_embed: bfloat16 [2, 768], replicated, may hold values from -5 to 5
- gain_one: bfloat16 [768], replicated, may hold values from 0.5 to 1.5
- shift_one: bfloat16 [768], replicated, may hold values from -2 to 2
- w_inner: bfloat16 [768, 3072], replicated, may hold values from -0.21875 to 0.21875
- bias_inner: bfloat16 [3072], replicated, may hold values from -2 to 2
- w_outer: bfloat16 [3072, 768], replicated, may hold values from -0.109375 to 0.109375
- bias_outer: bfloat16 [768], replicated, may hold values from -2 to 2
- gain_two: bfloat16 [768], replicated, may hold values from 0.5 to 1.5
- shift_two: bfloat16 [768], replicated, may hold values from -2 to 2
- content_cotangent: bfloat16 [32, 512, 768], P(('batch', 'mem')), may hold values from -6 to 6
- query_cotangent: bfloat16 [32, 512, 768], P(('batch', 'mem')), may hold values from -6 to 6
Outputs:
- content_out: bfloat16 [32, 512, 768], P(('batch', 'mem'))
- query_out: bfloat16 [32, 512, 768], P(('batch', 'mem'))
- grad_content_in: bfloat16 [32, 512, 768], P(('batch', 'mem'))
- grad_query_in: bfloat16 [32, 512, 768], P(('batch', 'mem'))
- grad_w_query: float32 [768, 768], replicated
- grad_w_key: float32 [768, 768], replicated
- grad_w_value: float32 [768, 768], replicated
- grad_w_out: float32 [768, 768], replicated
- grad_w_rel: float32 [768, 768], replicated
- grad_bias_content: float32 [768], replicated
- grad_bias_position: float32 [768], replicated
- grad_bias_segment: float32 [768], replicated
- grad_segment_embed: float32 [2, 768], replicated
- grad_gain_one: float32 [768], replicated
- grad_shift_one: float32 [768], replicated
- grad_w_inner: float32 [768, 3072], replicated
- grad_bias_inner: float32 [3072], replicated
- grad_w_outer: float32 [3072, 768], replicated
- grad_bias_outer: float32 [768], replicated
- grad_gain_two: float32 [768], replicated
- grad_shift_two: float32 [768], replicated
The draws below stay inside these ranges and needn't reach their ends.
Inputs may be any that keep to these rules, and one draw needn't show every extreme that they name: `sequence_lengths`: the number of live current tokens of each sequence; over all sequences they sum to 12288, and one sequence has all 512. `order_rank`: each row is a permutation of 0 to 511.
All inputs are finite; a program needn't handle non-finite values. No bound on the sum of `sequence_lengths` on one device may be relied on, other than what follows from the above.
Results may differ from the reference program's by a relative error of at most 0.03.
Values may be sent and summed in bfloat16 or wider, within the bound.
No kernel may reach another device: no remote copies, remote signals or barrier semaphores. Data moves between devices by JAX's collectives and lax.ppermute only.
A program may use at most 448 MiB of HBM per device.

```python
import math
import jax
import jax.numpy as jnp
import numpy as np
from jax import lax

D = 768
HEADS = 12
FF = 3072
HEAD = 64
SEG = 512
MEM = 384
SEQS = 32


def set_ends(drawn, own_key, low, top_value):
    place = [jax.random.randint(jax.random.fold_in(own_key, axis), (), 0, length) for axis, length in enumerate(drawn.shape)]
    longest = drawn.shape.index(max(drawn.shape))
    beside = place[:longest] + [(place[longest] + 1) % drawn.shape[longest]] + place[longest + 1:]
    return drawn.at[tuple(place)].set(low).at[tuple(beside)].set(top_value)


def shard_levels(key, dims, cuts, least, largest):
    def one(dim, shards_of):
        steps = jax.random.uniform(jax.random.fold_in(jax.random.fold_in(key, 6), dim), (shards_of,), jnp.float32, least / len(cuts), largest / len(cuts))
        return jnp.repeat(jnp.exp(steps), dims[dim] // shards_of).reshape((-1,) + (1,) * (len(dims) - dim - 1))

    loudness = one(*cuts[0])
    for cut in cuts[1:]:
        loudness = loudness * one(*cut)
    return loudness


def length_profile(count, total, bound, skew):
    loads = [(1 << 20) // math.isqrt(rank ** skew) + 1 for rank in range(2, count + 1)]
    rest, holding = total - bound - (count - 1), [1] * (count - 1)
    while rest > 0:
        movable = [i for i in range(count - 1) if holding[i] < bound]
        whole, remaining = sum([loads[i] for i in movable]), rest
        for i in movable:
            extra = min(bound - holding[i], max(1, remaining * loads[i] // whole), rest)
            holding[i] = holding[i] + extra
            rest = rest - extra
    return np.array([bound] + holding)


def ragged_sizes(stream_key, count, total, bound, lean):
    if count == 2:
        one = jax.random.randint(stream_key, (), max(1, total - bound), min(bound, total - 1) + 1)
        return jnp.stack([one, total - one])
    lengths = jnp.asarray(length_profile(count, total, bound, lean), jnp.int32)
    couples = (count - 1) // 2
    giver, receiver = lengths[1:1 + 2 * couples:2], lengths[2:2 + 2 * couples:2]
    margin = jnp.minimum(giver - 1, bound - receiver)
    moved = jax.random.randint(jax.random.fold_in(stream_key, 1), (couples,), 0, 1 << 20) % (margin + 1)
    lengths = lengths.at[1:1 + 2 * couples:2].set(giver - moved).at[2:2 + 2 * couples:2].set(receiver + moved)
    return lengths[jax.random.permutation(jax.random.fold_in(stream_key, 2), count)]


def noise(key, extent, spread, most, split=(), kind=jnp.bfloat16):
    factor_of = shard_levels(key, extent, split, -0.22, 0.18) if split else 1.0
    values = jax.random.normal(key, extent, jnp.float32) * spread * factor_of
    return jnp.minimum(jnp.maximum(values, -most), most).astype(kind)


def setup_inputs(seed: int = 0) -> dict:
    key_of = jax.random.split(jax.random.key(seed), 26)
    content_in = noise(key_of[0], (SEQS, SEG, D), 1.0, 6.0, ((0, 32),))
    query_in = noise(key_of[1], (SEQS, SEG, D), 1.0, 6.0, ((0, 32),))
    memory = noise(key_of[2], (SEQS, MEM, D), 1.0, 6.0, ((0, 8), (1, 4)))
    sequence_lengths = ragged_sizes(key_of[3], SEQS, 3 * SEQS * SEG // 4, SEG, 0).astype(jnp.int32)
    order_rank = jax.vmap(lambda own: jax.random.permutation(own, SEG))(jax.random.split(key_of[4], SEQS)).reshape((SEQS, SEG)).astype(jnp.int32)
    segment_ids = set_ends(jax.random.randint(key_of[5], (SEQS, SEG), 0, 2), jax.random.fold_in(key_of[5], 1), 0, 1).astype(jnp.int32)
    w_query = noise(key_of[6], (D, D), D ** -0.5, 0.21875)
    w_key = noise(key_of[7], (D, D), D ** -0.5, 0.21875)
    w_value = noise(key_of[8], (D, D), D ** -0.5, 0.21875)
    w_out = noise(key_of[9], (D, D), (max(D // 64, 1)) ** -0.5, 1.75)
    w_rel = noise(key_of[10], (D, D), D ** -0.5, 0.21875)
    bias_content = noise(key_of[11], (D,), 0.5, 3.0)
    bias_position = noise(key_of[12], (D,), 0.5, 3.0)
    bias_segment = noise(key_of[13], (D,), 0.5, 3.0)
    segment_embed = noise(key_of[14], (2, D), 1.0, 5.0)
    gain_one = jnp.clip(1.0 + 0.1 * jax.random.normal(key_of[15], (D,), jnp.float32), 0.5, 1.5).astype(jnp.bfloat16)
    shift_one = noise(key_of[16], (D,), 0.3, 2.0)
    w_inner = noise(key_of[17], (D, FF), D ** -0.5, 0.21875)
    bias_inner = noise(key_of[18], (FF,), 0.3, 2.0)
    w_outer = noise(key_of[19], (FF, D), FF ** -0.5, 0.109375)
    bias_outer = noise(key_of[20], (D,), 0.3, 2.0)
    gain_two = jnp.clip(1.0 + 0.1 * jax.random.normal(key_of[21], (D,), jnp.float32), 0.5, 1.5).astype(jnp.bfloat16)
    shift_two = noise(key_of[22], (D,), 0.3, 2.0)
    content_cotangent = noise(key_of[23], (SEQS, SEG, D), 1.0, 6.0, ((0, 32),))
    query_cotangent = noise(key_of[24], (SEQS, SEG, D), 1.0, 6.0, ((0, 32),))
    return dict(content_in=content_in, query_in=query_in, memory=memory, sequence_lengths=sequence_lengths, order_rank=order_rank, segment_ids=segment_ids, w_query=w_query, w_key=w_key, w_value=w_value, w_out=w_out, w_rel=w_rel, bias_content=bias_content, bias_position=bias_position, bias_segment=bias_segment, segment_embed=segment_embed, gain_one=gain_one, shift_one=shift_one, w_inner=w_inner, bias_inner=bias_inner, w_outer=w_outer, bias_outer=bias_outer, gain_two=gain_two, shift_two=shift_two, content_cotangent=content_cotangent, query_cotangent=query_cotangent)


@jax.custom_vjp
def low(v):
    return lax.optimization_barrier(v.astype(jnp.bfloat16)).astype(jnp.float32)

@jax.custom_vjp
def low_back(v):
    return v

def low_keep(v):
    return (low(v), None)

def low_pass(kept, grad):
    return (grad,)

def back_keep(v):
    return (v, None)

def back_low(kept, grad):
    return (low(grad),)
low.defvjp(low_keep, low_pass)
low_back.defvjp(back_keep, back_low)
norm_epsilon = 1e-06
highest = lax.Precision.HIGHEST

def rounded_both(tensor):
    return low(low_back(tensor))

def layer_norm(tensor, norm_gain, norm_shift):
    centred = tensor - lax.optimization_barrier(jnp.mean(tensor, axis=-1, keepdims=True))
    variance = lax.optimization_barrier(jnp.mean(centred * centred, axis=-1, keepdims=True))
    return centred * lax.rsqrt(variance + norm_epsilon) * norm_gain + norm_shift

def sinusoid(memory_count, segment_count, feature_count):
    distance = (memory_count + segment_count - 1 - jnp.arange(memory_count + 2 * segment_count - 1, dtype=jnp.int32)).astype(jnp.float32)
    frequency = 1.0 / 10000.0 ** (jnp.arange(0, feature_count, 2, dtype=jnp.int32).astype(jnp.float32) / feature_count)
    phases = distance[:, None] * frequency[None, :]
    return jnp.concatenate([jnp.sin(phases), jnp.cos(phases)], axis=1)

def relative_shift(score_grid):
    head_count, row_count, column_count = score_grid.shape
    flattened = score_grid.reshape(head_count, row_count * column_count)[:, row_count - 1:row_count - 1 + row_count * (column_count - 1)]
    return flattened.reshape(head_count, row_count, column_count - 1)[:, :, :column_count - row_count + 1]

def sequence_layer(weights, content, query_rows, memory_rows, length, order_row, segment):
    w_query, w_key, w_value, w_out, w_rel, bias_content, bias_position, bias_segment, segment_embed, gain_one, shift_one, w_inner, bias_inner, w_outer, bias_outer, gain_two, shift_two = weights
    key_count = MEM + SEG
    relative_count = MEM + 2 * SEG - 1
    frame_rows = jnp.concatenate([memory_rows, content], axis=0)
    key_heads = rounded_both(jnp.dot(frame_rows, w_key, precision=highest)).reshape(key_count, HEADS, HEAD)
    value_heads = rounded_both(jnp.dot(frame_rows, w_value, precision=highest)).reshape(key_count, HEADS, HEAD)
    relative_heads = rounded_both(jnp.dot(low(sinusoid(MEM, SEG, D)), w_rel, precision=highest)).reshape(relative_count, HEADS, HEAD)
    segment_table = segment_embed.reshape(2, HEADS, HEAD)
    key_place = jnp.arange(key_count, dtype=jnp.int32) - MEM
    key_rank = jnp.concatenate([jnp.full((MEM,), -1, jnp.int32), order_row])
    key_segment = jnp.concatenate([jnp.zeros((MEM,), jnp.int32), segment])
    key_live = key_place < length
    differ = segment[:, None] != key_segment[None, :]
    content_allowed = key_live[None, :] & (key_rank[None, :] <= order_row[:, None])
    query_allowed = key_live[None, :] & (key_rank[None, :] < order_row[:, None])

    def stream(inputs, allowed):
        projected = low_back(jnp.dot(inputs, w_query, precision=highest))
        query_content = rounded_both(projected + bias_content).reshape(SEG, HEADS, HEAD)
        query_position = rounded_both(projected + bias_position).reshape(SEG, HEADS, HEAD)
        query_segment = rounded_both(projected + bias_segment).reshape(SEG, HEADS, HEAD)
        content_score = jnp.einsum('ihd,jhd->hij', query_content, key_heads, precision=highest)
        position_score = relative_shift(jnp.einsum('ihd,uhd->hiu', query_position, relative_heads, precision=highest))
        segment_terms = jnp.einsum('ihd,chd->hic', query_segment, segment_table, precision=highest)
        segment_score = jnp.where(differ[None], segment_terms[:, :, 1:2], segment_terms[:, :, 0:1])
        score_sum = low_back(content_score + position_score + segment_score)
        logits = jnp.where(allowed[None], score_sum * HEAD ** (-0.5), -1e+30)
        softmax_out = jax.nn.softmax(logits, axis=-1)
        mixture = rounded_both(jnp.einsum('hij,jhd->ihd', low(softmax_out), value_heads, precision=highest).reshape(SEG, D))
        attended = low_back(jnp.dot(mixture, w_out, precision=highest))
        normed_one = layer_norm(inputs + attended, gain_one, shift_one)
        inner_pre = low_back(jnp.dot(low(normed_one), w_inner, precision=highest) + bias_inner)
        activated = low(jax.nn.gelu(inner_pre, approximate=False))
        outer_sum = low_back(jnp.dot(activated, w_outer, precision=highest) + bias_outer)
        return layer_norm(normed_one + outer_sum, gain_two, shift_two)
    return (stream(content, content_allowed), stream(query_rows, query_allowed))

def reference(content_in, query_in, memory, sequence_lengths, order_rank, segment_ids, w_query, w_key, w_value, w_out, w_rel, bias_content, bias_position, bias_segment, segment_embed, gain_one, shift_one, w_inner, bias_inner, w_outer, bias_outer, gain_two, shift_two, content_cotangent, query_cotangent):
    weights = tuple((tensor.astype(jnp.float32) for tensor in (w_query, w_key, w_value, w_out, w_rel, bias_content, bias_position, bias_segment, segment_embed, gain_one, shift_one, w_inner, bias_inner, w_outer, bias_outer, gain_two, shift_two)))
    memory_full = memory.astype(jnp.float32)

    def forward(params, content_all, query_all):

        def per_sequence(packed):
            content, query_rows, memory_rows, length, order_row, segment = packed
            return jax.checkpoint(sequence_layer)(params, content, query_rows, memory_rows, length, order_row, segment)
        return lax.map(per_sequence, (content_all, query_all, memory_full, sequence_lengths, order_rank, segment_ids))
    outputs, pullback = jax.vjp(forward, weights, content_in.astype(jnp.float32), query_in.astype(jnp.float32))
    weight_grads, grad_content, grad_query = pullback((content_cotangent.astype(jnp.float32), query_cotangent.astype(jnp.float32)))
    return (outputs[0].astype(jnp.bfloat16), outputs[1].astype(jnp.bfloat16), grad_content.astype(jnp.bfloat16), grad_query.astype(jnp.bfloat16), weight_grads[0], weight_grads[1], weight_grads[2], weight_grads[3], weight_grads[4], weight_grads[5], weight_grads[6], weight_grads[7], weight_grads[8], weight_grads[9], weight_grads[10], weight_grads[11], weight_grads[12], weight_grads[13], weight_grads[14], weight_grads[15], weight_grads[16])
```

```python
import jax
import jax.numpy as jnp
from jax import lax
from jax.experimental import pallas as pl
from jax.experimental.pallas import tpu as pltpu
from jax.sharding import PartitionSpec as P

D = 768
HEADS = 12
HEAD = 64
SEG = 512
MEM = 384
KEYS = MEM + SEG
REL = MEM + 2 * SEG
PAIR = 2 * HEAD
PAIRS = HEADS // 2
ROWS = 256
SUB = 128
WIN = KEYS + SUB
FAR = -1e30
LOG2E = 1.4426950408889634
SCALE = HEAD**-0.5
VMEM_BYTES = 60 * 1024 * 1024
nt = (((1,), (1,)), ((), ()))
nn = (((1,), (0,)), ((), ()))
tn = (((0,), (0,)), ((), ()))


def mm(left, right, dims):
    return lax.dot_general(left, right, dims, preferred_element_type=jnp.float32)


def lane_low(rows):
    return lax.broadcasted_iota(jnp.int32, (rows, PAIR), 1) < HEAD


def forward_kernel(
    qc_ref, qp_ref, qs_ref, k_ref, v_ref, rel_ref, emb_ref, qseg_ref, kseg_ref, qrank_ref, krank_ref,
    mix_ref, inv_ref, prob_ref, kcat, vcat,
):
    half = pl.program_id(2)

    @pl.when((pl.program_id(1) == 0) & (half == 0))
    def _():
        low = lane_low(KEYS)
        same = kseg_ref[...] == 0
        kcat[0, :, :PAIR] = k_ref[...]
        kcat[1, :, :PAIR] = k_ref[...]
        zero_row = emb_ref[0:1, :].astype(jnp.float32)
        one_row = emb_ref[1:2, :].astype(jnp.float32)
        zero_roll = pltpu.roll(zero_row, HEAD, 1)
        one_roll = pltpu.roll(one_row, HEAD, 1)
        low_row = lane_low(1)
        for head in range(2):
            if head == 0:
                near = jnp.where(low_row, zero_row, one_roll)
                away = jnp.where(low_row, one_row, zero_roll)
            else:
                near = jnp.where(low_row, zero_roll, one_row)
                away = jnp.where(low_row, one_roll, zero_row)
            kcat[head, :, PAIR:] = jnp.where(same, near, away).astype(jnp.bfloat16)
        vcat[:, :PAIR] = v_ref[...]
        vcat[:, PAIR:] = jnp.ones((KEYS, PAIR), jnp.bfloat16)

    low = lane_low(ROWS)
    zero = jnp.zeros((ROWS, PAIR), jnp.bfloat16)
    qc = qc_ref[...]
    qp = qp_ref[...]
    qs = qs_ref[...]
    qs_roll = pltpu.roll(qs.astype(jnp.float32), HEAD, 1).astype(jnp.bfloat16)
    first = qseg_ref[...] == 0
    seg_keep = first == low
    krank = krank_ref[...]
    mixed = []
    inverse = []
    for head in range(2):
        mine = low if head == 0 else ~low
        twice = jnp.where(mine, qs, qs_roll)
        qcat = jnp.concatenate(
            [jnp.where(mine, qc, zero), jnp.where(seg_keep, twice, zero)], axis=1
        )
        score = mm(qcat, kcat[head], nt)
        qp_mine = jnp.where(mine, qp, zero)
        parts = []
        for sub in range(ROWS // SUB):
            tile = half * (ROWS // SUB) + sub
            window = rel_ref[pl.ds(3 - tile, WIN // SUB)].reshape(WIN, PAIR)
            grid = mm(qp_mine[sub * SUB : (sub + 1) * SUB], window, nt)
            shifted = pltpu.roll(grid, WIN - SUB + 1, 1, stride=1, stride_axis=0)[:, :KEYS]
            logit = score[sub * SUB : (sub + 1) * SUB] + shifted
            current = jnp.where(
                krank <= qrank_ref[sub * SUB : (sub + 1) * SUB, :], logit[:, MEM:], FAR
            )
            past = logit[:, :MEM]
            top = jnp.maximum(
                jnp.max(past, axis=-1, keepdims=True), jnp.max(current, axis=-1, keepdims=True)
            )
            factor = SCALE * LOG2E
            soft = jnp.concatenate(
                [jnp.exp2((past - top) * factor), jnp.exp2((current - top) * factor)], axis=1
            ).astype(jnp.bfloat16)
            prob_ref[head, sub * SUB : (sub + 1) * SUB, :] = soft
            parts.append(soft)
        summed = mm(jnp.concatenate(parts, axis=0), vcat[...], nn)
        scale = 1.0 / summed[:, PAIR:]
        mixed.append(summed[:, :PAIR] * scale)
        inverse.append(scale)
    mix_ref[...] = jnp.where(low, mixed[0], mixed[1]).astype(jnp.bfloat16)
    inv_ref[...] = jnp.where(low, inverse[0], inverse[1])


def attention_forward(qc, qp, qs, keys, values, rel, emb, qseg, kseg, qrank, krank):
    halves = SEG // ROWS
    row = pl.BlockSpec((ROWS, PAIR), lambda p, s, h: (s * halves + h, p))
    col = pl.BlockSpec((ROWS, 1), lambda p, s, h: (s * halves + h, 0))
    pair = lambda rows: pl.BlockSpec((rows, PAIR), lambda p, s, h: (0, p))
    return pl.pallas_call(
        forward_kernel,
        grid=(PAIRS, 2, halves),
        in_specs=[
            row, row, row, pair(KEYS), pair(KEYS),
            pl.BlockSpec((REL // SUB, SUB, PAIR), lambda p, s, h: (0, 0, p)),
            pair(2), col,
            pl.BlockSpec((KEYS, 1), lambda p, s, h: (0, 0)),
            col,
            pl.BlockSpec((1, SEG), lambda p, s, h: (0, 0)),
        ],
        out_specs=[
            row, row,
            pl.BlockSpec((None, 2, ROWS, KEYS), lambda p, s, h: (p, 0, s * halves + h, 0)),
        ],
        out_shape=[
            jax.ShapeDtypeStruct((2 * SEG, D), jnp.bfloat16),
            jax.ShapeDtypeStruct((2 * SEG, D), jnp.float32),
            jax.ShapeDtypeStruct((PAIRS, 2, 2 * SEG, KEYS), jnp.bfloat16),
        ],
        scratch_shapes=[
            pltpu.VMEM((2, KEYS, 2 * PAIR), jnp.bfloat16),
            pltpu.VMEM((KEYS, 2 * PAIR), jnp.bfloat16),
        ],
        compiler_params=pltpu.CompilerParams(
            dimension_semantics=("arbitrary",) * 3, vmem_limit_bytes=VMEM_BYTES
        ),
        name="attention_forward",
    )(qc, qp, qs, keys, values, rel.reshape(REL // SUB, SUB, D), emb, qseg, kseg, qrank, krank)


def backward_kernel(
    prob_ref, dmix_ref, mix_ref, inv_ref, qc_ref, qp_ref, qs_ref, k_ref, v_ref, rel_ref, emb_ref,
    qseg_ref, kseg_ref,
    dproj_ref, dk_ref, dv_ref, drel_ref, small_ref,
    kcat, dk_acc, dv_acc, drel_acc,
):
    stream = pl.program_id(1)
    half = pl.program_id(2)
    halves = SEG // ROWS

    @pl.when((stream == 0) & (half == 0))
    def _():
        kcat[:, :PAIR] = k_ref[...]
        kcat[:, PAIR:] = jnp.where((kseg_ref[...] == 0) == lane_low(KEYS), 1.0, 0.0).astype(
            jnp.bfloat16
        )
        dk_acc[...] = jnp.zeros_like(dk_acc)
        dv_acc[...] = jnp.zeros_like(dv_acc)
        drel_acc[...] = jnp.zeros_like(drel_acc)
        small_ref[...] = jnp.zeros_like(small_ref)

    low = lane_low(ROWS)
    low_sub = lane_low(SUB)
    zero = jnp.zeros((ROWS, PAIR), jnp.bfloat16)
    flip = jnp.where(
        lax.broadcasted_iota(jnp.int32, (SUB, SUB), 0) + lax.broadcasted_iota(jnp.int32, (SUB, SUB), 1)
        == SUB - 1,
        1.0, 0.0,
    ).astype(jnp.bfloat16)
    dmix = (dmix_ref[...].astype(jnp.float32) * (inv_ref[...] * SCALE)).astype(jnp.bfloat16)
    weighted = dmix.astype(jnp.float32) * mix_ref[...].astype(jnp.float32)
    qc = qc_ref[...]
    qp = qp_ref[...]
    qs = qs_ref[...].astype(jnp.float32)
    flipped = [
        mm(flip, qp[s * SUB : (s + 1) * SUB], nn).astype(jnp.bfloat16) for s in range(ROWS // SUB)
    ]
    first = qseg_ref[...] == 0
    emb = emb_ref[...].astype(jnp.float32)
    dqc = []
    dqs = []
    seg_sum = []
    dqp = [[] for _ in range(ROWS // SUB)]
    grids = [[] for _ in range(ROWS // SUB)]
    totals = []
    dm_heads = []
    qc_heads = []
    for head in range(2):
        mine = low if head == 0 else ~low
        dm = jnp.where(mine, dmix, zero)
        dm_heads.append(dm)
        qc_heads.append(jnp.where(mine, qc, zero))
        row_sum = jnp.sum(jnp.where(mine, weighted, 0.0), axis=-1, keepdims=True)
        dprob = mm(dm, v_ref[...], nt)
        total = (prob_ref[head].astype(jnp.float32) * (dprob - row_sum)).astype(jnp.bfloat16)
        totals.append(total)
        back = mm(total, kcat[...], nn)
        dqc.append(back[:, :PAIR])
        sums = back[:, PAIR:]
        sums_roll = pltpu.roll(sums, HEAD, 1)
        key_zero = jnp.where(low, sums, sums_roll)
        key_one = jnp.where(low, sums_roll, sums)
        same = jnp.where(first, key_zero, key_one)
        other = jnp.where(first, key_one, key_zero)
        dqs.append(same * emb[0:1] + other * emb[1:2])
        seg_sum.append((same, other))
        for s in range(ROWS // SUB):
            tile = half * (ROWS // SUB) + s
            turned = mm(flip, total[s * SUB : (s + 1) * SUB], nn)
            padded = jnp.concatenate([turned, jnp.zeros((SUB, SUB), jnp.float32)], axis=1)
            grid = pltpu.roll(padded, 0, 1, stride=1, stride_axis=0).astype(jnp.bfloat16)
            grids[s].append(grid)
            window = rel_ref[pl.ds(3 - tile, WIN // SUB)].reshape(WIN, PAIR)
            dqp[s].append(mm(grid, window, nn))
    prob_all = prob_ref[...].reshape(2 * ROWS, KEYS)
    dv_acc[...] += mm(jnp.concatenate(dm_heads, axis=0), prob_all, tn)
    dk_acc[...] += mm(jnp.concatenate(qc_heads, axis=0), jnp.concatenate(totals, axis=0), tn)
    position_parts = []
    for s in range(ROWS // SUB):
        tile = half * (ROWS // SUB) + s
        zero_sub = jnp.zeros((SUB, PAIR), jnp.bfloat16)
        left = jnp.concatenate(
            [jnp.where(low_sub, flipped[s], zero_sub), jnp.where(low_sub, zero_sub, flipped[s])],
            axis=0,
        )
        drel = mm(left, jnp.concatenate(grids[s], axis=0), tn)
        for block in range(WIN // SUB):
            drel_acc[3 - tile + block] += drel[:, block * SUB : (block + 1) * SUB]
        turned = jnp.where(low_sub, dqp[s][0], dqp[s][1]).astype(jnp.bfloat16)
        position_parts.append(mm(flip, turned, nn))
    dqp_wide = jnp.concatenate(position_parts, axis=0)
    dqc_wide = jnp.where(low, dqc[0], dqc[1]).astype(jnp.bfloat16).astype(jnp.float32)
    dqs_wide = jnp.where(low, dqs[0], dqs[1]).astype(jnp.bfloat16).astype(jnp.float32)
    dproj_ref[...] = (dqc_wide + dqp_wide + dqs_wide).astype(jnp.bfloat16)
    same = jnp.where(low, seg_sum[0][0], seg_sum[1][0])
    other = jnp.where(low, seg_sum[0][1], seg_sum[1][1])
    rows = [
        dqc_wide, dqp_wide, dqs_wide, same * qs, other * qs,
    ]
    for index, value in enumerate(rows):
        small_ref[index : index + 1, :] += jnp.sum(value, axis=0, keepdims=True)

    @pl.when((stream == 1) & (half == halves - 1))
    def _():
        dk_ref[...] = dk_acc[...].T.astype(jnp.bfloat16)
        dv_ref[...] = (dv_acc[...].T * (1.0 / SCALE)).astype(jnp.bfloat16)
        for block in range(REL // SUB):
            drel_ref[block] = drel_acc[block].T.astype(jnp.bfloat16)


def attention_backward(
    prob, dmix, mix, inv, qc, qp, qs, keys, values, rel, emb, qseg, kseg
):
    halves = SEG // ROWS
    row = pl.BlockSpec((ROWS, PAIR), lambda p, s, h: (s * halves + h, p))
    col = pl.BlockSpec((ROWS, 1), lambda p, s, h: (s * halves + h, 0))
    pair = lambda rows: pl.BlockSpec((rows, PAIR), lambda p, s, h: (0, p))
    rel_block = pl.BlockSpec((REL // SUB, SUB, PAIR), lambda p, s, h: (0, 0, p))
    outs = pl.pallas_call(
        backward_kernel,
        grid=(PAIRS, 2, halves),
        in_specs=[
            pl.BlockSpec((None, 2, ROWS, KEYS), lambda p, s, h: (p, 0, s * halves + h, 0)),
            row, row, row, row, row, row, pair(KEYS), pair(KEYS), rel_block, pair(2), col,
            pl.BlockSpec((KEYS, 1), lambda p, s, h: (0, 0)),
        ],
        out_specs=[row, pair(KEYS), pair(KEYS), rel_block, pair(8)],
        out_shape=[
            jax.ShapeDtypeStruct((2 * SEG, D), jnp.bfloat16),
            jax.ShapeDtypeStruct((KEYS, D), jnp.bfloat16),
            jax.ShapeDtypeStruct((KEYS, D), jnp.bfloat16),
            jax.ShapeDtypeStruct((REL // SUB, SUB, D), jnp.bfloat16),
            jax.ShapeDtypeStruct((8, D), jnp.float32),
        ],
        scratch_shapes=[
            pltpu.VMEM((KEYS, 2 * PAIR), jnp.bfloat16),
            pltpu.VMEM((PAIR, KEYS), jnp.float32),
            pltpu.VMEM((PAIR, KEYS), jnp.float32),
            pltpu.VMEM((REL // SUB, PAIR, SUB), jnp.float32),
        ],
        compiler_params=pltpu.CompilerParams(
            dimension_semantics=("arbitrary",) * 3, vmem_limit_bytes=VMEM_BYTES
        ),
        name="attention_backward",
    )(prob, dmix, mix, inv, qc, qp, qs, keys, values, rel.reshape(REL // SUB, SUB, D), emb, qseg, kseg)
    return outs[0], outs[1], outs[2], outs[3].reshape(REL, D), outs[4]


norm_epsilon = 1e-06


def layer_norm(tensor, norm_gain, norm_shift):
    centred = tensor - jnp.mean(tensor, axis=-1, keepdims=True)
    variance = jnp.mean(centred * centred, axis=-1, keepdims=True)
    return centred * lax.rsqrt(variance + norm_epsilon) * norm_gain + norm_shift


def gelu_exact(tensor):
    return jax.nn.gelu(tensor, approximate=False)


def sinusoid():
    fine_count = 32
    frequency = 1.0 / 10000.0 ** (
        jnp.arange(0, D, 2, dtype=jnp.int32).astype(jnp.float32) / D
    )
    coarse = (KEYS - 1 - fine_count * jnp.arange(REL // fine_count, dtype=jnp.int32)).astype(
        jnp.float32
    )[:, None] * frequency[None]
    fine = jnp.arange(fine_count, dtype=jnp.int32).astype(jnp.float32)[:, None] * frequency[None]
    sin_coarse, cos_coarse = jnp.sin(coarse)[:, None], jnp.cos(coarse)[:, None]
    sin_fine, cos_fine = jnp.sin(fine)[None], jnp.cos(fine)[None]
    sine = sin_coarse * cos_fine - cos_coarse * sin_fine
    cosine = cos_coarse * cos_fine + sin_coarse * sin_fine
    return jnp.concatenate([sine, cosine], axis=-1).reshape(REL, D).astype(jnp.bfloat16)


def shards(
    content_in, query_in, memory, sequence_lengths, order_rank, segment_ids,
    w_query, w_key, w_value, w_out, w_rel,
    bias_content, bias_position, bias_segment, segment_embed,
    gain_one, shift_one, w_inner, bias_inner, w_outer, bias_outer, gain_two, shift_two,
    content_cotangent, query_cotangent,
):
    wide = lambda tensor: tensor.astype(jnp.float32)
    low = lambda tensor: tensor.astype(jnp.bfloat16)
    past = lax.all_to_all(memory, "mem", split_axis=0, concat_axis=1, tiled=True)[0]
    content = content_in[0]
    inputs = jnp.concatenate([content, query_in[0]], axis=0)
    cotangent = jnp.concatenate([content_cotangent[0], query_cotangent[0]], axis=0)
    segment = segment_ids[0]
    rank = order_rank[0]
    length = sequence_lengths[0]
    query_seg = jnp.concatenate([segment, segment])[:, None]
    key_seg = jnp.concatenate([jnp.zeros((MEM,), jnp.int32), segment])[:, None]
    query_rank = jnp.concatenate([rank, rank - 1])[:, None]
    key_rank = jnp.where(jnp.arange(SEG, dtype=jnp.int32) < length, rank, 2 * SEG)[None, :]

    positions = sinusoid()
    relative = low(mm(positions, w_rel, nn))
    frame = jnp.concatenate([past, content], axis=0)
    keys = low(mm(frame, w_key, nn))
    values = low(mm(frame, w_value, nn))
    projected = mm(inputs, w_query, nn)
    query_content = low(projected + wide(bias_content))
    query_position = low(projected + wide(bias_position))
    query_segment = low(projected + wide(bias_segment))
    mixture, inverse, probs = attention_forward(
        query_content, query_position, query_segment, keys, values, relative, segment_embed,
        query_seg, key_seg, query_rank, key_rank,
    )
    gain_first, shift_first = wide(gain_one), wide(shift_one)
    gain_second, shift_second = wide(gain_two), wide(shift_two)
    normed_one, norm_back_one = jax.vjp(
        layer_norm, wide(inputs) + mm(mixture, w_out, nn), gain_first, shift_first
    )
    normed_low = low(normed_one)
    activated, gelu_back = jax.vjp(gelu_exact, mm(normed_low, w_inner, nn) + wide(bias_inner))
    active_low = low(activated)
    final_out, norm_back_two = jax.vjp(
        layer_norm,
        normed_one + mm(active_low, w_outer, nn) + wide(bias_outer),
        gain_second,
        shift_second,
    )
    grad_final, grad_second_gain, grad_second_shift = norm_back_two(wide(cotangent))
    grad_outer_low = low(grad_final)
    grad_outer_bias = jnp.sum(wide(grad_outer_low), axis=0)
    grad_outer_w = low(mm(active_low, grad_outer_low, tn))
    (grad_inner_pre,) = gelu_back(mm(grad_outer_low, w_outer, nt))
    grad_inner_low = low(grad_inner_pre)
    grad_inner_bias = jnp.sum(wide(grad_inner_low), axis=0)
    grad_inner_w = low(mm(normed_low, grad_inner_low, tn))
    grad_residual, grad_first_gain, grad_first_shift = norm_back_one(
        grad_final + mm(grad_inner_low, w_inner, nt)
    )
    grad_attended = low(grad_residual)
    grad_out_w = low(mm(mixture, grad_attended, tn))
    grad_mixture = low(mm(grad_attended, w_out, nt))
    grad_projected, grad_keys, grad_values, grad_relative, small = attention_backward(
        probs, grad_mixture, mixture, inverse, query_content, query_position, query_segment,
        keys, values, relative, segment_embed, query_seg, key_seg,
    )
    grad_query_w = low(mm(inputs, grad_projected, tn))
    grad_key_w = low(mm(frame, grad_keys, tn))
    grad_value_w = low(mm(frame, grad_values, tn))
    grad_rel_w = low(mm(positions, grad_relative, tn))
    grad_inputs = grad_residual + mm(grad_projected, w_query, nt)
    grad_content = (
        grad_inputs[:SEG] + mm(grad_keys[MEM:], w_key, nt) + mm(grad_values[MEM:], w_value, nt)
    )
    both = ("batch", "mem")
    big = lax.psum(
        (grad_query_w, grad_key_w, grad_value_w, grad_out_w, grad_rel_w, grad_inner_w, grad_outer_w),
        both,
    )
    query_sum, key_sum, value_sum, out_sum, rel_sum, inner_sum, outer_sum = [wide(t) for t in big]
    vectors = jnp.concatenate(
        [
            small[:5].reshape(-1), grad_first_gain, grad_first_shift, grad_inner_bias,
            grad_outer_bias, grad_second_gain, grad_second_shift,
        ]
    )
    vectors = lax.psum(vectors, both)
    pieces = {}
    start = 0
    for name, count in (
        ("content", D), ("position", D), ("segment", D), ("embed", 2 * D), ("gain1", D),
        ("shift1", D), ("inner", bias_inner.shape[0]), ("outer", D), ("gain2", D), ("shift2", D),
    ):
        pieces[name] = vectors[start : start + count]
        start += count
    return (
        low(final_out[None, :SEG]), low(final_out[None, SEG:]),
        low(grad_content[None]), low(grad_inputs[None, SEG:]),
        query_sum, key_sum, value_sum, out_sum, rel_sum,
        pieces["content"], pieces["position"], pieces["segment"], pieces["embed"].reshape(2, D),
        pieces["gain1"], pieces["shift1"], inner_sum, pieces["inner"], outer_sum, pieces["outer"],
        pieces["gain2"], pieces["shift2"],
    )


def solution(mesh):
    both = ("batch", "mem")
    rows = P(both, None, None)
    return jax.shard_map(
        shards,
        mesh=mesh,
        in_specs=(rows, rows, P("batch", "mem", None), P(both), P(both, None), P(both, None))
        + (P(),) * 17
        + (rows, rows),
        out_specs=(rows,) * 4 + (P(),) * 17,
        check_vma=False,
    )
```

```python
import jax
import jax.numpy as jnp
from jax import lax
from jax.experimental import pallas as pl
from jax.experimental.pallas import tpu as pltpu
from jax.sharding import PartitionSpec as P

D = 768
HEADS = 12
HEAD = 64
SEG = 512
MEM = 384
KEYS = MEM + SEG
REL = MEM + 2 * SEG
PAIR = 2 * HEAD
PAIRS = HEADS // 2
ROWS = 256
SUB = 128
CHUNK = 32
WIN = KEYS + SUB
FAR = -1e30
LOG2E = 1.4426950408889634
SCALE = HEAD**-0.5
VMEM_BYTES = 60 * 1024 * 1024
nt = (((1,), (1,)), ((), ()))
nn = (((1,), (0,)), ((), ()))
tn = (((0,), (0,)), ((), ()))


def mm(left, right, dims):
    return lax.dot_general(left, right, dims, preferred_element_type=jnp.float32)


def lane_low(rows):
    return lax.broadcasted_iota(jnp.int32, (rows, PAIR), 1) < HEAD


def tile_spans(tile):
    start = pl.multiple_of(tile * SUB, SUB)
    return [start, start + SEG]


def both_rows(ref, spans):
    return jnp.concatenate([ref[pl.ds(start, SUB), :] for start in spans], axis=0)


def forward_kernel(
    qc_ref, qp_ref, qs_ref, k_ref, v_ref, rel_ref, emb_ref, side_ref, key_side_ref, krank_ref,
    mix_ref, inv_ref, prob_ref, kcat, vcat,
):
    low_keys = lane_low(KEYS)
    same = key_side_ref[:, 0:1] == 0
    zero_row = emb_ref[0:1, :].astype(jnp.float32)
    one_row = emb_ref[1:2, :].astype(jnp.float32)
    zero_roll = pltpu.roll(zero_row, HEAD, 1)
    one_roll = pltpu.roll(one_row, HEAD, 1)
    low_row = lane_low(1)
    for head in range(2):
        if head == 0:
            near = jnp.where(low_row, zero_row, one_roll)
            away = jnp.where(low_row, one_row, zero_roll)
        else:
            near = jnp.where(low_row, zero_roll, one_row)
            away = jnp.where(low_row, one_roll, zero_row)
        kcat[head, :, :PAIR] = k_ref[...]
        kcat[head, :, PAIR:] = jnp.where(same, near, away).astype(jnp.bfloat16)
    vcat[:, :PAIR] = v_ref[...]
    vcat[:, PAIR:] = jnp.ones((KEYS, PAIR), jnp.bfloat16)

    def block(tile, carry):
        spans = tile_spans(tile)
        low = lane_low(ROWS)
        zero = jnp.zeros((ROWS, PAIR), jnp.bfloat16)
        qc = both_rows(qc_ref, spans)
        qp = both_rows(qp_ref, spans)
        qs = both_rows(qs_ref, spans)
        qs_roll = pltpu.roll(qs.astype(jnp.float32), HEAD, 1).astype(jnp.bfloat16)
        side = both_rows(side_ref, spans)
        seg_keep = (side[:, 0:1] == 0) == low
        krank = krank_ref[...]
        factor = SCALE * LOG2E
        window = rel_ref[pl.ds(3 - tile, WIN // SUB)].reshape(WIN, PAIR)
        grid = mm(
            jnp.concatenate([jnp.where(low, qp, zero), jnp.where(low, zero, qp)], axis=0), window, nt
        )
        parts = []
        for head in range(2):
            mine = low if head == 0 else ~low
            twice = jnp.where(mine, qs, qs_roll)
            qcat = jnp.concatenate(
                [jnp.where(mine, qc, zero), jnp.where(seg_keep, twice, zero)], axis=1
            )
            score = mm(qcat, kcat[head], nt)
            for row in range(0, ROWS, CHUNK):
                at = row % SUB
                shifted = pltpu.roll(
                    grid[head * ROWS + row : head * ROWS + row + CHUNK],
                    WIN - SUB + 1 + at, 1, stride=1, stride_axis=0,
                )[:, :KEYS]
                logit = score[row : row + CHUNK] + shifted
                current = jnp.where(krank <= side[row : row + CHUNK, 1:2], logit[:, MEM:], FAR)
                logit = jnp.concatenate([logit[:, :MEM], current], axis=1)
                top = jnp.max(logit, axis=-1, keepdims=True)
                soft = jnp.exp2((logit - top) * factor).astype(jnp.bfloat16)
                prob_ref[head, pl.ds(spans[row // SUB] + at, CHUNK), :] = soft
                parts.append(soft)
        summed = mm(jnp.concatenate(parts, axis=0), vcat[...], nn)
        scale = 1.0 / summed[:, PAIR:]
        mixed = summed[:, :PAIR] * scale
        mixed = jnp.where(low, mixed[:ROWS], mixed[ROWS:]).astype(jnp.bfloat16)
        scale = jnp.where(low, scale[:ROWS], scale[ROWS:])
        for index, start in enumerate(spans):
            mix_ref[pl.ds(start, SUB), :] = mixed[index * SUB : (index + 1) * SUB]
            inv_ref[pl.ds(start, SUB), :] = scale[index * SUB : (index + 1) * SUB]
        return carry

    lax.fori_loop(0, SEG // SUB, block, 0)


def whole(rows, lanes):
    return pl.BlockSpec((rows, lanes), lambda p: (0, 0))


def attention_forward(qc, qp, qs, keys, values, rel, emb, side, key_side, krank):
    pair = lambda rows: pl.BlockSpec((rows, PAIR), lambda p: (0, p))
    return pl.pallas_call(
        forward_kernel,
        grid=(PAIRS,),
        in_specs=[
            pair(2 * SEG), pair(2 * SEG), pair(2 * SEG), pair(KEYS), pair(KEYS),
            pl.BlockSpec((REL // SUB, SUB, PAIR), lambda p: (0, 0, p)),
            pair(2), whole(*side.shape), whole(*key_side.shape), whole(1, SEG),
        ],
        out_specs=[
            pair(2 * SEG), pair(2 * SEG),
            pl.BlockSpec((None, 2, 2 * SEG, KEYS), lambda p: (p, 0, 0, 0)),
        ],
        out_shape=[
            jax.ShapeDtypeStruct((2 * SEG, D), jnp.bfloat16),
            jax.ShapeDtypeStruct((2 * SEG, D), jnp.float32),
            jax.ShapeDtypeStruct((PAIRS, 2, 2 * SEG, KEYS), jnp.bfloat16),
        ],
        scratch_shapes=[
            pltpu.VMEM((2, KEYS, 2 * PAIR), jnp.bfloat16),
            pltpu.VMEM((KEYS, 2 * PAIR), jnp.bfloat16),
        ],
        compiler_params=pltpu.CompilerParams(
            dimension_semantics=("arbitrary",), vmem_limit_bytes=VMEM_BYTES
        ),
        cost_estimate=pl.CostEstimate(
            flops=30000000000, transcendentals=11000000, bytes_accessed=30000000
        ),
        name="attention_forward",
    )(qc, qp, qs, keys, values, rel.reshape(REL // SUB, SUB, D), emb, side, key_side, krank)


def backward_kernel(
    prob_ref, dmix_ref, mix_ref, inv_ref, qc_ref, qp_ref, qs_ref, k_ref, v_ref, rel_ref, emb_ref,
    side_ref, key_side_ref,
    dproj_ref, dk_ref, dv_ref, drel_ref, small_ref,
    kcat, dk_acc, dv_acc, drel_acc,
):
    kcat[:, :PAIR] = k_ref[...]
    kcat[:, PAIR:] = jnp.where((key_side_ref[:, 0:1] == 0) == lane_low(KEYS), 1.0, 0.0).astype(
        jnp.bfloat16
    )
    dk_acc[...] = jnp.zeros_like(dk_acc)
    dv_acc[...] = jnp.zeros_like(dv_acc)
    drel_acc[...] = jnp.zeros_like(drel_acc)
    small_ref[...] = jnp.zeros_like(small_ref)

    def block(tile, carry):
        spans = tile_spans(tile)
        low = lane_low(ROWS)
        zero = jnp.zeros((ROWS, PAIR), jnp.bfloat16)
        row_index = lax.broadcasted_iota(jnp.int32, (ROWS, ROWS), 0)
        column_index = lax.broadcasted_iota(jnp.int32, (ROWS, ROWS), 1)
        flip = jnp.where(
            (row_index // SUB == column_index // SUB)
            & (row_index % SUB + column_index % SUB == SUB - 1),
            1.0, 0.0,
        ).astype(jnp.bfloat16)
        dmix = (
            both_rows(dmix_ref, spans).astype(jnp.float32) * (both_rows(inv_ref, spans) * SCALE)
        ).astype(jnp.bfloat16)
        weighted = dmix.astype(jnp.float32) * both_rows(mix_ref, spans).astype(jnp.float32)
        qc = both_rows(qc_ref, spans)
        qp = both_rows(qp_ref, spans)
        qs = both_rows(qs_ref, spans).astype(jnp.float32)
        qp_turned = mm(flip, qp, nn).astype(jnp.bfloat16)
        first = both_rows(side_ref, spans)[:, 0:1] == 0
        emb = emb_ref[...].astype(jnp.float32)
        dm = jnp.concatenate([jnp.where(low, dmix, zero), jnp.where(low, zero, dmix)], axis=0)
        qc_both = jnp.concatenate([jnp.where(low, qc, zero), jnp.where(low, zero, qc)], axis=0)
        qp_both = jnp.concatenate(
            [jnp.where(low, qp_turned, zero), jnp.where(low, zero, qp_turned)], axis=0
        )
        row_sum = jnp.concatenate(
            [
                jnp.sum(jnp.where(low, weighted, 0.0), axis=-1, keepdims=True),
                jnp.sum(jnp.where(low, 0.0, weighted), axis=-1, keepdims=True),
            ],
            axis=0,
        )
        prob = jnp.concatenate([both_rows(prob_ref.at[head], spans) for head in range(2)], axis=0)
        dprob = mm(dm, v_ref[...], nt)
        total = jnp.concatenate(
            [
                (
                    prob[at : at + CHUNK].astype(jnp.float32)
                    * (dprob[at : at + CHUNK] - row_sum[at : at + CHUNK])
                ).astype(jnp.bfloat16)
                for at in range(0, 2 * ROWS, CHUNK)
            ],
            axis=0,
        )
        back = mm(total, kcat[...], nn)
        turned = [mm(flip, total[head * ROWS : (head + 1) * ROWS], nn) for head in range(2)]
        grid = jnp.concatenate(
            [
                pltpu.roll(
                    jnp.concatenate(
                        [turned[head][row : row + CHUNK], jnp.zeros((CHUNK, SUB), jnp.float32)],
                        axis=1,
                    ),
                    row % SUB, 1, stride=1, stride_axis=0,
                ).astype(jnp.bfloat16)
                for head in range(2)
                for row in range(0, ROWS, CHUNK)
            ],
            axis=0,
        )
        window = rel_ref[pl.ds(3 - tile, WIN // SUB)].reshape(WIN, PAIR)
        dqp = mm(grid, window, nn)
        dqp = jnp.where(low, dqp[:ROWS], dqp[ROWS:]).astype(jnp.bfloat16)
        dqp_wide = mm(flip, dqp, nn)
        dv_acc[...] += mm(dm, prob, tn)
        dk_acc[...] += mm(qc_both, total, tn)
        drel = mm(qp_both, grid, tn)
        for part in range(WIN // SUB):
            drel_acc[3 - tile + part] += drel[:, part * SUB : (part + 1) * SUB]
        dqc_wide = (
            jnp.where(low, back[:ROWS, :PAIR], back[ROWS:, :PAIR])
            .astype(jnp.bfloat16)
            .astype(jnp.float32)
        )
        sums = [back[head * ROWS : (head + 1) * ROWS, PAIR:] for head in range(2)]
        rolled = [pltpu.roll(part, HEAD, 1) for part in sums]
        key_zero = jnp.where(low, sums[0], rolled[1])
        key_one = jnp.where(low, rolled[0], sums[1])
        near = jnp.where(first, key_zero, key_one)
        other = jnp.where(first, key_one, key_zero)
        dqs_wide = (near * emb[0:1] + other * emb[1:2]).astype(jnp.bfloat16).astype(jnp.float32)
        dproj = (dqc_wide + dqp_wide + dqs_wide).astype(jnp.bfloat16)
        for index, start in enumerate(spans):
            dproj_ref[pl.ds(start, SUB), :] = dproj[index * SUB : (index + 1) * SUB]
        rows = [dqc_wide, dqp_wide, dqs_wide, near * qs, other * qs]
        for row, value in enumerate(rows):
            small_ref[row : row + 1, :] += jnp.sum(value, axis=0, keepdims=True)
        return carry

    lax.fori_loop(0, SEG // SUB, block, 0)
    dk_ref[...] = dk_acc[...].T.astype(jnp.bfloat16)
    dv_ref[...] = (dv_acc[...].T * (1.0 / SCALE)).astype(jnp.bfloat16)
    for part in range(REL // SUB):
        drel_ref[part] = drel_acc[part].T.astype(jnp.bfloat16)


def attention_backward(
    base, pairs, prob, dmix, mix, inv, qc, qp, qs, keys, values, rel, emb, side, key_side
):
    pair = lambda rows: pl.BlockSpec((rows, PAIR), lambda p: (0, base + p))
    pair_out = lambda rows: pl.BlockSpec((rows, PAIR), lambda p: (0, p))
    rel_block = pl.BlockSpec((REL // SUB, SUB, PAIR), lambda p: (0, 0, base + p))
    lanes = pairs * PAIR
    outs = pl.pallas_call(
        backward_kernel,
        grid=(pairs,),
        in_specs=[
            pl.BlockSpec((None, 2, 2 * SEG, KEYS), lambda p: (base + p, 0, 0, 0)),
            pair(2 * SEG), pair(2 * SEG), pair(2 * SEG), pair(2 * SEG), pair(2 * SEG), pair(2 * SEG),
            pair(KEYS), pair(KEYS), rel_block, pair(2), whole(*side.shape), whole(*key_side.shape),
        ],
        out_specs=[
            pair_out(2 * SEG), pair_out(KEYS), pair_out(KEYS),
            pl.BlockSpec((REL // SUB, SUB, PAIR), lambda p: (0, 0, p)), pair_out(8),
        ],
        out_shape=[
            jax.ShapeDtypeStruct((2 * SEG, lanes), jnp.bfloat16),
            jax.ShapeDtypeStruct((KEYS, lanes), jnp.bfloat16),
            jax.ShapeDtypeStruct((KEYS, lanes), jnp.bfloat16),
            jax.ShapeDtypeStruct((REL // SUB, SUB, lanes), jnp.bfloat16),
            jax.ShapeDtypeStruct((8, lanes), jnp.float32),
        ],
        scratch_shapes=[
            pltpu.VMEM((KEYS, 2 * PAIR), jnp.bfloat16),
            pltpu.VMEM((PAIR, KEYS), jnp.float32),
            pltpu.VMEM((PAIR, KEYS), jnp.float32),
            pltpu.VMEM((REL // SUB, PAIR, SUB), jnp.float32),
        ],
        compiler_params=pltpu.CompilerParams(
            dimension_semantics=("arbitrary",), vmem_limit_bytes=VMEM_BYTES
        ),
        cost_estimate=pl.CostEstimate(
            flops=pairs * 7000000000, transcendentals=0, bytes_accessed=pairs * 6000000
        ),
        name="attention_backward",
    )(
        prob, dmix, mix, inv, qc, qp, qs, keys, values, rel.reshape(REL // SUB, SUB, D), emb, side,
        key_side,
    )
    return outs[0], outs[1], outs[2], outs[3].reshape(REL, lanes), outs[4]


norm_epsilon = 1e-06
TOKENS = 256
FF_CHUNK = 768
half_erfc = (0.5 * 0.254829592, 0.5 * -0.284496736, 0.5 * 1.421413741, 0.5 * -1.453152027, 0.5 * 1.061405429)


def gelu_pair(x):
    gauss = jnp.exp2(x * x * (-0.5 * LOG2E))
    t = 1.0 / (1.0 + (0.3275911 * 0.7071067811865476) * jnp.abs(x))
    a1, a2, a3, a4, a5 = half_erfc
    tail = t * (a1 + t * (a2 + t * (a3 + t * (a4 + t * a5)))) * gauss
    cdf = jnp.where(x >= 0.0, 1.0 - tail, tail)
    return x * cdf, cdf + x * gauss * 0.3989422804014327


def normalise(tensor):
    centred = tensor - jnp.mean(tensor, axis=-1, keepdims=True)
    inverse = lax.rsqrt(jnp.mean(centred * centred, axis=-1, keepdims=True) + norm_epsilon)
    return centred * inverse, inverse


def norm_back(grad, hat, inverse):
    return inverse * (
        grad
        - jnp.mean(grad, axis=-1, keepdims=True)
        - hat * jnp.mean(grad * hat, axis=-1, keepdims=True)
    )


def token_kernel(
    x_ref, mix_ref, cot_ref, wo_ref, wi_ref, wf_ref, bias_inner_ref, rows_ref,
    final_ref, active_ref, outer_ref, inner_ref, attended_ref, dmix_ref, low_ref, residual_ref,
    sums_ref, inner_sum_ref,
    slope,
):
    @pl.when(pl.program_id(0) == 0)
    def _():
        sums_ref[...] = jnp.zeros_like(sums_ref)
        inner_sum_ref[...] = jnp.zeros_like(inner_sum_ref)

    gain_one, shift_one = rows_ref[0:1, :], rows_ref[1:2, :]
    gain_two, shift_two = rows_ref[2:3, :], rows_ref[3:4, :]
    bias_outer = rows_ref[4:5, :]
    hat_one, inverse_one = normalise(
        x_ref[...].astype(jnp.float32) + mm(mix_ref[...], wo_ref[...], nn)
    )
    normed = hat_one * gain_one + shift_one
    normed_low = normed.astype(jnp.bfloat16)
    low_ref[...] = normed_low
    chunks = [slice(at, at + FF_CHUNK) for at in range(0, wi_ref.shape[1], FF_CHUNK)]
    pre = mm(normed_low, wi_ref[:, chunks[0]], nn)
    total = normed + bias_outer
    for index, chunk in enumerate(chunks):
        here = pre + bias_inner_ref[:, chunk]
        if index + 1 < len(chunks):
            pre = mm(normed_low, wi_ref[:, chunks[index + 1]], nn)
        value, derivative = gelu_pair(here)
        value = value.astype(jnp.bfloat16)
        active_ref[:, chunk] = value
        slope[:, chunk] = derivative
        total = total + mm(value, wf_ref[chunk, :], nn)
    hat_two, inverse_two = normalise(total)
    final_ref[...] = (hat_two * gain_two + shift_two).astype(jnp.bfloat16)
    cot = cot_ref[...].astype(jnp.float32)
    grad_total = norm_back(cot * gain_two, hat_two, inverse_two)
    grad_outer = grad_total.astype(jnp.bfloat16)
    outer_ref[...] = grad_outer
    sums_ref[2:3, :] += jnp.sum(cot * hat_two, axis=0, keepdims=True)
    sums_ref[3:4, :] += jnp.sum(cot, axis=0, keepdims=True)
    sums_ref[4:5, :] += jnp.sum(grad_outer.astype(jnp.float32), axis=0, keepdims=True)
    back = mm(grad_outer, wf_ref[chunks[0], :], nt)
    for index, chunk in enumerate(chunks):
        here = back
        if index + 1 < len(chunks):
            back = mm(grad_outer, wf_ref[chunks[index + 1], :], nt)
        grad_inner = (here * slope[:, chunk]).astype(jnp.bfloat16)
        inner_ref[:, chunk] = grad_inner
        inner_sum_ref[:, chunk] += jnp.sum(grad_inner.astype(jnp.float32), axis=0, keepdims=True)
        grad_total = grad_total + mm(grad_inner, wi_ref[:, chunk], nt)
    sums_ref[0:1, :] += jnp.sum(grad_total * hat_one, axis=0, keepdims=True)
    sums_ref[1:2, :] += jnp.sum(grad_total, axis=0, keepdims=True)
    residual = norm_back(grad_total * gain_one, hat_one, inverse_one)
    residual_ref[...] = residual
    attended = residual.astype(jnp.bfloat16)
    attended_ref[...] = attended
    dmix_ref[...] = mm(attended, wo_ref[...], nt).astype(jnp.bfloat16)


def token_layer(x, mix, cot, w_out, w_inner, w_outer, bias_inner, rows):
    count = x.shape[0]
    hidden = w_inner.shape[1]
    tile = lambda lanes: pl.BlockSpec((TOKENS, lanes), lambda i: (i, 0))
    once = lambda a, b: pl.BlockSpec((a, b), lambda i: (0, 0), pipeline_mode=pl.Buffered(1))
    sums = lambda a, b: pl.BlockSpec((a, b), lambda i: (0, 0))
    low = lambda lanes: jax.ShapeDtypeStruct((count, lanes), jnp.bfloat16)
    return pl.pallas_call(
        token_kernel,
        grid=(count // TOKENS,),
        in_specs=[
            tile(D), tile(D), tile(D), once(D, D), once(D, hidden), once(hidden, D),
            once(1, hidden), once(8, D),
        ],
        out_specs=[
            tile(D), tile(hidden), tile(D), tile(hidden), tile(D), tile(D), tile(D), tile(D),
            sums(8, D), sums(1, hidden),
        ],
        out_shape=[
            low(D), low(hidden), low(D), low(hidden), low(D), low(D), low(D),
            jax.ShapeDtypeStruct((count, D), jnp.float32),
            jax.ShapeDtypeStruct((8, D), jnp.float32),
            jax.ShapeDtypeStruct((1, hidden), jnp.float32),
        ],
        scratch_shapes=[pltpu.VMEM((TOKENS, hidden), jnp.float32)],
        compiler_params=pltpu.CompilerParams(
            dimension_semantics=("arbitrary",), vmem_limit_bytes=VMEM_BYTES
        ),
        cost_estimate=pl.CostEstimate(
            flops=22000000000, transcendentals=6000000, bytes_accessed=40000000
        ),
        name="token_layer",
    )(x, mix, cot, w_out, w_inner, w_outer, bias_inner, rows)


def chip_bits():
    bits = []
    bit = 2
    while bit < lax.axis_size("batch"):
        bits.append(bit)
        bit *= 2
    return bits


def digit(bit):
    return lax.axis_index("batch") // bit % 2


def across(tensor, bit):
    count = lax.axis_size("batch")
    return lax.ppermute(tensor, "batch", [(i, i ^ bit) for i in range(count)])


def along(tensor, shift):
    ring = lax.axis_size("mem")
    return lax.ppermute(tensor, "mem", [(i, (i + shift) % ring) for i in range(ring)])


def rows_of(tensor, start, count):
    return lax.dynamic_slice(tensor, (start, 0), (count, tensor.shape[1]))


class Sum:
    def __init__(self, tensor, order):
        bits = chip_bits()
        self.bits = [1] + (bits if order == 0 else bits[::-1])
        self.state = tensor
        self.at = 0
        self.stages = 2 * len(self.bits) + 2

    def step(self):
        count, tensor = len(self.bits), self.state
        ring, me = lax.axis_size("mem"), lax.axis_index("mem")
        if self.at < count:
            bit = self.bits[self.at]
            half = tensor.shape[0] // 2
            mine = digit(bit)
            got = across(rows_of(tensor, (1 - mine) * half, half), bit)
            kept = rows_of(tensor, mine * half, half)
            self.state = (kept.astype(jnp.float32) + got.astype(jnp.float32)).astype(jnp.bfloat16)
        elif self.at == count:
            block = tensor.shape[0] // ring
            total = rows_of(tensor, me * block, block).astype(jnp.float32)
            for shift in range(1, ring):
                sent = rows_of(tensor, (me + shift) % ring * block, block)
                total = total + along(sent, shift).astype(jnp.float32)
            self.state = total.astype(jnp.bfloat16)
        elif self.at == count + 1:
            parts = [tensor] + [along(tensor, shift) for shift in range(1, ring)]
            self.state = jnp.concatenate(parts, axis=0)
        else:
            bit = self.bits[2 * count + 1 - self.at]
            self.state = jnp.concatenate([tensor, across(tensor, bit)], axis=0)
        self.at += 1

    def places(self):
        ring = lax.axis_size("mem")
        weight = ring * lax.axis_size("batch") // 2
        index = jnp.arange(2 * weight, dtype=jnp.int32)
        place = (lax.axis_index("mem") - index % ring) % ring
        for bit in self.bits:
            place = place + (index // weight % 2 + digit(bit)) % 2 * weight
            weight //= 2
        return place


class Small:
    def __init__(self, tensor):
        self.state = tensor
        self.at = 0
        self.bits = [1] + chip_bits()
        self.mem_bits = []
        bit = 1
        while bit < lax.axis_size("mem"):
            self.mem_bits.append(bit)
            bit *= 2
        self.stages = len(self.bits) + len(self.mem_bits)

    def step(self):
        ring = lax.axis_size("mem")
        if self.at < len(self.bits):
            got = across(self.state, self.bits[self.at])
        else:
            bit = self.mem_bits[self.at - len(self.bits)]
            got = lax.ppermute(self.state, "mem", [(i, i ^ bit) for i in range(ring)])
        self.state = self.state + got
        self.at += 1


def together(active, tree):
    states, tree = lax.optimization_barrier(([item.state for item in active], tree))
    for item, state in zip(active, states):
        item.state = state
    return tree


def step_all(active):
    for item in active:
        if item.at < item.stages:
            item.step()


def settle_kernel(place_ref, in_ref, out_ref):
    rows = in_ref.shape[0] // place_ref.shape[0]
    per_step = out_ref.shape[0] // rows
    for item in range(per_step):
        start = pl.multiple_of(place_ref[pl.program_id(0) * per_step + item] * rows, 8)
        out_ref[item * rows : (item + 1) * rows, :] = in_ref[pl.ds(start, rows), :].astype(jnp.float32)


def settle(item):
    tensor, place = item.state, item.places()
    blocks = place.shape[0]
    rows, lanes = tensor.shape
    if rows // blocks % 8:
        return tensor.reshape(blocks, -1, lanes)[place].reshape(rows, lanes).astype(jnp.float32)
    steps = 4
    return pl.pallas_call(
        settle_kernel,
        grid_spec=pltpu.PrefetchScalarGridSpec(
            num_scalar_prefetch=1,
            grid=(steps,),
            in_specs=[pl.BlockSpec((rows, lanes), lambda i, p: (0, 0))],
            out_specs=pl.BlockSpec((rows // steps, lanes), lambda i, p: (i, 0)),
        ),
        out_shape=jax.ShapeDtypeStruct((rows, lanes), jnp.float32),
        compiler_params=pltpu.CompilerParams(vmem_limit_bytes=48 * 1024 * 1024),
        name="settle",
    )(place, tensor)


def sinusoid():
    fine_count = 32
    frequency = 1.0 / 10000.0 ** (
        jnp.arange(0, D, 2, dtype=jnp.int32).astype(jnp.float32) / D
    )
    coarse = (KEYS - 1 - fine_count * jnp.arange(REL // fine_count, dtype=jnp.int32)).astype(
        jnp.float32
    )[:, None] * frequency[None]
    fine = jnp.arange(fine_count, dtype=jnp.int32).astype(jnp.float32)[:, None] * frequency[None]
    sin_coarse, cos_coarse = jnp.sin(coarse)[:, None], jnp.cos(coarse)[:, None]
    sin_fine, cos_fine = jnp.sin(fine)[None], jnp.cos(fine)[None]
    sine = sin_coarse * cos_fine - cos_coarse * sin_fine
    cosine = cos_coarse * cos_fine + sin_coarse * sin_fine
    return jnp.concatenate([sine, cosine], axis=-1).reshape(REL, D).astype(jnp.bfloat16)


def shards(
    content_in, query_in, memory, sequence_lengths, order_rank, segment_ids,
    w_query, w_key, w_value, w_out, w_rel,
    bias_content, bias_position, bias_segment, segment_embed,
    gain_one, shift_one, w_inner, bias_inner, w_outer, bias_outer, gain_two, shift_two,
    content_cotangent, query_cotangent,
):
    wide = lambda tensor: tensor.astype(jnp.float32)
    low = lambda tensor: tensor.astype(jnp.bfloat16)
    both = ("batch", "mem")
    past = lax.all_to_all(memory, "mem", split_axis=0, concat_axis=1, tiled=True)[0]
    content = content_in[0]
    inputs = jnp.concatenate([content, query_in[0]], axis=0)
    cotangent = jnp.concatenate([content_cotangent[0], query_cotangent[0]], axis=0)
    segment = segment_ids[0]
    rank = order_rank[0]
    zeros = jnp.zeros((2 * SEG, 6), jnp.int32)
    side = jnp.concatenate(
        [
            jnp.concatenate([segment, segment])[:, None],
            jnp.concatenate([rank, rank - 1])[:, None],
            zeros,
        ],
        axis=1,
    )
    key_side = jnp.concatenate([jnp.zeros((MEM, 8), jnp.int32), side[:SEG]], axis=0)
    live = jnp.arange(SEG, dtype=jnp.int32) < sequence_lengths[0]
    key_rank = jnp.where(live, rank, 2 * SEG)[None, :]

    positions = sinusoid()
    relative = low(mm(positions, w_rel, nn))
    frame = jnp.concatenate([past, content], axis=0)
    keys = low(mm(frame, w_key, nn))
    values = low(mm(frame, w_value, nn))
    projected = mm(inputs, w_query, nn)
    query_content = low(projected + wide(bias_content))
    query_position = low(projected + wide(bias_position))
    query_segment = low(projected + wide(bias_segment))
    mixture, inverse, probs = attention_forward(
        query_content, query_position, query_segment, keys, values, relative, segment_embed,
        side, key_side, key_rank,
    )
    rows = jnp.stack(
        [wide(t) for t in (gain_one, shift_one, gain_two, shift_two, bias_outer)]
        + [jnp.zeros((D,), jnp.float32)] * 3
    )
    (
        final_out, active_low, grad_outer_low, grad_inner_low, grad_attended, grad_mixture,
        normed_low, grad_residual, token_sums, inner_bias_sum,
    ) = token_layer(
        inputs, mixture, cotangent, w_out, w_inner, w_outer, wide(bias_inner)[None], rows
    )
    grad_outer_w = low(mm(active_low, grad_outer_low, tn))
    grad_inner_w = low(mm(normed_low, grad_inner_low, tn))
    grad_mixture, grad_outer_w, grad_inner_w = lax.optimization_barrier(
        (grad_mixture, grad_outer_w, grad_inner_w)
    )
    outer_sum, inner_sum = [wide(t) for t in lax.psum((grad_outer_w, grad_inner_w), both)]
    grad_projected, grad_keys, grad_values, grad_relative, small = attention_backward(
        0, PAIRS, probs, grad_mixture, mixture, inverse, query_content, query_position,
        query_segment, keys, values, relative, segment_embed, side, key_side,
    )
    sums = [
        Sum(low(mm(left, right, tn)), order)
        for left, right, order in (
            (mixture, grad_attended, 0), (inputs, grad_projected, 1), (frame, grad_keys, 0),
            (frame, grad_values, 1), (positions, grad_relative, 0),
        )
    ]
    vectors = Small(
        jnp.concatenate([small[:5], token_sums[:5], inner_bias_sum.reshape(-1, D),
                         jnp.zeros((2, D), jnp.float32)], axis=0)
    )
    for item in sums + [vectors]:
        while item.at < item.stages:
            item.step()
    out_sum, query_sum, key_sum, value_sum, rel_sum = [settle(item) for item in sums]
    grad_inputs = grad_residual + mm(grad_projected, w_query, nt)
    grad_content = (
        grad_inputs[:SEG] + mm(grad_keys[MEM:], w_key, nt) + mm(grad_values[MEM:], w_value, nt)
    )
    vectors = vectors.state
    names = ("content", "position", "segment", "embed0", "embed1", "gain1", "shift1", "gain2", "shift2", "outer")
    pieces = {name: vectors[index] for index, name in enumerate(names)}
    pieces["embed"] = vectors[3:5]
    pieces["inner"] = vectors[10:14].reshape(-1)
    return (
        low(final_out[None, :SEG]), low(final_out[None, SEG:]),
        low(grad_content[None]), low(grad_inputs[None, SEG:]),
        query_sum, key_sum, value_sum, out_sum, rel_sum,
        pieces["content"], pieces["position"], pieces["segment"], pieces["embed"].reshape(2, D),
        pieces["gain1"], pieces["shift1"], inner_sum, pieces["inner"], outer_sum, pieces["outer"],
        pieces["gain2"], pieces["shift2"],
    )


def solution(mesh):
    both = ("batch", "mem")
    rows = P(both, None, None)
    return jax.shard_map(
        shards,
        mesh=mesh,
        in_specs=(rows, rows, P("batch", "mem", None), P(both), P(both, None), P(both, None))
        + (P(),) * 17
        + (rows, rows),
        out_specs=(rows,) * 4 + (P(),) * 17,
        check_vma=False,
    )
```

```python
import jax
import jax.numpy as jnp
from jax import lax
from jax.experimental import pallas as pl
from jax.experimental.pallas import tpu as pltpu
from jax.sharding import PartitionSpec as P

D = 768
HEADS = 12
HEAD = 64
SEG = 512
MEM = 384
KEYS = MEM + SEG
REL = MEM + 2 * SEG
PAIR = 2 * HEAD
PAIRS = HEADS // 2
ROWS = 256
SUB = 128
CHUNK = 32
WIN = KEYS + SUB
FAR = -1e30
LOG2E = 1.4426950408889634
SCALE = HEAD**-0.5
VMEM_BYTES = 60 * 1024 * 1024
nt = (((1,), (1,)), ((), ()))
nn = (((1,), (0,)), ((), ()))
tn = (((0,), (0,)), ((), ()))


def mm(left, right, dims):
    return lax.dot_general(left, right, dims, preferred_element_type=jnp.float32)


def lane_low(rows):
    return lax.broadcasted_iota(jnp.int32, (rows, PAIR), 1) < HEAD


def tile_spans(tile):
    start = pl.multiple_of(tile * SUB, SUB)
    return [start, start + SEG]


def both_rows(ref, spans):
    return jnp.concatenate([ref[pl.ds(start, SUB), :] for start in spans], axis=0)


def forward_kernel(
    qc_ref, qp_ref, qs_ref, k_ref, v_ref, rel_ref, emb_ref, side_ref, key_side_ref, krank_ref,
    mix_ref, inv_ref, prob_ref, kcat, vcat,
):
    low_keys = lane_low(KEYS)
    same = key_side_ref[:, 0:1] == 0
    zero_row = emb_ref[0:1, :].astype(jnp.float32)
    one_row = emb_ref[1:2, :].astype(jnp.float32)
    zero_roll = pltpu.roll(zero_row, HEAD, 1)
    one_roll = pltpu.roll(one_row, HEAD, 1)
    low_row = lane_low(1)
    for head in range(2):
        if head == 0:
            near = jnp.where(low_row, zero_row, one_roll)
            away = jnp.where(low_row, one_row, zero_roll)
        else:
            near = jnp.where(low_row, zero_roll, one_row)
            away = jnp.where(low_row, one_roll, zero_row)
        kcat[head, :, :PAIR] = k_ref[...]
        kcat[head, :, PAIR:] = jnp.where(same, near, away).astype(jnp.bfloat16)
    vcat[:, :PAIR] = v_ref[...]
    vcat[:, PAIR:] = jnp.ones((KEYS, PAIR), jnp.bfloat16)

    def block(tile, carry):
        spans = tile_spans(tile)
        low = lane_low(ROWS)
        zero = jnp.zeros((ROWS, PAIR), jnp.bfloat16)
        qc = both_rows(qc_ref, spans)
        qp = both_rows(qp_ref, spans)
        qs = both_rows(qs_ref, spans)
        qs_roll = pltpu.roll(qs.astype(jnp.float32), HEAD, 1).astype(jnp.bfloat16)
        side = both_rows(side_ref, spans)
        seg_keep = (side[:, 0:1] == 0) == low
        krank = krank_ref[...]
        factor = SCALE * LOG2E
        window = rel_ref[pl.ds(3 - tile, WIN // SUB)].reshape(WIN, PAIR)
        grid = mm(
            jnp.concatenate([jnp.where(low, qp, zero), jnp.where(low, zero, qp)], axis=0), window, nt
        )
        parts = []
        for head in range(2):
            mine = low if head == 0 else ~low
            twice = jnp.where(mine, qs, qs_roll)
            qcat = jnp.concatenate(
                [jnp.where(mine, qc, zero), jnp.where(seg_keep, twice, zero)], axis=1
            )
            score = mm(qcat, kcat[head], nt)
            for row in range(0, ROWS, CHUNK):
                at = row % SUB
                shifted = pltpu.roll(
                    grid[head * ROWS + row : head * ROWS + row + CHUNK],
                    WIN - SUB + 1 + at, 1, stride=1, stride_axis=0,
                )[:, :KEYS]
                logit = score[row : row + CHUNK] + shifted
                current = jnp.where(krank <= side[row : row + CHUNK, 1:2], logit[:, MEM:], FAR)
                logit = jnp.concatenate([logit[:, :MEM], current], axis=1)
                top = jnp.max(logit, axis=-1, keepdims=True)
                soft = jnp.exp2((logit - top) * factor).astype(jnp.bfloat16)
                prob_ref[head, pl.ds(spans[row // SUB] + at, CHUNK), :] = soft
                parts.append(soft)
        summed = mm(jnp.concatenate(parts, axis=0), vcat[...], nn)
        scale = 1.0 / summed[:, PAIR:]
        mixed = summed[:, :PAIR] * scale
        mixed = jnp.where(low, mixed[:ROWS], mixed[ROWS:]).astype(jnp.bfloat16)
        scale = jnp.where(low, scale[:ROWS], scale[ROWS:])
        for index, start in enumerate(spans):
            mix_ref[pl.ds(start, SUB), :] = mixed[index * SUB : (index + 1) * SUB]
            inv_ref[pl.ds(start, SUB), :] = scale[index * SUB : (index + 1) * SUB]
        return carry

    lax.fori_loop(0, SEG // SUB, block, 0)


def whole(rows, lanes):
    return pl.BlockSpec((rows, lanes), lambda p: (0, 0))


def attention_forward(qc, qp, qs, keys, values, rel, emb, side, key_side, krank):
    pair = lambda rows: pl.BlockSpec((rows, PAIR), lambda p: (0, p))
    return pl.pallas_call(
        forward_kernel,
        grid=(PAIRS,),
        in_specs=[
            pair(2 * SEG), pair(2 * SEG), pair(2 * SEG), pair(KEYS), pair(KEYS),
            pl.BlockSpec((REL // SUB, SUB, PAIR), lambda p: (0, 0, p)),
            pair(2), whole(*side.shape), whole(*key_side.shape), whole(1, SEG),
        ],
        out_specs=[
            pair(2 * SEG), pair(2 * SEG),
            pl.BlockSpec((None, 2, 2 * SEG, KEYS), lambda p: (p, 0, 0, 0)),
        ],
        out_shape=[
            jax.ShapeDtypeStruct((2 * SEG, D), jnp.bfloat16),
            jax.ShapeDtypeStruct((2 * SEG, D), jnp.float32),
            jax.ShapeDtypeStruct((PAIRS, 2, 2 * SEG, KEYS), jnp.bfloat16),
        ],
        scratch_shapes=[
            pltpu.VMEM((2, KEYS, 2 * PAIR), jnp.bfloat16),
            pltpu.VMEM((KEYS, 2 * PAIR), jnp.bfloat16),
        ],
        compiler_params=pltpu.CompilerParams(
            dimension_semantics=("arbitrary",), vmem_limit_bytes=VMEM_BYTES
        ),
        cost_estimate=pl.CostEstimate(
            flops=30000000000, transcendentals=11000000, bytes_accessed=30000000
        ),
        name="attention_forward",
    )(qc, qp, qs, keys, values, rel.reshape(REL // SUB, SUB, D), emb, side, key_side, krank)


def backward_kernel(
    prob_ref, dmix_ref, mix_ref, inv_ref, qc_ref, qp_ref, qs_ref, k_ref, v_ref, rel_ref, emb_ref,
    side_ref, key_side_ref, inputs_ref, frame_ref, positions_ref, *rest,
):
    dproj_ref, dk_ref, dv_ref, small_ref, bucket_ref, kcat, dk_acc, dv_acc, drel_acc = rest[-9:]
    kcat[:, :PAIR] = k_ref[...]
    kcat[:, PAIR:] = jnp.where((key_side_ref[:, 0:1] == 0) == lane_low(KEYS), 1.0, 0.0).astype(
        jnp.bfloat16
    )
    dk_acc[...] = jnp.zeros_like(dk_acc)
    dv_acc[...] = jnp.zeros_like(dv_acc)
    drel_acc[...] = jnp.zeros_like(drel_acc)
    small_ref[...] = jnp.zeros_like(small_ref)

    def block(tile, carry):
        spans = tile_spans(tile)
        low = lane_low(ROWS)
        zero = jnp.zeros((ROWS, PAIR), jnp.bfloat16)
        row_index = lax.broadcasted_iota(jnp.int32, (ROWS, ROWS), 0)
        column_index = lax.broadcasted_iota(jnp.int32, (ROWS, ROWS), 1)
        flip = jnp.where(
            (row_index // SUB == column_index // SUB)
            & (row_index % SUB + column_index % SUB == SUB - 1),
            1.0, 0.0,
        ).astype(jnp.bfloat16)
        dmix = (
            both_rows(dmix_ref, spans).astype(jnp.float32) * (both_rows(inv_ref, spans) * SCALE)
        ).astype(jnp.bfloat16)
        weighted = dmix.astype(jnp.float32) * both_rows(mix_ref, spans).astype(jnp.float32)
        qc = both_rows(qc_ref, spans)
        qp = both_rows(qp_ref, spans)
        qs = both_rows(qs_ref, spans).astype(jnp.float32)
        qp_turned = mm(flip, qp, nn).astype(jnp.bfloat16)
        first = both_rows(side_ref, spans)[:, 0:1] == 0
        emb = emb_ref[...].astype(jnp.float32)
        dm = jnp.concatenate([jnp.where(low, dmix, zero), jnp.where(low, zero, dmix)], axis=0)
        qc_both = jnp.concatenate([jnp.where(low, qc, zero), jnp.where(low, zero, qc)], axis=0)
        qp_both = jnp.concatenate(
            [jnp.where(low, qp_turned, zero), jnp.where(low, zero, qp_turned)], axis=0
        )
        row_sum = jnp.concatenate(
            [
                jnp.sum(jnp.where(low, weighted, 0.0), axis=-1, keepdims=True),
                jnp.sum(jnp.where(low, 0.0, weighted), axis=-1, keepdims=True),
            ],
            axis=0,
        )
        prob = jnp.concatenate([both_rows(prob_ref.at[head], spans) for head in range(2)], axis=0)
        dprob = mm(dm, v_ref[...], nt)
        total = jnp.concatenate(
            [
                (
                    prob[at : at + CHUNK].astype(jnp.float32)
                    * (dprob[at : at + CHUNK] - row_sum[at : at + CHUNK])
                ).astype(jnp.bfloat16)
                for at in range(0, 2 * ROWS, CHUNK)
            ],
            axis=0,
        )
        back = mm(total, kcat[...], nn)
        turned = [mm(flip, total[head * ROWS : (head + 1) * ROWS], nn) for head in range(2)]
        grid = jnp.concatenate(
            [
                pltpu.roll(
                    jnp.concatenate(
                        [turned[head][row : row + CHUNK], jnp.zeros((CHUNK, SUB), jnp.float32)],
                        axis=1,
                    ),
                    row % SUB, 1, stride=1, stride_axis=0,
                ).astype(jnp.bfloat16)
                for head in range(2)
                for row in range(0, ROWS, CHUNK)
            ],
            axis=0,
        )
        window = rel_ref[pl.ds(3 - tile, WIN // SUB)].reshape(WIN, PAIR)
        dqp = mm(grid, window, nn)
        dqp = jnp.where(low, dqp[:ROWS], dqp[ROWS:]).astype(jnp.bfloat16)
        dqp_wide = mm(flip, dqp, nn)
        dv_acc[...] += mm(dm, prob, tn)
        dk_acc[...] += mm(qc_both, total, tn)
        drel = mm(qp_both, grid, tn)
        for part in range(WIN // SUB):
            drel_acc[3 - tile + part] += drel[:, part * SUB : (part + 1) * SUB]
        dqc_wide = (
            jnp.where(low, back[:ROWS, :PAIR], back[ROWS:, :PAIR])
            .astype(jnp.bfloat16)
            .astype(jnp.float32)
        )
        sums = [back[head * ROWS : (head + 1) * ROWS, PAIR:] for head in range(2)]
        rolled = [pltpu.roll(part, HEAD, 1) for part in sums]
        key_zero = jnp.where(low, sums[0], rolled[1])
        key_one = jnp.where(low, rolled[0], sums[1])
        near = jnp.where(first, key_zero, key_one)
        other = jnp.where(first, key_one, key_zero)
        dqs_wide = (near * emb[0:1] + other * emb[1:2]).astype(jnp.bfloat16).astype(jnp.float32)
        dproj = (dqc_wide + dqp_wide + dqs_wide).astype(jnp.bfloat16)
        for index, start in enumerate(spans):
            dproj_ref[pl.ds(start, SUB), :] = dproj[index * SUB : (index + 1) * SUB]
        rows = [dqc_wide, dqp_wide, dqs_wide, near * qs, other * qs]
        for row, value in enumerate(rows):
            small_ref[row : row + 1, :] += jnp.sum(value, axis=0, keepdims=True)
        return carry

    lax.fori_loop(0, SEG // SUB, block, 0, unroll=True)
    dk_low = dk_acc[...].astype(jnp.bfloat16)
    dv_low = (dv_acc[...] * (1.0 / SCALE)).astype(jnp.bfloat16)
    dk_ref[...] = dk_low.T
    dv_ref[...] = dv_low.T
    drel_low = jnp.concatenate(
        [drel_acc[part] for part in range(REL // SUB)], axis=1
    ).astype(jnp.bfloat16)
    grads = (
        mm(dproj_ref[...], inputs_ref[...], tn), mm(dk_low, frame_ref[...], nn),
        mm(dv_low, frame_ref[...], nn), mm(drel_low, positions_ref[...], nn),
    )
    for index, grad in enumerate(grads):
        bucket_ref[index * PAIR : (index + 1) * PAIR, :] = grad.astype(jnp.bfloat16)


def attention_backward(
    first, count, bucket_block, chain, prob, dmix, mix, inv, qc, qp, qs, keys, values, rel, emb, side,
    key_side, inputs, frame, positions,
):
    pair = lambda rows: pl.BlockSpec((rows, PAIR), lambda p: (0, first + p))
    rel_block = pl.BlockSpec((REL // SUB, SUB, PAIR), lambda p: (0, 0, first + p))
    bucket_rows = chain[4] if isinstance(chain[4], int) else chain[4].shape[0]
    passed = [item for item in chain if not isinstance(item, int) and item is not None]
    places = [at for at, item in enumerate(chain) if not isinstance(item, int) and item is not None]
    return pl.pallas_call(
        backward_kernel,
        grid=(count,),
        in_specs=[
            pl.BlockSpec((None, 2, 2 * SEG, KEYS), lambda p: (first + p, 0, 0, 0)),
            pair(2 * SEG), pair(2 * SEG), pair(2 * SEG), pair(2 * SEG), pair(2 * SEG), pair(2 * SEG),
            pair(KEYS), pair(KEYS), rel_block, pair(2), whole(*side.shape), whole(*key_side.shape),
            whole(2 * SEG, D), whole(KEYS, D), whole(REL, D),
        ]
        + [pl.BlockSpec(memory_space=pl.ANY)] * len(passed),
        out_specs=[
            pair(2 * SEG), pair(KEYS), pair(KEYS), pair(8),
            pl.BlockSpec((4 * PAIR, D), lambda p: (bucket_block + p, 0)),
        ],
        out_shape=[
            jax.ShapeDtypeStruct((2 * SEG, D), jnp.bfloat16),
            jax.ShapeDtypeStruct((KEYS, D), jnp.bfloat16),
            jax.ShapeDtypeStruct((KEYS, D), jnp.bfloat16),
            jax.ShapeDtypeStruct((8, D), jnp.float32),
            jax.ShapeDtypeStruct((bucket_rows, D), jnp.bfloat16),
        ],
        scratch_shapes=[
            pltpu.VMEM((KEYS, 2 * PAIR), jnp.bfloat16),
            pltpu.VMEM((PAIR, KEYS), jnp.float32),
            pltpu.VMEM((PAIR, KEYS), jnp.float32),
            pltpu.VMEM((REL // SUB, PAIR, SUB), jnp.float32),
        ],
        input_output_aliases={16 + index: at for index, at in enumerate(places)},
        compiler_params=pltpu.CompilerParams(
            dimension_semantics=("arbitrary",), vmem_limit_bytes=VMEM_BYTES
        ),
        cost_estimate=pl.CostEstimate(
            flops=count * 8000000000, transcendentals=0, bytes_accessed=count * 8000000
        ),
        name="attention_backward",
    )(
        prob, dmix, mix, inv, qc, qp, qs, keys, values, rel.reshape(REL // SUB, SUB, D), emb, side,
        key_side, inputs, frame, positions, *passed,
    )


norm_epsilon = 1e-06
TOKENS = 256
FF_CHUNK = 768
half_erfc = (0.5 * 0.254829592, 0.5 * -0.284496736, 0.5 * 1.421413741, 0.5 * -1.453152027, 0.5 * 1.061405429)


def gelu_pair(x):
    gauss = jnp.exp2(x * x * (-0.5 * LOG2E))
    t = 1.0 / (1.0 + (0.3275911 * 0.7071067811865476) * jnp.abs(x))
    a1, a2, a3, a4, a5 = half_erfc
    tail = t * (a1 + t * (a2 + t * (a3 + t * (a4 + t * a5)))) * gauss
    cdf = jnp.where(x >= 0.0, 1.0 - tail, tail)
    return x * cdf, cdf + x * gauss * 0.3989422804014327


def normalise(tensor):
    centred = tensor - jnp.mean(tensor, axis=-1, keepdims=True)
    inverse = lax.rsqrt(jnp.mean(centred * centred, axis=-1, keepdims=True) + norm_epsilon)
    return centred * inverse, inverse


def norm_back(grad, hat, inverse):
    return inverse * (
        grad
        - jnp.mean(grad, axis=-1, keepdims=True)
        - hat * jnp.mean(grad * hat, axis=-1, keepdims=True)
    )


def token_kernel(
    x_ref, mix_ref, cot_ref, wo_ref, wi_ref, wf_ref, bias_inner_ref, rows_ref,
    final_ref, active_ref, outer_ref, inner_ref, attended_ref, dmix_ref, low_ref, residual_ref,
    sums_ref, inner_sum_ref,
    slope,
):
    @pl.when(pl.program_id(0) == 0)
    def _():
        sums_ref[...] = jnp.zeros_like(sums_ref)
        inner_sum_ref[...] = jnp.zeros_like(inner_sum_ref)

    gain_one, shift_one = rows_ref[0:1, :], rows_ref[1:2, :]
    gain_two, shift_two = rows_ref[2:3, :], rows_ref[3:4, :]
    bias_outer = rows_ref[4:5, :]
    hat_one, inverse_one = normalise(
        x_ref[...].astype(jnp.float32) + mm(mix_ref[...], wo_ref[...], nn)
    )
    normed = hat_one * gain_one + shift_one
    normed_low = normed.astype(jnp.bfloat16)
    low_ref[...] = normed_low
    chunks = [slice(at, at + FF_CHUNK) for at in range(0, wi_ref.shape[1], FF_CHUNK)]
    pre = mm(normed_low, wi_ref[:, chunks[0]], nn)
    total = normed + bias_outer
    for index, chunk in enumerate(chunks):
        here = pre + bias_inner_ref[:, chunk]
        if index + 1 < len(chunks):
            pre = mm(normed_low, wi_ref[:, chunks[index + 1]], nn)
        value, derivative = gelu_pair(here)
        value = value.astype(jnp.bfloat16)
        active_ref[:, chunk] = value
        slope[:, chunk] = derivative
        total = total + mm(value, wf_ref[chunk, :], nn)
    hat_two, inverse_two = normalise(total)
    final_ref[...] = (hat_two * gain_two + shift_two).astype(jnp.bfloat16)
    cot = cot_ref[...].astype(jnp.float32)
    grad_total = norm_back(cot * gain_two, hat_two, inverse_two)
    grad_outer = grad_total.astype(jnp.bfloat16)
    outer_ref[...] = grad_outer
    sums_ref[2:3, :] += jnp.sum(cot * hat_two, axis=0, keepdims=True)
    sums_ref[3:4, :] += jnp.sum(cot, axis=0, keepdims=True)
    sums_ref[4:5, :] += jnp.sum(grad_outer.astype(jnp.float32), axis=0, keepdims=True)
    back = mm(grad_outer, wf_ref[chunks[0], :], nt)
    for index, chunk in enumerate(chunks):
        here = back
        if index + 1 < len(chunks):
            back = mm(grad_outer, wf_ref[chunks[index + 1], :], nt)
        grad_inner = (here * slope[:, chunk]).astype(jnp.bfloat16)
        inner_ref[:, chunk] = grad_inner
        inner_sum_ref[:, chunk] += jnp.sum(grad_inner.astype(jnp.float32), axis=0, keepdims=True)
        grad_total = grad_total + mm(grad_inner, wi_ref[:, chunk], nt)
    sums_ref[0:1, :] += jnp.sum(grad_total * hat_one, axis=0, keepdims=True)
    sums_ref[1:2, :] += jnp.sum(grad_total, axis=0, keepdims=True)
    residual = norm_back(grad_total * gain_one, hat_one, inverse_one)
    residual_ref[...] = residual
    attended = residual.astype(jnp.bfloat16)
    attended_ref[...] = attended
    dmix_ref[...] = mm(attended, wo_ref[...], nt).astype(jnp.bfloat16)


def token_layer(x, mix, cot, w_out, w_inner, w_outer, bias_inner, rows):
    count = x.shape[0]
    hidden = w_inner.shape[1]
    tile = lambda lanes: pl.BlockSpec((TOKENS, lanes), lambda i: (i, 0))
    once = lambda a, b: pl.BlockSpec((a, b), lambda i: (0, 0), pipeline_mode=pl.Buffered(1))
    sums = lambda a, b: pl.BlockSpec((a, b), lambda i: (0, 0))
    low = lambda lanes: jax.ShapeDtypeStruct((count, lanes), jnp.bfloat16)
    return pl.pallas_call(
        token_kernel,
        grid=(count // TOKENS,),
        in_specs=[
            tile(D), tile(D), tile(D), once(D, D), once(D, hidden), once(hidden, D),
            once(1, hidden), once(8, D),
        ],
        out_specs=[
            tile(D), tile(hidden), tile(D), tile(hidden), tile(D), tile(D), tile(D), tile(D),
            sums(8, D), sums(1, hidden),
        ],
        out_shape=[
            low(D), low(hidden), low(D), low(hidden), low(D), low(D), low(D),
            jax.ShapeDtypeStruct((count, D), jnp.float32),
            jax.ShapeDtypeStruct((8, D), jnp.float32),
            jax.ShapeDtypeStruct((1, hidden), jnp.float32),
        ],
        scratch_shapes=[pltpu.VMEM((TOKENS, hidden), jnp.float32)],
        compiler_params=pltpu.CompilerParams(
            dimension_semantics=("arbitrary",), vmem_limit_bytes=VMEM_BYTES
        ),
        cost_estimate=pl.CostEstimate(
            flops=22000000000, transcendentals=6000000, bytes_accessed=40000000
        ),
        name="token_layer",
    )(x, mix, cot, w_out, w_inner, w_outer, bias_inner, rows)


def chip_bits():
    bits = []
    bit = 2
    while bit < lax.axis_size("batch"):
        bits.append(bit)
        bit *= 2
    return bits


def digit(bit):
    return lax.axis_index("batch") // bit % 2


def across(tensor, bits):
    count = lax.axis_size("batch")
    return lax.ppermute(tensor, "batch", [(i, i ^ bits[i & 1]) for i in range(count)])


def own_digit(bits):
    return jnp.where(digit(1) == 1, digit(bits[1]), digit(bits[0]))


def along(tensor, shift):
    ring = lax.axis_size("mem")
    return lax.ppermute(tensor, "mem", [(i, (i + shift) % ring) for i in range(ring)])


def rows_of(tensor, start, count):
    return lax.dynamic_slice(tensor, (start, 0), (count, tensor.shape[1]))


class Sum:
    def __init__(self, tensor):
        bits = chip_bits()
        self.bits = [(1, 1)] + list(zip(bits, bits[::-1]))
        self.state = tensor
        self.at = 0
        self.stages = 2 * len(self.bits) + 2

    def step(self):
        count, tensor = len(self.bits), self.state
        ring, me = lax.axis_size("mem"), lax.axis_index("mem")
        if self.at < count:
            bit = self.bits[self.at]
            half = tensor.shape[0] // 2
            mine = own_digit(bit)
            got = across(rows_of(tensor, (1 - mine) * half, half), bit)
            kept = rows_of(tensor, mine * half, half)
            self.state = (kept.astype(jnp.float32) + got.astype(jnp.float32)).astype(jnp.bfloat16)
        elif self.at == count:
            block = tensor.shape[0] // ring
            total = rows_of(tensor, me * block, block).astype(jnp.float32)
            for shift in range(1, ring):
                sent = rows_of(tensor, (me + shift) % ring * block, block)
                total = total + along(sent, shift).astype(jnp.float32)
            self.state = total.astype(jnp.bfloat16)
        elif self.at == count + 1:
            parts = [tensor] + [along(tensor, shift) for shift in range(1, ring)]
            self.state = jnp.concatenate(parts, axis=0)
        else:
            bit = self.bits[2 * count + 1 - self.at]
            self.state = jnp.concatenate([tensor, across(tensor, bit)], axis=0)
        self.at += 1

    def places(self):
        ring = lax.axis_size("mem")
        weight = ring * lax.axis_size("batch") // 2
        index = jnp.arange(2 * weight, dtype=jnp.int32)
        place = (lax.axis_index("mem") - index % ring) % ring
        core = index // weight % 2
        for even, odd in self.bits:
            own = jnp.where(core == 1, digit(odd), digit(even))
            place = place + (index // weight % 2 + own) % 2 * weight
            weight //= 2
        return place


def placed(item):
    tensor, place = item.state, item.places()
    blocks = place.shape[0]
    if tensor.shape[0] // blocks % 8:
        tensor = tensor.reshape(blocks, -1, tensor.shape[1])[place].reshape(tensor.shape)
        place = jnp.arange(8, dtype=jnp.int32)
    return tensor, place


def block_of(place_ref, in_ref, index):
    rows = in_ref.shape[0] // place_ref.shape[0]
    start = pl.multiple_of(place_ref[index] * rows, 8)
    return in_ref[pl.ds(start, rows), :].astype(jnp.float32)


def settle_pairs_kernel(place_ref, in_ref, *rest):
    outs, full = rest[:-1], rest[-1]
    rows = in_ref.shape[0] // place_ref.shape[0]
    grads = PAIRS * 4 * PAIR

    @pl.when(pl.program_id(0) == 0)
    def _():
        for item in range(place_ref.shape[0]):
            full[item * rows : (item + 1) * rows, :] = block_of(place_ref, in_ref, item)
        outs[4][...] = full[grads : grads + D, :]
        outs[5][...] = full[grads + D : grads + D + outs[5].shape[0], :]

    for index in range(4):
        start = pl.multiple_of((pl.program_id(0) * 4 + index) * PAIR, PAIR)
        outs[index][...] = full[pl.ds(start, PAIR), :].T


def settle_pairs(item):
    tensor, place = placed(item)
    rows, lanes = tensor.shape
    square = jax.ShapeDtypeStruct((D, D), jnp.float32)
    whole_out = lambda count: pl.BlockSpec((count, lanes), lambda i, p: (0, 0))
    return pl.pallas_call(
        settle_pairs_kernel,
        grid_spec=pltpu.PrefetchScalarGridSpec(
            num_scalar_prefetch=1,
            grid=(PAIRS,),
            in_specs=[pl.BlockSpec((rows, lanes), lambda i, p: (0, 0))],
            out_specs=[pl.BlockSpec((lanes, PAIR), lambda i, p: (0, i))] * 4
            + [whole_out(D), whole_out(VECTORS)],
            scratch_shapes=[pltpu.VMEM((rows, lanes), jnp.float32)],
        ),
        out_shape=[square] * 5 + [jax.ShapeDtypeStruct((VECTORS, lanes), jnp.float32)],
        compiler_params=pltpu.CompilerParams(vmem_limit_bytes=48 * 1024 * 1024),
        name="settle_pairs",
    )(place, tensor)


def sinusoid():
    fine_count = 32
    frequency = 1.0 / 10000.0 ** (
        jnp.arange(0, D, 2, dtype=jnp.int32).astype(jnp.float32) / D
    )
    coarse = (KEYS - 1 - fine_count * jnp.arange(REL // fine_count, dtype=jnp.int32)).astype(
        jnp.float32
    )[:, None] * frequency[None]
    fine = jnp.arange(fine_count, dtype=jnp.int32).astype(jnp.float32)[:, None] * frequency[None]
    sin_coarse, cos_coarse = jnp.sin(coarse)[:, None], jnp.cos(coarse)[:, None]
    sin_fine, cos_fine = jnp.sin(fine)[None], jnp.cos(fine)[None]
    sine = sin_coarse * cos_fine - cos_coarse * sin_fine
    cosine = cos_coarse * cos_fine + sin_coarse * sin_fine
    return jnp.concatenate([sine, cosine], axis=-1).reshape(REL, D).astype(jnp.bfloat16)


EXTRA = 256
VECTORS = 24


WIDE = 512


def wide_grads_kernel(outer_ref, active_ref, low_ref, inner_ref, out_ref, left):
    part = pl.program_id(0)

    @pl.when(pl.program_id(1) == 0)
    def _():
        @pl.when(part == 0)
        def _():
            left[...] = outer_ref[...].T

        @pl.when(part == 1)
        def _():
            left[...] = low_ref[...].T

    @pl.when(part == 0)
    def _():
        out_ref[...] = mm(left[...], active_ref[...], nn).astype(jnp.bfloat16)

    @pl.when(part == 1)
    def _():
        out_ref[...] = mm(left[...], inner_ref[...], nn).astype(jnp.bfloat16)


def wide_grads(grad_outer, active, normed_low, grad_inner):
    tokens, hidden = active.shape
    steps = hidden // WIDE
    return pl.pallas_call(
        wide_grads_kernel,
        grid=(2, steps),
        in_specs=[
            pl.BlockSpec((tokens, D), lambda p, i: (0, 0)),
            pl.BlockSpec((tokens, WIDE), lambda p, i: (0, jnp.where(p == 0, i, steps - 1))),
            pl.BlockSpec((tokens, D), lambda p, i: (0, 0)),
            pl.BlockSpec((tokens, WIDE), lambda p, i: (0, jnp.where(p == 0, 0, i))),
        ],
        out_specs=pl.BlockSpec((D, WIDE), lambda p, i: (p, i)),
        out_shape=jax.ShapeDtypeStruct((2 * D, hidden), jnp.bfloat16),
        scratch_shapes=[pltpu.VMEM((D, tokens), jnp.bfloat16)],
        compiler_params=pltpu.CompilerParams(
            dimension_semantics=("arbitrary",) * 2, vmem_limit_bytes=VMEM_BYTES
        ),
        cost_estimate=pl.CostEstimate(
            flops=9700000000, transcendentals=0, bytes_accessed=25000000
        ),
        name="wide_grads",
    )(grad_outer, active, normed_low, grad_inner)


def widen_kernel(outer_ref, inner_ref, outer_out, inner_out):
    outer_out[...] = outer_ref[...].astype(jnp.float32).T
    inner_out[...] = inner_ref[...].astype(jnp.float32)


def widen(summed):
    hidden = summed.shape[1]
    return pl.pallas_call(
        widen_kernel,
        grid=(hidden // WIDE,),
        in_specs=[
            pl.BlockSpec((D, WIDE), lambda i: (0, i)),
            pl.BlockSpec((D, WIDE), lambda i: (1, i)),
        ],
        out_specs=[
            pl.BlockSpec((WIDE, D), lambda i: (i, 0)),
            pl.BlockSpec((D, WIDE), lambda i: (0, i)),
        ],
        out_shape=[
            jax.ShapeDtypeStruct((hidden, D), jnp.float32),
            jax.ShapeDtypeStruct((D, hidden), jnp.float32),
        ],
        compiler_params=pltpu.CompilerParams(vmem_limit_bytes=VMEM_BYTES),
        name="widen",
    )(summed, summed)


def shards(
    content_in, query_in, memory, sequence_lengths, order_rank, segment_ids,
    w_query, w_key, w_value, w_out, w_rel,
    bias_content, bias_position, bias_segment, segment_embed,
    gain_one, shift_one, w_inner, bias_inner, w_outer, bias_outer, gain_two, shift_two,
    content_cotangent, query_cotangent,
):
    wide = lambda tensor: tensor.astype(jnp.float32)
    low = lambda tensor: tensor.astype(jnp.bfloat16)
    both = ("batch", "mem")
    past = lax.all_to_all(memory, "mem", split_axis=0, concat_axis=1, tiled=True)[0]
    content = content_in[0]
    inputs = jnp.concatenate([content, query_in[0]], axis=0)
    cotangent = jnp.concatenate([content_cotangent[0], query_cotangent[0]], axis=0)
    segment = segment_ids[0]
    rank = order_rank[0]
    zeros = jnp.zeros((2 * SEG, 6), jnp.int32)
    side = jnp.concatenate(
        [
            jnp.concatenate([segment, segment])[:, None],
            jnp.concatenate([rank, rank - 1])[:, None],
            zeros,
        ],
        axis=1,
    )
    key_side = jnp.concatenate([jnp.zeros((MEM, 8), jnp.int32), side[:SEG]], axis=0)
    live = jnp.arange(SEG, dtype=jnp.int32) < sequence_lengths[0]
    key_rank = jnp.where(live, rank, 2 * SEG)[None, :]

    positions = sinusoid()
    relative = low(mm(positions, w_rel, nn))
    frame = jnp.concatenate([past, content], axis=0)
    keys = low(mm(frame, w_key, nn))
    values = low(mm(frame, w_value, nn))
    projected = mm(inputs, w_query, nn)
    query_content = low(projected + wide(bias_content))
    query_position = low(projected + wide(bias_position))
    query_segment = low(projected + wide(bias_segment))
    mixture, inverse, probs = attention_forward(
        query_content, query_position, query_segment, keys, values, relative, segment_embed,
        side, key_side, key_rank,
    )
    rows = jnp.stack(
        [wide(t) for t in (gain_one, shift_one, gain_two, shift_two, bias_outer)]
        + [jnp.zeros((D,), jnp.float32)] * 3
    )
    (
        final_out, active_low, grad_outer_low, grad_inner_low, grad_attended, grad_mixture,
        normed_low, grad_residual, token_sums, inner_bias_sum,
    ) = token_layer(
        inputs, mixture, cotangent, w_out, w_inner, w_outer, wide(bias_inner)[None], rows
    )
    low_mm = lambda left, right: low(mm(left, right, tn))
    wide_sum = wide_grads(grad_outer_low, active_low, normed_low, grad_inner_low)
    wide_sum, grad_mixture, grad_attended = lax.optimization_barrier(
        (wide_sum, grad_mixture, grad_attended)
    )
    wide_sum = lax.psum(wide_sum, both)
    group_rows = PAIRS * 4 * PAIR

    def attention_part(operands):
        (
            probs, grad_mixture, mixture, inverse, query_content, query_position, query_segment,
            keys, values, relative, side, key_side, inputs, frame, positions, grad_attended,
            token_sums, inner_bias_sum, segment_embed, grad_residual, w_query, w_key, w_value,
        ) = operands
        grad_projected, grad_keys, grad_values, small, bucket = attention_backward(
            0, PAIRS, 0, [None] * 4 + [group_rows + D + EXTRA], probs, grad_mixture, mixture,
            inverse, query_content, query_position, query_segment, keys, values, relative,
            segment_embed, side, key_side, inputs, frame, positions,
        )
        vectors = jnp.concatenate(
            [token_sums, inner_bias_sum.reshape(-1, D), jnp.zeros((4, D), jnp.float32), small], axis=0
        )
        vectors = jnp.pad(vectors, ((0, EXTRA - vectors.shape[0]), (0, 0)))
        others = jnp.concatenate([low_mm(mixture, grad_attended), low(vectors)], axis=0)
        rest = Sum(lax.dynamic_update_slice(bucket, others, (group_rows, 0)))
        while rest.at < rest.stages:
            rest.step()
        grad_inputs = grad_residual + mm(grad_projected, w_query, nt)
        grad_content = (
            grad_inputs[:SEG] + mm(grad_keys[MEM:], w_key, nt) + mm(grad_values[MEM:], w_value, nt)
        )
        return low(grad_content), low(grad_inputs[SEG:]), rest.state

    operands = (
        probs, grad_mixture, mixture, inverse, query_content, query_position, query_segment, keys,
        values, relative, side, key_side, inputs, frame, positions, grad_attended, token_sums,
        inner_bias_sum, segment_embed, grad_residual, w_query, w_key, w_value,
    )
    shapes = jax.eval_shape(attention_part, operands)
    grad_content, grad_query, gathered = lax.cond(
        sequence_lengths[0] > -1,
        attention_part,
        lambda operands: tuple(jnp.zeros(item.shape, item.dtype) for item in shapes),
        operands,
    )
    rest = Sum(gathered)
    outer_sum, inner_sum = widen(wide_sum)
    query_sum, key_sum, value_sum, rel_sum, out_sum, vectors = settle_pairs(rest)
    pieces = {
        "gain1": vectors[0], "shift1": vectors[1], "gain2": vectors[2], "shift2": vectors[3],
        "outer": vectors[4], "inner": vectors[8:12].reshape(-1), "content": vectors[16],
        "position": vectors[17], "segment": vectors[18], "embed": vectors[19:21],
    }
    return (
        low(final_out[None, :SEG]), low(final_out[None, SEG:]),
        grad_content[None], grad_query[None],
        query_sum, key_sum, value_sum, out_sum, rel_sum,
        pieces["content"], pieces["position"], pieces["segment"], pieces["embed"].reshape(2, D),
        pieces["gain1"], pieces["shift1"], inner_sum, pieces["inner"], outer_sum, pieces["outer"],
        pieces["gain2"], pieces["shift2"],
    )


def solution(mesh):
    both = ("batch", "mem")
    rows = P(both, None, None)
    return jax.shard_map(
        shards,
        mesh=mesh,
        in_specs=(rows, rows, P("batch", "mem", None), P(both), P(both, None), P(both, None))
        + (P(),) * 17
        + (rows, rows),
        out_specs=(rows,) * 4 + (P(),) * 17,
        check_vma=False,
    )
```

```python
import jax
import jax.numpy as jnp
from jax import lax
from jax.experimental import pallas as pl
from jax.experimental.pallas import tpu as pltpu
from jax.sharding import PartitionSpec as P

D = 768
HEADS = 12
HEAD = 64
SEG = 512
MEM = 384
KEYS = MEM + SEG
REL = MEM + 2 * SEG
PAIR = 2 * HEAD
PAIRS = HEADS // 2
ROWS = 256
SUB = 128
CHUNK = 32
WIN = KEYS + SUB
FAR = -1e30
LOG2E = 1.4426950408889634
SCALE = HEAD**-0.5
VMEM_BYTES = 60 * 1024 * 1024
nt = (((1,), (1,)), ((), ()))
nn = (((1,), (0,)), ((), ()))
tn = (((0,), (0,)), ((), ()))


def mm(left, right, dims):
    return lax.dot_general(left, right, dims, preferred_element_type=jnp.float32)


def lane_low(rows):
    return lax.broadcasted_iota(jnp.int32, (rows, PAIR), 1) < HEAD


def tile_spans(tile):
    start = pl.multiple_of(tile * SUB, SUB)
    return [start, start + SEG]


def both_rows(ref, spans):
    return jnp.concatenate([ref[pl.ds(start, SUB), :] for start in spans], axis=0)


def forward_kernel(
    qc_ref, qp_ref, qs_ref, k_ref, v_ref, rel_ref, emb_ref, side_ref, key_side_ref, krank_ref,
    mix_ref, inv_ref, prob_ref, kcat, vcat,
):
    low_keys = lane_low(KEYS)
    same = key_side_ref[:, 0:1] == 0
    zero_row = emb_ref[0:1, :].astype(jnp.float32)
    one_row = emb_ref[1:2, :].astype(jnp.float32)
    zero_roll = pltpu.roll(zero_row, HEAD, 1)
    one_roll = pltpu.roll(one_row, HEAD, 1)
    low_row = lane_low(1)
    for head in range(2):
        if head == 0:
            near = jnp.where(low_row, zero_row, one_roll)
            away = jnp.where(low_row, one_row, zero_roll)
        else:
            near = jnp.where(low_row, zero_roll, one_row)
            away = jnp.where(low_row, one_roll, zero_row)
        kcat[head, :, :PAIR] = k_ref[...]
        kcat[head, :, PAIR:] = jnp.where(same, near, away).astype(jnp.bfloat16)
    vcat[:, :PAIR] = v_ref[...]
    vcat[:, PAIR:] = jnp.ones((KEYS, PAIR), jnp.bfloat16)

    def block(tile, carry):
        spans = tile_spans(tile)
        low = lane_low(ROWS)
        zero = jnp.zeros((ROWS, PAIR), jnp.bfloat16)
        qc = both_rows(qc_ref, spans)
        qp = both_rows(qp_ref, spans)
        qs = both_rows(qs_ref, spans)
        qs_roll = pltpu.roll(qs.astype(jnp.float32), HEAD, 1).astype(jnp.bfloat16)
        side = both_rows(side_ref, spans)
        seg_keep = (side[:, 0:1] == 0) == low
        krank = krank_ref[...]
        factor = SCALE * LOG2E
        window = rel_ref[pl.ds(3 - tile, WIN // SUB)].reshape(WIN, PAIR)
        grid = mm(
            jnp.concatenate([jnp.where(low, qp, zero), jnp.where(low, zero, qp)], axis=0), window, nt
        )
        parts = []
        for head in range(2):
            mine = low if head == 0 else ~low
            twice = jnp.where(mine, qs, qs_roll)
            qcat = jnp.concatenate(
                [jnp.where(mine, qc, zero), jnp.where(seg_keep, twice, zero)], axis=1
            )
            score = mm(qcat, kcat[head], nt)
            for row in range(0, ROWS, CHUNK):
                at = row % SUB
                shifted = pltpu.roll(
                    grid[head * ROWS + row : head * ROWS + row + CHUNK],
                    WIN - SUB + 1 + at, 1, stride=1, stride_axis=0,
                )[:, :KEYS]
                logit = score[row : row + CHUNK] + shifted
                current = jnp.where(krank <= side[row : row + CHUNK, 1:2], logit[:, MEM:], FAR)
                logit = jnp.concatenate([logit[:, :MEM], current], axis=1)
                top = jnp.max(logit, axis=-1, keepdims=True)
                soft = jnp.exp2((logit - top) * factor).astype(jnp.bfloat16)
                prob_ref[head, pl.ds(spans[row // SUB] + at, CHUNK), :] = soft
                parts.append(soft)
        summed = mm(jnp.concatenate(parts, axis=0), vcat[...], nn)
        scale = 1.0 / summed[:, PAIR:]
        mixed = summed[:, :PAIR] * scale
        mixed = jnp.where(low, mixed[:ROWS], mixed[ROWS:]).astype(jnp.bfloat16)
        scale = jnp.where(low, scale[:ROWS], scale[ROWS:])
        for index, start in enumerate(spans):
            mix_ref[pl.ds(start, SUB), :] = mixed[index * SUB : (index + 1) * SUB]
            inv_ref[pl.ds(start, SUB), :] = scale[index * SUB : (index + 1) * SUB]
        return carry

    lax.fori_loop(0, SEG // SUB, block, 0)


def whole(rows, lanes):
    return pl.BlockSpec((rows, lanes), lambda p: (0, 0))


def attention_forward(qc, qp, qs, keys, values, rel, emb, side, key_side, krank):
    pair = lambda rows: pl.BlockSpec((rows, PAIR), lambda p: (0, p))
    return pl.pallas_call(
        forward_kernel,
        grid=(PAIRS,),
        in_specs=[
            pair(2 * SEG), pair(2 * SEG), pair(2 * SEG), pair(KEYS), pair(KEYS),
            pl.BlockSpec((REL // SUB, SUB, PAIR), lambda p: (0, 0, p)),
            pair(2), whole(*side.shape), whole(*key_side.shape), whole(1, SEG),
        ],
        out_specs=[
            pair(2 * SEG), pair(2 * SEG),
            pl.BlockSpec((None, 2, 2 * SEG, KEYS), lambda p: (p, 0, 0, 0)),
        ],
        out_shape=[
            jax.ShapeDtypeStruct((2 * SEG, D), jnp.bfloat16),
            jax.ShapeDtypeStruct((2 * SEG, D), jnp.float32),
            jax.ShapeDtypeStruct((PAIRS, 2, 2 * SEG, KEYS), jnp.bfloat16),
        ],
        scratch_shapes=[
            pltpu.VMEM((2, KEYS, 2 * PAIR), jnp.bfloat16),
            pltpu.VMEM((KEYS, 2 * PAIR), jnp.bfloat16),
        ],
        compiler_params=pltpu.CompilerParams(
            dimension_semantics=("arbitrary",), vmem_limit_bytes=VMEM_BYTES
        ),
        cost_estimate=pl.CostEstimate(
            flops=30000000000, transcendentals=11000000, bytes_accessed=30000000
        ),
        name="attention_forward",
    )(qc, qp, qs, keys, values, rel.reshape(REL // SUB, SUB, D), emb, side, key_side, krank)


def backward_kernel(
    prob_ref, dmix_ref, mix_ref, inv_ref, qc_ref, qp_ref, qs_ref, k_ref, v_ref, rel_ref, emb_ref,
    side_ref, key_side_ref, inputs_ref, frame_ref, positions_ref, *rest,
):
    dproj_ref, dk_ref, dv_ref, small_ref, bucket_ref, kcat, dk_acc, dv_acc, drel_acc = rest[-9:]
    kcat[:, :PAIR] = k_ref[...]
    kcat[:, PAIR:] = jnp.where((key_side_ref[:, 0:1] == 0) == lane_low(KEYS), 1.0, 0.0).astype(
        jnp.bfloat16
    )
    dk_acc[...] = jnp.zeros_like(dk_acc)
    dv_acc[...] = jnp.zeros_like(dv_acc)
    drel_acc[...] = jnp.zeros_like(drel_acc)
    small_ref[...] = jnp.zeros_like(small_ref)

    def block(tile, carry):
        spans = tile_spans(tile)
        low = lane_low(ROWS)
        zero = jnp.zeros((ROWS, PAIR), jnp.bfloat16)
        row_index = lax.broadcasted_iota(jnp.int32, (ROWS, ROWS), 0)
        column_index = lax.broadcasted_iota(jnp.int32, (ROWS, ROWS), 1)
        flip = jnp.where(
            (row_index // SUB == column_index // SUB)
            & (row_index % SUB + column_index % SUB == SUB - 1),
            1.0, 0.0,
        ).astype(jnp.bfloat16)
        dmix = (
            both_rows(dmix_ref, spans).astype(jnp.float32) * (both_rows(inv_ref, spans) * SCALE)
        ).astype(jnp.bfloat16)
        weighted = dmix.astype(jnp.float32) * both_rows(mix_ref, spans).astype(jnp.float32)
        qc = both_rows(qc_ref, spans)
        qp = both_rows(qp_ref, spans)
        qs = both_rows(qs_ref, spans).astype(jnp.float32)
        qp_turned = mm(flip, qp, nn).astype(jnp.bfloat16)
        first = both_rows(side_ref, spans)[:, 0:1] == 0
        emb = emb_ref[...].astype(jnp.float32)
        dm = jnp.concatenate([jnp.where(low, dmix, zero), jnp.where(low, zero, dmix)], axis=0)
        qc_both = jnp.concatenate([jnp.where(low, qc, zero), jnp.where(low, zero, qc)], axis=0)
        qp_both = jnp.concatenate(
            [jnp.where(low, qp_turned, zero), jnp.where(low, zero, qp_turned)], axis=0
        )
        row_sum = jnp.concatenate(
            [
                jnp.sum(jnp.where(low, weighted, 0.0), axis=-1, keepdims=True),
                jnp.sum(jnp.where(low, 0.0, weighted), axis=-1, keepdims=True),
            ],
            axis=0,
        )
        prob = jnp.concatenate([both_rows(prob_ref.at[head], spans) for head in range(2)], axis=0)
        dprob = mm(dm, v_ref[...], nt)
        total = jnp.concatenate(
            [
                (
                    prob[at : at + CHUNK].astype(jnp.float32)
                    * (dprob[at : at + CHUNK] - row_sum[at : at + CHUNK])
                ).astype(jnp.bfloat16)
                for at in range(0, 2 * ROWS, CHUNK)
            ],
            axis=0,
        )
        back = mm(total, kcat[...], nn)
        turned = [mm(flip, total[head * ROWS : (head + 1) * ROWS], nn) for head in range(2)]
        grid = jnp.concatenate(
            [
                pltpu.roll(
                    jnp.concatenate(
                        [turned[head][row : row + CHUNK], jnp.zeros((CHUNK, SUB), jnp.float32)],
                        axis=1,
                    ),
                    row % SUB, 1, stride=1, stride_axis=0,
                ).astype(jnp.bfloat16)
                for head in range(2)
                for row in range(0, ROWS, CHUNK)
            ],
            axis=0,
        )
        window = rel_ref[pl.ds(3 - tile, WIN // SUB)].reshape(WIN, PAIR)
        dqp = mm(grid, window, nn)
        dqp = jnp.where(low, dqp[:ROWS], dqp[ROWS:]).astype(jnp.bfloat16)
        dqp_wide = mm(flip, dqp, nn)
        dv_acc[...] += mm(dm, prob, tn)
        dk_acc[...] += mm(qc_both, total, tn)
        drel = mm(qp_both, grid, tn)
        for part in range(WIN // SUB):
            drel_acc[3 - tile + part] += drel[:, part * SUB : (part + 1) * SUB]
        dqc_wide = (
            jnp.where(low, back[:ROWS, :PAIR], back[ROWS:, :PAIR])
            .astype(jnp.bfloat16)
            .astype(jnp.float32)
        )
        sums = [back[head * ROWS : (head + 1) * ROWS, PAIR:] for head in range(2)]
        rolled = [pltpu.roll(part, HEAD, 1) for part in sums]
        key_zero = jnp.where(low, sums[0], rolled[1])
        key_one = jnp.where(low, rolled[0], sums[1])
        near = jnp.where(first, key_zero, key_one)
        other = jnp.where(first, key_one, key_zero)
        dqs_wide = (near * emb[0:1] + other * emb[1:2]).astype(jnp.bfloat16).astype(jnp.float32)
        dproj = (dqc_wide + dqp_wide + dqs_wide).astype(jnp.bfloat16)
        for index, start in enumerate(spans):
            dproj_ref[pl.ds(start, SUB), :] = dproj[index * SUB : (index + 1) * SUB]
        rows = [dqc_wide, dqp_wide, dqs_wide, near * qs, other * qs]
        for row, value in enumerate(rows):
            small_ref[row : row + 1, :] += jnp.sum(value, axis=0, keepdims=True)
        return carry

    lax.fori_loop(0, SEG // SUB, block, 0, unroll=True)
    dk_low = dk_acc[...].astype(jnp.bfloat16)
    dv_low = (dv_acc[...] * (1.0 / SCALE)).astype(jnp.bfloat16)
    dk_ref[...] = dk_low.T
    dv_ref[...] = dv_low.T
    drel_low = jnp.concatenate(
        [drel_acc[part] for part in range(REL // SUB)], axis=1
    ).astype(jnp.bfloat16)
    grads = (
        mm(dproj_ref[...], inputs_ref[...], tn), mm(dk_low, frame_ref[...], nn),
        mm(dv_low, frame_ref[...], nn), mm(drel_low, positions_ref[...], nn),
    )
    for index, grad in enumerate(grads):
        bucket_ref[index * PAIR : (index + 1) * PAIR, :] = grad.astype(jnp.bfloat16)


def attention_backward(
    first, count, bucket_block, chain, prob, dmix, mix, inv, qc, qp, qs, keys, values, rel, emb, side,
    key_side, inputs, frame, positions,
):
    pair = lambda rows: pl.BlockSpec((rows, PAIR), lambda p: (0, first + p))
    rel_block = pl.BlockSpec((REL // SUB, SUB, PAIR), lambda p: (0, 0, first + p))
    bucket_rows = chain[4] if isinstance(chain[4], int) else chain[4].shape[0]
    passed = [item for item in chain if not isinstance(item, int) and item is not None]
    places = [at for at, item in enumerate(chain) if not isinstance(item, int) and item is not None]
    return pl.pallas_call(
        backward_kernel,
        grid=(count,),
        in_specs=[
            pl.BlockSpec((None, 2, 2 * SEG, KEYS), lambda p: (first + p, 0, 0, 0)),
            pair(2 * SEG), pair(2 * SEG), pair(2 * SEG), pair(2 * SEG), pair(2 * SEG), pair(2 * SEG),
            pair(KEYS), pair(KEYS), rel_block, pair(2), whole(*side.shape), whole(*key_side.shape),
            whole(2 * SEG, D), whole(KEYS, D), whole(REL, D),
        ]
        + [pl.BlockSpec(memory_space=pl.ANY)] * len(passed),
        out_specs=[
            pair(2 * SEG), pair(KEYS), pair(KEYS), pair(8),
            pl.BlockSpec((4 * PAIR, D), lambda p: (bucket_block + p, 0)),
        ],
        out_shape=[
            jax.ShapeDtypeStruct((2 * SEG, D), jnp.bfloat16),
            jax.ShapeDtypeStruct((KEYS, D), jnp.bfloat16),
            jax.ShapeDtypeStruct((KEYS, D), jnp.bfloat16),
            jax.ShapeDtypeStruct((8, D), jnp.float32),
            jax.ShapeDtypeStruct((bucket_rows, D), jnp.bfloat16),
        ],
        scratch_shapes=[
            pltpu.VMEM((KEYS, 2 * PAIR), jnp.bfloat16),
            pltpu.VMEM((PAIR, KEYS), jnp.float32),
            pltpu.VMEM((PAIR, KEYS), jnp.float32),
            pltpu.VMEM((REL // SUB, PAIR, SUB), jnp.float32),
        ],
        input_output_aliases={16 + index: at for index, at in enumerate(places)},
        compiler_params=pltpu.CompilerParams(
            dimension_semantics=("arbitrary",), vmem_limit_bytes=VMEM_BYTES
        ),
        cost_estimate=pl.CostEstimate(
            flops=count * 8000000000, transcendentals=0, bytes_accessed=count * 8000000
        ),
        name="attention_backward",
    )(
        prob, dmix, mix, inv, qc, qp, qs, keys, values, rel.reshape(REL // SUB, SUB, D), emb, side,
        key_side, inputs, frame, positions, *passed,
    )


norm_epsilon = 1e-06
TOKENS = 256
FF_CHUNK = 768
half_erfc = (0.5 * 0.254829592, 0.5 * -0.284496736, 0.5 * 1.421413741, 0.5 * -1.453152027, 0.5 * 1.061405429)


def gelu_pair(x):
    gauss = jnp.exp2(x * x * (-0.5 * LOG2E))
    t = 1.0 / (1.0 + (0.3275911 * 0.7071067811865476) * jnp.abs(x))
    a1, a2, a3, a4, a5 = half_erfc
    tail = t * (a1 + t * (a2 + t * (a3 + t * (a4 + t * a5)))) * gauss
    cdf = jnp.where(x >= 0.0, 1.0 - tail, tail)
    return x * cdf, cdf + x * gauss * 0.3989422804014327


def normalise(tensor):
    centred = tensor - jnp.mean(tensor, axis=-1, keepdims=True)
    inverse = lax.rsqrt(jnp.mean(centred * centred, axis=-1, keepdims=True) + norm_epsilon)
    return centred * inverse, inverse


def norm_back(grad, hat, inverse):
    return inverse * (
        grad
        - jnp.mean(grad, axis=-1, keepdims=True)
        - hat * jnp.mean(grad * hat, axis=-1, keepdims=True)
    )


def token_kernel(
    x_ref, mix_ref, cot_ref, wo_ref, wi_ref, wf_ref, bias_inner_ref, rows_ref,
    final_ref, active_ref, outer_ref, inner_ref, attended_ref, dmix_ref, low_ref, residual_ref,
    sums_ref, inner_sum_ref,
    slope,
):
    @pl.when(pl.program_id(0) == 0)
    def _():
        sums_ref[...] = jnp.zeros_like(sums_ref)
        inner_sum_ref[...] = jnp.zeros_like(inner_sum_ref)

    gain_one, shift_one = rows_ref[0:1, :], rows_ref[1:2, :]
    gain_two, shift_two = rows_ref[2:3, :], rows_ref[3:4, :]
    bias_outer = rows_ref[4:5, :]
    hat_one, inverse_one = normalise(
        x_ref[...].astype(jnp.float32) + mm(mix_ref[...], wo_ref[...], nn)
    )
    normed = hat_one * gain_one + shift_one
    normed_low = normed.astype(jnp.bfloat16)
    low_ref[...] = normed_low
    chunks = [slice(at, at + FF_CHUNK) for at in range(0, wi_ref.shape[1], FF_CHUNK)]
    pre = mm(normed_low, wi_ref[:, chunks[0]], nn)
    total = normed + bias_outer
    for index, chunk in enumerate(chunks):
        here = pre + bias_inner_ref[:, chunk]
        if index + 1 < len(chunks):
            pre = mm(normed_low, wi_ref[:, chunks[index + 1]], nn)
        value, derivative = gelu_pair(here)
        value = value.astype(jnp.bfloat16)
        active_ref[:, chunk] = value
        slope[:, chunk] = derivative
        total = total + mm(value, wf_ref[chunk, :], nn)
    hat_two, inverse_two = normalise(total)
    final_ref[...] = (hat_two * gain_two + shift_two).astype(jnp.bfloat16)
    cot = cot_ref[...].astype(jnp.float32)
    grad_total = norm_back(cot * gain_two, hat_two, inverse_two)
    grad_outer = grad_total.astype(jnp.bfloat16)
    outer_ref[...] = grad_outer
    sums_ref[2:3, :] += jnp.sum(cot * hat_two, axis=0, keepdims=True)
    sums_ref[3:4, :] += jnp.sum(cot, axis=0, keepdims=True)
    sums_ref[4:5, :] += jnp.sum(grad_outer.astype(jnp.float32), axis=0, keepdims=True)
    back = mm(grad_outer, wf_ref[chunks[0], :], nt)
    for index, chunk in enumerate(chunks):
        here = back
        if index + 1 < len(chunks):
            back = mm(grad_outer, wf_ref[chunks[index + 1], :], nt)
        grad_inner = (here * slope[:, chunk]).astype(jnp.bfloat16)
        inner_ref[:, chunk] = grad_inner
        inner_sum_ref[:, chunk] += jnp.sum(grad_inner.astype(jnp.float32), axis=0, keepdims=True)
        grad_total = grad_total + mm(grad_inner, wi_ref[:, chunk], nt)
    sums_ref[0:1, :] += jnp.sum(grad_total * hat_one, axis=0, keepdims=True)
    sums_ref[1:2, :] += jnp.sum(grad_total, axis=0, keepdims=True)
    residual = norm_back(grad_total * gain_one, hat_one, inverse_one)
    residual_ref[...] = residual
    attended = residual.astype(jnp.bfloat16)
    attended_ref[...] = attended
    dmix_ref[...] = mm(attended, wo_ref[...], nt).astype(jnp.bfloat16)


def token_layer(x, mix, cot, w_out, w_inner, w_outer, bias_inner, rows):
    count = x.shape[0]
    hidden = w_inner.shape[1]
    tile = lambda lanes: pl.BlockSpec((TOKENS, lanes), lambda i: (i, 0))
    once = lambda a, b: pl.BlockSpec((a, b), lambda i: (0, 0), pipeline_mode=pl.Buffered(1))
    sums = lambda a, b: pl.BlockSpec((a, b), lambda i: (0, 0))
    low = lambda lanes: jax.ShapeDtypeStruct((count, lanes), jnp.bfloat16)
    return pl.pallas_call(
        token_kernel,
        grid=(count // TOKENS,),
        in_specs=[
            tile(D), tile(D), tile(D), once(D, D), once(D, hidden), once(hidden, D),
            once(1, hidden), once(8, D),
        ],
        out_specs=[
            tile(D), tile(hidden), tile(D), tile(hidden), tile(D), tile(D), tile(D), tile(D),
            sums(8, D), sums(1, hidden),
        ],
        out_shape=[
            low(D), low(hidden), low(D), low(hidden), low(D), low(D), low(D),
            jax.ShapeDtypeStruct((count, D), jnp.float32),
            jax.ShapeDtypeStruct((8, D), jnp.float32),
            jax.ShapeDtypeStruct((1, hidden), jnp.float32),
        ],
        scratch_shapes=[pltpu.VMEM((TOKENS, hidden), jnp.float32)],
        compiler_params=pltpu.CompilerParams(
            dimension_semantics=("arbitrary",), vmem_limit_bytes=VMEM_BYTES
        ),
        cost_estimate=pl.CostEstimate(
            flops=22000000000, transcendentals=6000000, bytes_accessed=40000000
        ),
        name="token_layer",
    )(x, mix, cot, w_out, w_inner, w_outer, bias_inner, rows)


def chip_bits():
    bits = []
    bit = 2
    while bit < lax.axis_size("batch"):
        bits.append(bit)
        bit *= 2
    return bits


def digit(bit):
    return lax.axis_index("batch") // bit % 2


def across(tensor, bits):
    count = lax.axis_size("batch")
    return lax.ppermute(tensor, "batch", [(i, i ^ bits[i & 1]) for i in range(count)])


def own_digit(bits):
    return jnp.where(digit(1) == 1, digit(bits[1]), digit(bits[0]))


def along(tensor, shift):
    ring = lax.axis_size("mem")
    return lax.ppermute(tensor, "mem", [(i, (i + shift) % ring) for i in range(ring)])


def rows_of(tensor, start, count):
    return lax.dynamic_slice(tensor, (start, 0), (count, tensor.shape[1]))


class Sum:
    def __init__(self, tensor):
        bits = chip_bits()
        self.bits = [(1, 1)] + list(zip(bits, bits[::-1]))
        self.state = tensor
        self.at = 0
        self.stages = 2 * len(self.bits) + 2

    def step(self):
        count, tensor = len(self.bits), self.state
        ring, me = lax.axis_size("mem"), lax.axis_index("mem")
        if self.at < count:
            bit = self.bits[self.at]
            half = tensor.shape[0] // 2
            mine = own_digit(bit)
            got = across(rows_of(tensor, (1 - mine) * half, half), bit)
            kept = rows_of(tensor, mine * half, half)
            self.state = (kept.astype(jnp.float32) + got.astype(jnp.float32)).astype(jnp.bfloat16)
        elif self.at == count:
            block = tensor.shape[0] // ring
            total = rows_of(tensor, me * block, block).astype(jnp.float32)
            for shift in range(1, ring):
                sent = rows_of(tensor, (me + shift) % ring * block, block)
                total = total + along(sent, shift).astype(jnp.float32)
            self.state = total.astype(jnp.bfloat16)
        elif self.at == count + 1:
            parts = [tensor] + [along(tensor, shift) for shift in range(1, ring)]
            self.state = jnp.concatenate(parts, axis=0)
        else:
            bit = self.bits[2 * count + 1 - self.at]
            self.state = jnp.concatenate([tensor, across(tensor, bit)], axis=0)
        self.at += 1

    def places(self):
        ring = lax.axis_size("mem")
        weight = ring * lax.axis_size("batch") // 2
        index = jnp.arange(2 * weight, dtype=jnp.int32)
        place = (lax.axis_index("mem") - index % ring) % ring
        core = index // weight % 2
        for even, odd in self.bits:
            own = jnp.where(core == 1, digit(odd), digit(even))
            place = place + (index // weight % 2 + own) % 2 * weight
            weight //= 2
        return place


def together(active, tree):
    states, tree = lax.optimization_barrier(([item.state for item in active], tree))
    for item, state in zip(active, states):
        item.state = state
    return tree


def placed(item):
    tensor, place = item.state, item.places()
    blocks = place.shape[0]
    if tensor.shape[0] // blocks % 8:
        tensor = tensor.reshape(blocks, -1, tensor.shape[1])[place].reshape(tensor.shape)
        place = jnp.arange(8, dtype=jnp.int32)
    return tensor, place


def block_of(place_ref, in_ref, index):
    rows = in_ref.shape[0] // place_ref.shape[0]
    start = pl.multiple_of(place_ref[index] * rows, 8)
    return in_ref[pl.ds(start, rows), :].astype(jnp.float32)


def settle_pairs_kernel(place_ref, in_ref, *rest):
    outs, full = rest[-6:-1], rest[-1]
    rows = in_ref.shape[0] // place_ref.shape[0]

    @pl.when(pl.program_id(0) == 0)
    def _():
        for item in range(place_ref.shape[0]):
            full[item * rows : (item + 1) * rows, :] = block_of(place_ref, in_ref, item)
        grads = PAIRS // 2 * 4 * PAIR
        outs[4][...] = full[grads : grads + outs[4].shape[0], :]

    for index in range(4):
        start = pl.multiple_of((pl.program_id(0) * 4 + index) * PAIR, PAIR)
        outs[index][...] = full[pl.ds(start, PAIR), :].T


def settle_pairs(item, first, count, earlier, after):
    tensor, place = placed(item)
    rows, lanes = tensor.shape
    square = jax.ShapeDtypeStruct((D, D), jnp.float32)
    return pl.pallas_call(
        settle_pairs_kernel,
        grid_spec=pltpu.PrefetchScalarGridSpec(
            num_scalar_prefetch=1,
            grid=(count,),
            in_specs=[pl.BlockSpec((rows, lanes), lambda i, p: (0, 0))]
            + [pl.BlockSpec(memory_space=pl.ANY)] * len(earlier),
            out_specs=[pl.BlockSpec((lanes, PAIR), lambda i, p: (0, first + i))] * 4
            + [pl.BlockSpec((after, lanes), lambda i, p: (0, 0))],
            scratch_shapes=[pltpu.VMEM((rows, lanes), jnp.float32)],
        ),
        out_shape=[square] * 4 + [jax.ShapeDtypeStruct((after, lanes), jnp.float32)],
        input_output_aliases={2 + index: index for index in range(len(earlier))},
        compiler_params=pltpu.CompilerParams(vmem_limit_bytes=48 * 1024 * 1024),
        name="settle_pairs",
    )(place, tensor, *earlier)


def sinusoid():
    fine_count = 32
    frequency = 1.0 / 10000.0 ** (
        jnp.arange(0, D, 2, dtype=jnp.int32).astype(jnp.float32) / D
    )
    coarse = (KEYS - 1 - fine_count * jnp.arange(REL // fine_count, dtype=jnp.int32)).astype(
        jnp.float32
    )[:, None] * frequency[None]
    fine = jnp.arange(fine_count, dtype=jnp.int32).astype(jnp.float32)[:, None] * frequency[None]
    sin_coarse, cos_coarse = jnp.sin(coarse)[:, None], jnp.cos(coarse)[:, None]
    sin_fine, cos_fine = jnp.sin(fine)[None], jnp.cos(fine)[None]
    sine = sin_coarse * cos_fine - cos_coarse * sin_fine
    cosine = cos_coarse * cos_fine + sin_coarse * sin_fine
    return jnp.concatenate([sine, cosine], axis=-1).reshape(REL, D).astype(jnp.bfloat16)


EXTRA = 256
VECTORS = 24


WIDE = 512


def wide_grads_kernel(outer_ref, active_ref, low_ref, inner_ref, out_ref, left):
    part = pl.program_id(0)

    @pl.when(pl.program_id(1) == 0)
    def _():
        @pl.when(part == 0)
        def _():
            left[...] = outer_ref[...].T

        @pl.when(part == 1)
        def _():
            left[...] = low_ref[...].T

    @pl.when(part == 0)
    def _():
        out_ref[...] = mm(left[...], active_ref[...], nn).astype(jnp.bfloat16)

    @pl.when(part == 1)
    def _():
        out_ref[...] = mm(left[...], inner_ref[...], nn).astype(jnp.bfloat16)


def wide_grads(grad_outer, active, normed_low, grad_inner):
    tokens, hidden = active.shape
    steps = hidden // WIDE
    return pl.pallas_call(
        wide_grads_kernel,
        grid=(2, steps),
        in_specs=[
            pl.BlockSpec((tokens, D), lambda p, i: (0, 0)),
            pl.BlockSpec((tokens, WIDE), lambda p, i: (0, jnp.where(p == 0, i, steps - 1))),
            pl.BlockSpec((tokens, D), lambda p, i: (0, 0)),
            pl.BlockSpec((tokens, WIDE), lambda p, i: (0, jnp.where(p == 0, 0, i))),
        ],
        out_specs=pl.BlockSpec((D, WIDE), lambda p, i: (p, i)),
        out_shape=jax.ShapeDtypeStruct((2 * D, hidden), jnp.bfloat16),
        scratch_shapes=[pltpu.VMEM((D, tokens), jnp.bfloat16)],
        compiler_params=pltpu.CompilerParams(
            dimension_semantics=("arbitrary",) * 2, vmem_limit_bytes=VMEM_BYTES
        ),
        cost_estimate=pl.CostEstimate(
            flops=9700000000, transcendentals=0, bytes_accessed=25000000
        ),
        name="wide_grads",
    )(grad_outer, active, normed_low, grad_inner)


def widen_kernel(outer_ref, inner_ref, outer_out, inner_out):
    outer_out[...] = outer_ref[...].astype(jnp.float32).T
    inner_out[...] = inner_ref[...].astype(jnp.float32)


def widen(summed):
    hidden = summed.shape[1]
    return pl.pallas_call(
        widen_kernel,
        grid=(hidden // WIDE,),
        in_specs=[
            pl.BlockSpec((D, WIDE), lambda i: (0, i)),
            pl.BlockSpec((D, WIDE), lambda i: (1, i)),
        ],
        out_specs=[
            pl.BlockSpec((WIDE, D), lambda i: (i, 0)),
            pl.BlockSpec((D, WIDE), lambda i: (0, i)),
        ],
        out_shape=[
            jax.ShapeDtypeStruct((hidden, D), jnp.float32),
            jax.ShapeDtypeStruct((D, hidden), jnp.float32),
        ],
        compiler_params=pltpu.CompilerParams(vmem_limit_bytes=VMEM_BYTES),
        name="widen",
    )(summed, summed)


def shards(
    content_in, query_in, memory, sequence_lengths, order_rank, segment_ids,
    w_query, w_key, w_value, w_out, w_rel,
    bias_content, bias_position, bias_segment, segment_embed,
    gain_one, shift_one, w_inner, bias_inner, w_outer, bias_outer, gain_two, shift_two,
    content_cotangent, query_cotangent,
):
    wide = lambda tensor: tensor.astype(jnp.float32)
    low = lambda tensor: tensor.astype(jnp.bfloat16)
    both = ("batch", "mem")
    past = lax.all_to_all(memory, "mem", split_axis=0, concat_axis=1, tiled=True)[0]
    content = content_in[0]
    inputs = jnp.concatenate([content, query_in[0]], axis=0)
    cotangent = jnp.concatenate([content_cotangent[0], query_cotangent[0]], axis=0)
    segment = segment_ids[0]
    rank = order_rank[0]
    zeros = jnp.zeros((2 * SEG, 6), jnp.int32)
    side = jnp.concatenate(
        [
            jnp.concatenate([segment, segment])[:, None],
            jnp.concatenate([rank, rank - 1])[:, None],
            zeros,
        ],
        axis=1,
    )
    key_side = jnp.concatenate([jnp.zeros((MEM, 8), jnp.int32), side[:SEG]], axis=0)
    live = jnp.arange(SEG, dtype=jnp.int32) < sequence_lengths[0]
    key_rank = jnp.where(live, rank, 2 * SEG)[None, :]

    positions = sinusoid()
    relative = low(mm(positions, w_rel, nn))
    frame = jnp.concatenate([past, content], axis=0)
    keys = low(mm(frame, w_key, nn))
    values = low(mm(frame, w_value, nn))
    projected = mm(inputs, w_query, nn)
    query_content = low(projected + wide(bias_content))
    query_position = low(projected + wide(bias_position))
    query_segment = low(projected + wide(bias_segment))
    mixture, inverse, probs = attention_forward(
        query_content, query_position, query_segment, keys, values, relative, segment_embed,
        side, key_side, key_rank,
    )
    rows = jnp.stack(
        [wide(t) for t in (gain_one, shift_one, gain_two, shift_two, bias_outer)]
        + [jnp.zeros((D,), jnp.float32)] * 3
    )
    (
        final_out, active_low, grad_outer_low, grad_inner_low, grad_attended, grad_mixture,
        normed_low, grad_residual, token_sums, inner_bias_sum,
    ) = token_layer(
        inputs, mixture, cotangent, w_out, w_inner, w_outer, wide(bias_inner)[None], rows
    )
    low_mm = lambda left, right: low(mm(left, right, tn))
    wide_sum = wide_grads(grad_outer_low, active_low, normed_low, grad_inner_low)
    wide_sum, grad_mixture, grad_attended = lax.optimization_barrier(
        (wide_sum, grad_mixture, grad_attended)
    )
    wide_sum = lax.psum(wide_sum, both)
    def attention_part(operands):
        (
            probs, grad_mixture, mixture, inverse, query_content, query_position, query_segment,
            keys, values, relative, side, key_side, inputs, frame, positions, grad_attended,
            token_sums, inner_bias_sum, segment_embed, grad_residual, w_query, w_key, w_value,
        ) = operands
        common = (
            mixture, inverse, query_content, query_position, query_segment, keys, values, relative,
            segment_embed, side, key_side, inputs, frame, positions,
        )
        half = PAIRS // 2
        group_rows = half * 4 * PAIR
        chain = attention_backward(
            0, half, 0, [None] * 4 + [group_rows + D], probs, grad_mixture, *common
        )
        early = Sum(lax.dynamic_update_slice(chain[4], low_mm(mixture, grad_attended), (group_rows, 0)))
        early.step()
        chain, grad_mixture = together([early], (list(chain[:4]), grad_mixture))
        early.step()
        chain = attention_backward(
            half, half, 0, chain + [group_rows + EXTRA], probs, grad_mixture, *common
        )
        grad_projected, grad_keys, grad_values, small, bucket = together([early], list(chain))
        vectors = jnp.concatenate(
            [token_sums, inner_bias_sum.reshape(-1, D), jnp.zeros((4, D), jnp.float32), small], axis=0
        )
        vectors = jnp.pad(vectors, ((0, EXTRA - vectors.shape[0]), (0, 0)))
        late = Sum(lax.dynamic_update_slice(bucket, low(vectors), (group_rows, 0)))
        while late.at < late.stages:
            late.step()
            if early.at < early.stages:
                early.step()
                together([late, early], ())
        *sums, out_sum = settle_pairs(early, 0, half, (), D)
        *sums, vectors = settle_pairs(late, half, half, sums, VECTORS)
        grad_inputs = grad_residual + mm(grad_projected, w_query, nt)
        grad_content = (
            grad_inputs[:SEG] + mm(grad_keys[MEM:], w_key, nt) + mm(grad_values[MEM:], w_value, nt)
        )
        return low(grad_content), low(grad_inputs[SEG:]), sums, out_sum, vectors

    operands = (
        probs, grad_mixture, mixture, inverse, query_content, query_position, query_segment, keys,
        values, relative, side, key_side, inputs, frame, positions, grad_attended, token_sums,
        inner_bias_sum, segment_embed, grad_residual, w_query, w_key, w_value,
    )
    shapes = jax.eval_shape(attention_part, operands)
    grad_content, grad_query, sums, out_sum, vectors = lax.cond(
        sequence_lengths[0] > -1,
        attention_part,
        lambda operands: jax.tree.map(lambda item: jnp.zeros(item.shape, item.dtype), shapes),
        operands,
    )
    query_sum, key_sum, value_sum, rel_sum = sums
    outer_sum, inner_sum = widen(wide_sum)
    pieces = {
        "gain1": vectors[0], "shift1": vectors[1], "gain2": vectors[2], "shift2": vectors[3],
        "outer": vectors[4], "inner": vectors[8:12].reshape(-1), "content": vectors[16],
        "position": vectors[17], "segment": vectors[18], "embed": vectors[19:21],
    }
    return (
        low(final_out[None, :SEG]), low(final_out[None, SEG:]),
        grad_content[None], grad_query[None],
        query_sum, key_sum, value_sum, out_sum, rel_sum,
        pieces["content"], pieces["position"], pieces["segment"], pieces["embed"].reshape(2, D),
        pieces["gain1"], pieces["shift1"], inner_sum, pieces["inner"], outer_sum, pieces["outer"],
        pieces["gain2"], pieces["shift2"],
    )


def solution(mesh):
    both = ("batch", "mem")
    rows = P(both, None, None)
    return jax.shard_map(
        shards,
        mesh=mesh,
        in_specs=(rows, rows, P("batch", "mem", None), P(both), P(both, None), P(both, None))
        + (P(),) * 17
        + (rows, rows),
        out_specs=(rows,) * 4 + (P(),) * 17,
        check_vma=False,
    )
```

```python
import functools

import jax
import jax.numpy as jnp
from jax import lax
from jax.experimental import pallas as pl
from jax.experimental.pallas import tpu as pltpu
from jax.sharding import PartitionSpec as P

D = 768
HEADS = 12
HEAD = 64
SEG = 512
MEM = 384
KEYS = MEM + SEG
REL = MEM + 2 * SEG
PAIR = 2 * HEAD
PAIRS = HEADS // 2
ROWS = 256
SUB = 128
CHUNK = 32
WIN = KEYS + SUB
FAR = -1e30
LOG2E = 1.4426950408889634
SCALE = HEAD**-0.5
VMEM_BYTES = 60 * 1024 * 1024
nt = (((1,), (1,)), ((), ()))
nn = (((1,), (0,)), ((), ()))
tn = (((0,), (0,)), ((), ()))


def mm(left, right, dims):
    return lax.dot_general(left, right, dims, preferred_element_type=jnp.float32)


def lane_low(rows):
    return lax.broadcasted_iota(jnp.int32, (rows, PAIR), 1) < HEAD


def tile_spans(tile):
    start = pl.multiple_of(tile * SUB, SUB)
    return [start, start + SEG]


def both_rows(ref, spans):
    return jnp.concatenate([ref[pl.ds(start, SUB), :] for start in spans], axis=0)


def spread(row_ref, out_ref):
    for at in range(0, SEG, SUB):
        block = jnp.broadcast_to(row_ref[:, at : at + SUB], (SUB, SUB))
        out_ref[at : at + SUB, :] = block.T


def twice_rows(ref, tile):
    rows = ref[pl.ds(pl.multiple_of(tile * SUB, SUB), SUB), :]
    return jnp.concatenate([rows, rows], axis=0)


def key_segment_zero(seg_col):
    return jnp.concatenate([jnp.ones((MEM, PAIR), jnp.bool_), seg_col[...] == 0], axis=0)


def forward_kernel(
    length_ref, qc_ref, qp_ref, qs_ref, k_ref, v_ref, rel_ref, emb_ref, seg_ref, rank_ref,
    mix_ref, inv_ref, prob_ref, kcat, vcat, seg_col, rank_col,
):
    @pl.when(pl.program_id(0) == 0)
    def _():
        spread(seg_ref, seg_col)
        spread(rank_ref, rank_col)

    same = key_segment_zero(seg_col)
    live = lax.broadcasted_iota(jnp.int32, (1, SEG), 1) < length_ref[0]
    krank = jnp.where(live, rank_ref[...], 2 * SEG)
    zero_row = emb_ref[0:1, :].astype(jnp.float32)
    one_row = emb_ref[1:2, :].astype(jnp.float32)
    zero_roll = pltpu.roll(zero_row, HEAD, 1)
    one_roll = pltpu.roll(one_row, HEAD, 1)
    low_row = lane_low(1)
    for head in range(2):
        if head == 0:
            near = jnp.where(low_row, zero_row, one_roll)
            away = jnp.where(low_row, one_row, zero_roll)
        else:
            near = jnp.where(low_row, zero_roll, one_row)
            away = jnp.where(low_row, one_roll, zero_row)
        kcat[head, :, :PAIR] = k_ref[...]
        kcat[head, :, PAIR:] = jnp.where(same, near, away).astype(jnp.bfloat16)
    vcat[:, :PAIR] = v_ref[...]
    vcat[:, PAIR:] = jnp.ones((KEYS, PAIR), jnp.bfloat16)

    def block(tile, carry):
        spans = tile_spans(tile)
        low = lane_low(ROWS)
        zero = jnp.zeros((ROWS, PAIR), jnp.bfloat16)
        qc = both_rows(qc_ref, spans)
        qp = both_rows(qp_ref, spans)
        qs = both_rows(qs_ref, spans)
        qs_roll = pltpu.roll(qs.astype(jnp.float32), HEAD, 1).astype(jnp.bfloat16)
        seg_keep = (twice_rows(seg_col, tile) == 0) == low
        rank = twice_rows(rank_col, tile) - jnp.where(
            lax.broadcasted_iota(jnp.int32, (ROWS, PAIR), 0) < SUB, 0, 1
        )
        rank = jnp.concatenate([rank] * (SEG // PAIR), axis=1)
        factor = SCALE * LOG2E
        window = rel_ref[pl.ds(3 - tile, WIN // SUB)].reshape(WIN, PAIR)
        grid = mm(
            jnp.concatenate([jnp.where(low, qp, zero), jnp.where(low, zero, qp)], axis=0), window, nt
        )
        parts = []
        for head in range(2):
            mine = low if head == 0 else ~low
            twice = jnp.where(mine, qs, qs_roll)
            qcat = jnp.concatenate(
                [jnp.where(mine, qc, zero), jnp.where(seg_keep, twice, zero)], axis=1
            )
            score = mm(qcat, kcat[head], nt)
            for row in range(0, ROWS, CHUNK):
                at = row % SUB
                shifted = pltpu.roll(
                    grid[head * ROWS + row : head * ROWS + row + CHUNK],
                    WIN - SUB + 1 + at, 1, stride=1, stride_axis=0,
                )[:, :KEYS]
                logit = score[row : row + CHUNK] + shifted
                current = jnp.where(krank <= rank[row : row + CHUNK], logit[:, MEM:], FAR)
                logit = jnp.concatenate([logit[:, :MEM], current], axis=1)
                top = jnp.max(logit, axis=-1, keepdims=True)
                soft = jnp.exp2((logit - top) * factor).astype(jnp.bfloat16)
                prob_ref[head, pl.ds(spans[row // SUB] + at, CHUNK), :] = soft
                parts.append(soft)
        summed = mm(jnp.concatenate(parts, axis=0), vcat[...], nn)
        scale = 1.0 / summed[:, PAIR:]
        mixed = summed[:, :PAIR] * scale
        mixed = jnp.where(low, mixed[:ROWS], mixed[ROWS:]).astype(jnp.bfloat16)
        scale = jnp.where(low, scale[:ROWS], scale[ROWS:])
        for index, start in enumerate(spans):
            mix_ref[pl.ds(start, SUB), :] = mixed[index * SUB : (index + 1) * SUB]
            inv_ref[pl.ds(start, SUB), :] = scale[index * SUB : (index + 1) * SUB]
        return carry

    lax.fori_loop(0, SEG // SUB, block, 0)


def whole(rows, lanes):
    return pl.BlockSpec((rows, lanes), lambda p: (0, 0))


def attention_forward(length, qc, qp, qs, keys, values, rel, emb, seg, rank):
    pair = lambda rows: pl.BlockSpec((rows, PAIR), lambda p: (0, p))
    return pl.pallas_call(
        forward_kernel,
        grid=(PAIRS,),
        in_specs=[
            pl.BlockSpec(memory_space=pltpu.SMEM),
            pair(2 * SEG), pair(2 * SEG), pair(2 * SEG), pair(KEYS), pair(KEYS),
            pl.BlockSpec((REL // SUB, SUB, PAIR), lambda p: (0, 0, p)),
            pair(2), whole(1, SEG), whole(1, SEG),
        ],
        out_specs=[
            pair(2 * SEG), pair(2 * SEG),
            pl.BlockSpec((None, 2, 2 * SEG, KEYS), lambda p: (p, 0, 0, 0)),
        ],
        out_shape=[
            jax.ShapeDtypeStruct((2 * SEG, D), jnp.bfloat16),
            jax.ShapeDtypeStruct((2 * SEG, D), jnp.float32),
            jax.ShapeDtypeStruct((PAIRS, 2, 2 * SEG, KEYS), jnp.bfloat16),
        ],
        scratch_shapes=[
            pltpu.VMEM((2, KEYS, 2 * PAIR), jnp.bfloat16),
            pltpu.VMEM((KEYS, 2 * PAIR), jnp.bfloat16),
            pltpu.VMEM((SEG, PAIR), jnp.int32),
            pltpu.VMEM((SEG, PAIR), jnp.int32),
        ],
        compiler_params=pltpu.CompilerParams(
            dimension_semantics=("arbitrary",), vmem_limit_bytes=VMEM_BYTES
        ),
        cost_estimate=pl.CostEstimate(
            flops=30000000000, transcendentals=11000000, bytes_accessed=30000000
        ),
        name="attention_forward",
    )(length, qc, qp, qs, keys, values, rel.reshape(REL // SUB, SUB, D), emb, seg, rank)


def backward_kernel(
    prob_ref, dmix_ref, mix_ref, inv_ref, qc_ref, qp_ref, qs_ref, k_ref, v_ref, rel_ref, emb_ref,
    seg_ref, inputs_ref, frame_ref, positions_ref, *rest,
):
    dproj_ref, dk_ref, dv_ref, small_ref, bucket_ref, kcat, dk_acc, dv_acc, drel_acc, seg_col = rest[-10:]

    @pl.when(pl.program_id(0) == 0)
    def _():
        spread(seg_ref, seg_col)

    kcat[:, :PAIR] = k_ref[...]
    kcat[:, PAIR:] = jnp.where(key_segment_zero(seg_col) == lane_low(KEYS), 1.0, 0.0).astype(
        jnp.bfloat16
    )
    dk_acc[...] = jnp.zeros_like(dk_acc)
    dv_acc[...] = jnp.zeros_like(dv_acc)
    drel_acc[...] = jnp.zeros_like(drel_acc)
    small_ref[...] = jnp.zeros_like(small_ref)

    def block(tile, carry):
        spans = tile_spans(tile)
        low = lane_low(ROWS)
        zero = jnp.zeros((ROWS, PAIR), jnp.bfloat16)
        row_index = lax.broadcasted_iota(jnp.int32, (ROWS, ROWS), 0)
        column_index = lax.broadcasted_iota(jnp.int32, (ROWS, ROWS), 1)
        flip = jnp.where(
            (row_index // SUB == column_index // SUB)
            & (row_index % SUB + column_index % SUB == SUB - 1),
            1.0, 0.0,
        ).astype(jnp.bfloat16)
        dmix = (
            both_rows(dmix_ref, spans).astype(jnp.float32) * (both_rows(inv_ref, spans) * SCALE)
        ).astype(jnp.bfloat16)
        weighted = dmix.astype(jnp.float32) * both_rows(mix_ref, spans).astype(jnp.float32)
        qc = both_rows(qc_ref, spans)
        qp = both_rows(qp_ref, spans)
        qs = both_rows(qs_ref, spans).astype(jnp.float32)
        qp_turned = mm(flip, qp, nn).astype(jnp.bfloat16)
        first_rows = twice_rows(seg_col, tile) == 0
        emb = emb_ref[...].astype(jnp.float32)
        dm = jnp.concatenate([jnp.where(low, dmix, zero), jnp.where(low, zero, dmix)], axis=0)
        qc_both = jnp.concatenate([jnp.where(low, qc, zero), jnp.where(low, zero, qc)], axis=0)
        qp_both = jnp.concatenate(
            [jnp.where(low, qp_turned, zero), jnp.where(low, zero, qp_turned)], axis=0
        )
        row_sum = jnp.concatenate(
            [
                jnp.sum(jnp.where(low, weighted, 0.0), axis=-1, keepdims=True),
                jnp.sum(jnp.where(low, 0.0, weighted), axis=-1, keepdims=True),
            ],
            axis=0,
        )
        prob = jnp.concatenate([both_rows(prob_ref.at[head], spans) for head in range(2)], axis=0)
        dprob = mm(dm, v_ref[...], nt)
        total = jnp.concatenate(
            [
                (
                    prob[at : at + CHUNK].astype(jnp.float32)
                    * (dprob[at : at + CHUNK] - row_sum[at : at + CHUNK])
                ).astype(jnp.bfloat16)
                for at in range(0, 2 * ROWS, CHUNK)
            ],
            axis=0,
        )
        back = mm(total, kcat[...], nn)
        turned = [mm(flip, total[head * ROWS : (head + 1) * ROWS], nn) for head in range(2)]
        grid = jnp.concatenate(
            [
                pltpu.roll(
                    jnp.concatenate(
                        [turned[head][row : row + CHUNK], jnp.zeros((CHUNK, SUB), jnp.float32)],
                        axis=1,
                    ),
                    row % SUB, 1, stride=1, stride_axis=0,
                ).astype(jnp.bfloat16)
                for head in range(2)
                for row in range(0, ROWS, CHUNK)
            ],
            axis=0,
        )
        window = rel_ref[pl.ds(3 - tile, WIN // SUB)].reshape(WIN, PAIR)
        dqp = mm(grid, window, nn)
        dqp = jnp.where(low, dqp[:ROWS], dqp[ROWS:]).astype(jnp.bfloat16)
        dqp_wide = mm(flip, dqp, nn)
        dv_acc[...] += mm(dm, prob, tn)
        dk_acc[...] += mm(qc_both, total, tn)
        drel = mm(qp_both, grid, tn)
        for part in range(WIN // SUB):
            drel_acc[3 - tile + part] += drel[:, part * SUB : (part + 1) * SUB]
        dqc_wide = (
            jnp.where(low, back[:ROWS, :PAIR], back[ROWS:, :PAIR])
            .astype(jnp.bfloat16)
            .astype(jnp.float32)
        )
        sums = [back[head * ROWS : (head + 1) * ROWS, PAIR:] for head in range(2)]
        rolled = [pltpu.roll(part, HEAD, 1) for part in sums]
        key_zero = jnp.where(low, sums[0], rolled[1])
        key_one = jnp.where(low, rolled[0], sums[1])
        near = jnp.where(first_rows, key_zero, key_one)
        other = jnp.where(first_rows, key_one, key_zero)
        dqs_wide = (near * emb[0:1] + other * emb[1:2]).astype(jnp.bfloat16).astype(jnp.float32)
        dproj = (dqc_wide + dqp_wide + dqs_wide).astype(jnp.bfloat16)
        for index, start in enumerate(spans):
            dproj_ref[pl.ds(start, SUB), :] = dproj[index * SUB : (index + 1) * SUB]
        rows = [dqc_wide, dqp_wide, dqs_wide, near * qs, other * qs]
        for row, value in enumerate(rows):
            small_ref[row : row + 1, :] += jnp.sum(value, axis=0, keepdims=True)
        return carry

    lax.fori_loop(0, SEG // SUB, block, 0, unroll=True)
    dk_low = dk_acc[...].astype(jnp.bfloat16)
    dv_low = (dv_acc[...] * (1.0 / SCALE)).astype(jnp.bfloat16)
    dk_ref[...] = dk_low.T
    dv_ref[...] = dv_low.T
    drel_low = jnp.concatenate(
        [drel_acc[part] for part in range(REL // SUB)], axis=1
    ).astype(jnp.bfloat16)
    grads = (
        mm(dproj_ref[...], inputs_ref[...], tn), mm(dk_low, frame_ref[...], nn),
        mm(dv_low, frame_ref[...], nn), mm(drel_low, positions_ref[...], nn),
    )
    for index, grad in enumerate(grads):
        bucket_ref[index * PAIR : (index + 1) * PAIR, :] = grad.astype(jnp.bfloat16)


def attention_backward(
    first, count, bucket_block, chain, prob, dmix, mix, inv, qc, qp, qs, keys, values, rel, emb, seg,
    inputs, frame, positions,
):
    pair = lambda rows: pl.BlockSpec((rows, PAIR), lambda p: (0, first + p))
    rel_block = pl.BlockSpec((REL // SUB, SUB, PAIR), lambda p: (0, 0, first + p))
    bucket_rows = chain[4] if isinstance(chain[4], int) else chain[4].shape[0]
    passed = [item for item in chain if not isinstance(item, int) and item is not None]
    places = [at for at, item in enumerate(chain) if not isinstance(item, int) and item is not None]
    return pl.pallas_call(
        backward_kernel,
        grid=(count,),
        in_specs=[
            pl.BlockSpec((None, 2, 2 * SEG, KEYS), lambda p: (first + p, 0, 0, 0)),
            pair(2 * SEG), pair(2 * SEG), pair(2 * SEG), pair(2 * SEG), pair(2 * SEG), pair(2 * SEG),
            pair(KEYS), pair(KEYS), rel_block, pair(2), whole(1, SEG),
            whole(2 * SEG, D), whole(KEYS, D), whole(REL, D),
        ]
        + [pl.BlockSpec(memory_space=pl.ANY)] * len(passed),
        out_specs=[
            pair(2 * SEG), pair(KEYS), pair(KEYS), pair(8),
            pl.BlockSpec((4 * PAIR, D), lambda p: (bucket_block + p, 0)),
        ],
        out_shape=[
            jax.ShapeDtypeStruct((2 * SEG, D), jnp.bfloat16),
            jax.ShapeDtypeStruct((KEYS, D), jnp.bfloat16),
            jax.ShapeDtypeStruct((KEYS, D), jnp.bfloat16),
            jax.ShapeDtypeStruct((8, D), jnp.float32),
            jax.ShapeDtypeStruct((bucket_rows, D), jnp.bfloat16),
        ],
        scratch_shapes=[
            pltpu.VMEM((KEYS, 2 * PAIR), jnp.bfloat16),
            pltpu.VMEM((PAIR, KEYS), jnp.float32),
            pltpu.VMEM((PAIR, KEYS), jnp.float32),
            pltpu.VMEM((REL // SUB, PAIR, SUB), jnp.float32),
            pltpu.VMEM((SEG, PAIR), jnp.int32),
        ],
        input_output_aliases={15 + index: at for index, at in enumerate(places)},
        compiler_params=pltpu.CompilerParams(
            dimension_semantics=("arbitrary",), vmem_limit_bytes=VMEM_BYTES
        ),
        cost_estimate=pl.CostEstimate(
            flops=count * 8000000000, transcendentals=0, bytes_accessed=count * 8000000
        ),
        name="attention_backward",
    )(
        prob, dmix, mix, inv, qc, qp, qs, keys, values, rel.reshape(REL // SUB, SUB, D), emb, seg,
        inputs, frame, positions, *passed,
    )


norm_epsilon = 1e-06
TOKENS = 256
FF_CHUNK = 768
half_erfc = (0.5 * 0.254829592, 0.5 * -0.284496736, 0.5 * 1.421413741, 0.5 * -1.453152027, 0.5 * 1.061405429)


def gelu_pair(x):
    gauss = jnp.exp2(x * x * (-0.5 * LOG2E))
    t = 1.0 / (1.0 + (0.3275911 * 0.7071067811865476) * jnp.abs(x))
    a1, a2, a3, a4, a5 = half_erfc
    tail = t * (a1 + t * (a2 + t * (a3 + t * (a4 + t * a5)))) * gauss
    cdf = jnp.where(x >= 0.0, 1.0 - tail, tail)
    return x * cdf, cdf + x * gauss * 0.3989422804014327


def normalise(tensor):
    centred = tensor - jnp.mean(tensor, axis=-1, keepdims=True)
    inverse = lax.rsqrt(jnp.mean(centred * centred, axis=-1, keepdims=True) + norm_epsilon)
    return centred * inverse, inverse


def norm_back(grad, hat, inverse):
    return inverse * (
        grad
        - jnp.mean(grad, axis=-1, keepdims=True)
        - hat * jnp.mean(grad * hat, axis=-1, keepdims=True)
    )


def token_kernel(
    x_ref, mix_ref, cot_ref, wo_ref, wi_ref, wf_ref, bias_inner_ref, rows_ref,
    final_ref, active_ref, outer_ref, inner_ref, attended_ref, dmix_ref, low_ref, residual_ref,
    sums_ref, inner_sum_ref,
    slope,
):
    @pl.when(pl.program_id(0) == 0)
    def _():
        sums_ref[...] = jnp.zeros_like(sums_ref)
        inner_sum_ref[...] = jnp.zeros_like(inner_sum_ref)

    gain_one, shift_one = rows_ref[0:1, :], rows_ref[1:2, :]
    gain_two, shift_two = rows_ref[2:3, :], rows_ref[3:4, :]
    bias_outer = rows_ref[4:5, :]
    hat_one, inverse_one = normalise(
        x_ref[...].astype(jnp.float32) + mm(mix_ref[...], wo_ref[...], nn)
    )
    normed = hat_one * gain_one + shift_one
    normed_low = normed.astype(jnp.bfloat16)
    low_ref[...] = normed_low
    chunks = [slice(at, at + FF_CHUNK) for at in range(0, wi_ref.shape[1], FF_CHUNK)]
    pre = mm(normed_low, wi_ref[:, chunks[0]], nn)
    total = normed + bias_outer
    for index, chunk in enumerate(chunks):
        here = pre + bias_inner_ref[:, chunk]
        if index + 1 < len(chunks):
            pre = mm(normed_low, wi_ref[:, chunks[index + 1]], nn)
        value, derivative = gelu_pair(here)
        value = value.astype(jnp.bfloat16)
        active_ref[:, chunk] = value
        slope[:, chunk] = derivative
        total = total + mm(value, wf_ref[chunk, :], nn)
    hat_two, inverse_two = normalise(total)
    final_ref[...] = (hat_two * gain_two + shift_two).astype(jnp.bfloat16)
    cot = cot_ref[...].astype(jnp.float32)
    grad_total = norm_back(cot * gain_two, hat_two, inverse_two)
    grad_outer = grad_total.astype(jnp.bfloat16)
    outer_ref[...] = grad_outer
    sums_ref[2:3, :] += jnp.sum(cot * hat_two, axis=0, keepdims=True)
    sums_ref[3:4, :] += jnp.sum(cot, axis=0, keepdims=True)
    sums_ref[4:5, :] += jnp.sum(grad_outer.astype(jnp.float32), axis=0, keepdims=True)
    back = mm(grad_outer, wf_ref[chunks[0], :], nt)
    for index, chunk in enumerate(chunks):
        here = back
        if index + 1 < len(chunks):
            back = mm(grad_outer, wf_ref[chunks[index + 1], :], nt)
        grad_inner = (here * slope[:, chunk]).astype(jnp.bfloat16)
        inner_ref[:, chunk] = grad_inner
        inner_sum_ref[:, chunk] += jnp.sum(grad_inner.astype(jnp.float32), axis=0, keepdims=True)
        grad_total = grad_total + mm(grad_inner, wi_ref[:, chunk], nt)
    sums_ref[0:1, :] += jnp.sum(grad_total * hat_one, axis=0, keepdims=True)
    sums_ref[1:2, :] += jnp.sum(grad_total, axis=0, keepdims=True)
    residual = norm_back(grad_total * gain_one, hat_one, inverse_one)
    residual_ref[...] = residual
    attended = residual.astype(jnp.bfloat16)
    attended_ref[...] = attended
    dmix_ref[...] = mm(attended, wo_ref[...], nt).astype(jnp.bfloat16)


def token_layer(x, mix, cot, w_out, w_inner, w_outer, bias_inner, rows):
    count = x.shape[0]
    hidden = w_inner.shape[1]
    tile = lambda lanes: pl.BlockSpec((TOKENS, lanes), lambda i: (i, 0))
    once = lambda a, b: pl.BlockSpec((a, b), lambda i: (0, 0), pipeline_mode=pl.Buffered(1))
    sums = lambda a, b: pl.BlockSpec((a, b), lambda i: (0, 0))
    low = lambda lanes: jax.ShapeDtypeStruct((count, lanes), jnp.bfloat16)
    return pl.pallas_call(
        token_kernel,
        grid=(count // TOKENS,),
        in_specs=[
            tile(D), tile(D), tile(D), once(D, D), once(D, hidden), once(hidden, D),
            once(1, hidden), once(8, D),
        ],
        out_specs=[
            tile(D), tile(hidden), tile(D), tile(hidden), tile(D), tile(D), tile(D), tile(D),
            sums(8, D), sums(1, hidden),
        ],
        out_shape=[
            low(D), low(hidden), low(D), low(hidden), low(D), low(D), low(D),
            jax.ShapeDtypeStruct((count, D), jnp.float32),
            jax.ShapeDtypeStruct((8, D), jnp.float32),
            jax.ShapeDtypeStruct((1, hidden), jnp.float32),
        ],
        scratch_shapes=[pltpu.VMEM((TOKENS, hidden), jnp.float32)],
        compiler_params=pltpu.CompilerParams(
            dimension_semantics=("arbitrary",), vmem_limit_bytes=VMEM_BYTES
        ),
        cost_estimate=pl.CostEstimate(
            flops=22000000000, transcendentals=6000000, bytes_accessed=40000000
        ),
        name="token_layer",
    )(x, mix, cot, w_out, w_inner, w_outer, bias_inner, rows)


def chip_bits():
    bits = []
    bit = 2
    while bit < lax.axis_size("batch"):
        bits.append(bit)
        bit *= 2
    return bits


def digit(bit):
    return lax.axis_index("batch") // bit % 2


def across(tensor, bits):
    count = lax.axis_size("batch")
    return lax.ppermute(tensor, "batch", [(i, i ^ bits[i & 1]) for i in range(count)])


def own_digit(bits):
    return jnp.where(digit(1) == 1, digit(bits[1]), digit(bits[0]))


def along(tensor, shift):
    ring = lax.axis_size("mem")
    return lax.ppermute(tensor, "mem", [(i, (i + shift) % ring) for i in range(ring)])


def rows_of(tensor, start, count):
    return lax.dynamic_slice(tensor, (start, 0), (count, tensor.shape[1]))


class Sum:
    def __init__(self, tensor):
        bits = chip_bits()
        self.bits = [(1, 1)] + list(zip(bits, bits[::-1]))
        self.state = tensor
        self.at = 0
        self.stages = 2 * len(self.bits) + 2

    def step(self):
        count, tensor = len(self.bits), self.state
        ring, me = lax.axis_size("mem"), lax.axis_index("mem")
        if self.at < count:
            bit = self.bits[self.at]
            half = tensor.shape[0] // 2
            mine = own_digit(bit)
            got = across(rows_of(tensor, (1 - mine) * half, half), bit)
            kept = rows_of(tensor, mine * half, half)
            self.state = (kept.astype(jnp.float32) + got.astype(jnp.float32)).astype(jnp.bfloat16)
        elif self.at == count:
            block = tensor.shape[0] // ring
            total = rows_of(tensor, me * block, block).astype(jnp.float32)
            for shift in range(1, ring):
                sent = rows_of(tensor, (me + shift) % ring * block, block)
                total = total + along(sent, shift).astype(jnp.float32)
            self.state = total.astype(jnp.bfloat16)
        elif self.at == count + 1:
            parts = [tensor] + [along(tensor, shift) for shift in range(1, ring)]
            self.state = jnp.concatenate(parts, axis=0)
        else:
            bit = self.bits[2 * count + 1 - self.at]
            self.state = jnp.concatenate([tensor, across(tensor, bit)], axis=0)
        self.at += 1

    def places(self):
        ring = lax.axis_size("mem")
        weight = ring * lax.axis_size("batch") // 2
        index = jnp.arange(2 * weight, dtype=jnp.int32)
        place = (lax.axis_index("mem") - index % ring) % ring
        core = index // weight % 2
        for even, odd in self.bits:
            own = jnp.where(core == 1, digit(odd), digit(even))
            place = place + (index // weight % 2 + own) % 2 * weight
            weight //= 2
        return place


def together(active, tree):
    states, tree = lax.optimization_barrier(([item.state for item in active], tree))
    for item, state in zip(active, states):
        item.state = state
    return tree


def placed(item):
    tensor, place = item.state, item.places()
    blocks = place.shape[0]
    if tensor.shape[0] // blocks % 8:
        tensor = tensor.reshape(blocks, -1, tensor.shape[1])[place].reshape(tensor.shape)
        place = jnp.arange(8, dtype=jnp.int32)
    return tensor, place


def block_of(place_ref, in_ref, index):
    rows = in_ref.shape[0] // place_ref.shape[0]
    start = pl.multiple_of(place_ref[index] * rows, 8)
    return in_ref[pl.ds(start, rows), :].astype(jnp.float32)


def settle_pairs_kernel(count, place_ref, in_ref, *rest):
    outs, full = rest[-6:-1], rest[-1]
    rows = in_ref.shape[0] // place_ref.shape[0]

    @pl.when(pl.program_id(0) == 0)
    def _():
        for item in range(place_ref.shape[0]):
            full[item * rows : (item + 1) * rows, :] = block_of(place_ref, in_ref, item)
        grads = count * 4 * PAIR
        outs[4][...] = full[grads : grads + outs[4].shape[0], :]

    for index in range(4):
        start = pl.multiple_of((pl.program_id(0) * 4 + index) * PAIR, PAIR)
        outs[index][...] = full[pl.ds(start, PAIR), :].T


def settle_pairs(item, first, count, earlier, after):
    tensor, place = placed(item)
    rows, lanes = tensor.shape
    square = jax.ShapeDtypeStruct((D, D), jnp.float32)
    return pl.pallas_call(
        functools.partial(settle_pairs_kernel, count),
        grid_spec=pltpu.PrefetchScalarGridSpec(
            num_scalar_prefetch=1,
            grid=(count,),
            in_specs=[pl.BlockSpec((rows, lanes), lambda i, p: (0, 0))]
            + [pl.BlockSpec(memory_space=pl.ANY)] * len(earlier),
            out_specs=[pl.BlockSpec((lanes, PAIR), lambda i, p: (0, first + i))] * 4
            + [pl.BlockSpec((after, lanes), lambda i, p: (0, 0))],
            scratch_shapes=[pltpu.VMEM((rows, lanes), jnp.float32)],
        ),
        out_shape=[square] * 4 + [jax.ShapeDtypeStruct((after, lanes), jnp.float32)],
        input_output_aliases={2 + index: index for index in range(len(earlier))},
        compiler_params=pltpu.CompilerParams(vmem_limit_bytes=48 * 1024 * 1024),
        name="settle_pairs",
    )(place, tensor, *earlier)


def sinusoid():
    fine_count = 32
    frequency = 1.0 / 10000.0 ** (
        jnp.arange(0, D, 2, dtype=jnp.int32).astype(jnp.float32) / D
    )
    coarse = (KEYS - 1 - fine_count * jnp.arange(REL // fine_count, dtype=jnp.int32)).astype(
        jnp.float32
    )[:, None] * frequency[None]
    fine = jnp.arange(fine_count, dtype=jnp.int32).astype(jnp.float32)[:, None] * frequency[None]
    sin_coarse, cos_coarse = jnp.sin(coarse)[:, None], jnp.cos(coarse)[:, None]
    sin_fine, cos_fine = jnp.sin(fine)[None], jnp.cos(fine)[None]
    sine = sin_coarse * cos_fine - cos_coarse * sin_fine
    cosine = cos_coarse * cos_fine + sin_coarse * sin_fine
    return jnp.concatenate([sine, cosine], axis=-1).reshape(REL, D).astype(jnp.bfloat16)


EXTRA = 256
FIRST = 3
VECTORS = 24


WIDE = 512


def widen_kernel(outer_ref, inner_ref, outer_out, inner_out):
    outer_out[...] = outer_ref[...].astype(jnp.float32).T
    inner_out[...] = inner_ref[...].astype(jnp.float32)


def widen(outer, inner):
    hidden = inner.shape[1]
    return pl.pallas_call(
        widen_kernel,
        grid=(hidden // WIDE,),
        in_specs=[
            pl.BlockSpec((D, WIDE), lambda i: (0, i)),
            pl.BlockSpec((D, WIDE), lambda i: (0, i)),
        ],
        out_specs=[
            pl.BlockSpec((WIDE, D), lambda i: (i, 0)),
            pl.BlockSpec((D, WIDE), lambda i: (0, i)),
        ],
        out_shape=[
            jax.ShapeDtypeStruct((hidden, D), jnp.float32),
            jax.ShapeDtypeStruct((D, hidden), jnp.float32),
        ],
        compiler_params=pltpu.CompilerParams(vmem_limit_bytes=VMEM_BYTES),
        name="widen",
    )(outer, inner)


def shards(
    content_in, query_in, memory, sequence_lengths, order_rank, segment_ids,
    w_query, w_key, w_value, w_out, w_rel,
    bias_content, bias_position, bias_segment, segment_embed,
    gain_one, shift_one, w_inner, bias_inner, w_outer, bias_outer, gain_two, shift_two,
    content_cotangent, query_cotangent,
):
    wide = lambda tensor: tensor.astype(jnp.float32)
    low = lambda tensor: tensor.astype(jnp.bfloat16)
    both = ("batch", "mem")
    past = lax.all_to_all(memory, "mem", split_axis=0, concat_axis=1, tiled=True)[0]
    content = content_in[0]
    inputs = jnp.concatenate([content, query_in[0]], axis=0)
    cotangent = jnp.concatenate([content_cotangent[0], query_cotangent[0]], axis=0)
    positions = sinusoid()
    relative = low(mm(positions, w_rel, nn))
    frame = jnp.concatenate([past, content], axis=0)
    keys = low(mm(frame, w_key, nn))
    values = low(mm(frame, w_value, nn))
    projected = mm(inputs, w_query, nn)
    query_content = low(projected + wide(bias_content))
    query_position = low(projected + wide(bias_position))
    query_segment = low(projected + wide(bias_segment))
    mixture, inverse, probs = attention_forward(
        sequence_lengths, query_content, query_position, query_segment, keys, values, relative,
        segment_embed, segment_ids, order_rank,
    )
    rows = jnp.stack(
        [wide(t) for t in (gain_one, shift_one, gain_two, shift_two, bias_outer)]
        + [jnp.zeros((D,), jnp.float32)] * 3
    )
    (
        final_out, active_low, grad_outer_low, grad_inner_low, grad_attended, grad_mixture,
        normed_low, grad_residual, token_sums, inner_bias_sum,
    ) = token_layer(
        inputs, mixture, cotangent, w_out, w_inner, w_outer, wide(bias_inner)[None], rows
    )
    low_mm = lambda left, right: low(mm(left, right, tn))
    grad_outer_w = low_mm(grad_outer_low, active_low)
    grad_inner_w = low_mm(normed_low, grad_inner_low)
    grad_outer_w, grad_inner_w, grad_mixture, grad_attended = lax.optimization_barrier(
        (grad_outer_w, grad_inner_w, grad_mixture, grad_attended)
    )
    outer_sum, inner_sum = lax.psum((grad_outer_w, grad_inner_w), both)

    def attention_part(operands):
        (
            probs, grad_mixture, mixture, inverse, query_content, query_position, query_segment,
            keys, values, relative, segment_ids, inputs, frame, positions, grad_attended,
            token_sums, inner_bias_sum, segment_embed, grad_residual, w_query, w_key, w_value, final_out,
        ) = operands
        common = (
            mixture, inverse, query_content, query_position, query_segment, keys, values, relative,
            segment_embed, segment_ids, inputs, frame, positions,
        )
        rows_of_pairs = lambda count: count * 4 * PAIR
        half, other = FIRST, PAIRS - FIRST
        chain = attention_backward(
            0, half, 0, [None] * 4 + [rows_of_pairs(half) + D], probs, grad_mixture, *common
        )
        early = Sum(lax.dynamic_update_slice(chain[4], low_mm(mixture, grad_attended), (rows_of_pairs(half), 0)))
        early.step()
        chain, grad_mixture = together([early], (list(chain[:4]), grad_mixture))
        early.step()
        chain = attention_backward(
            half, other, 0, chain + [rows_of_pairs(other) + EXTRA], probs, grad_mixture, *common
        )
        grad_projected, grad_keys, grad_values, small, bucket = together([early], list(chain))
        vectors = jnp.concatenate(
            [token_sums, inner_bias_sum.reshape(-1, D), jnp.zeros((4, D), jnp.float32), small], axis=0
        )
        vectors = jnp.pad(vectors, ((0, EXTRA - vectors.shape[0]), (0, 0)))
        late = Sum(lax.dynamic_update_slice(bucket, low(vectors), (rows_of_pairs(other), 0)))
        while late.at < late.stages:
            late.step()
            if early.at < early.stages:
                early.step()
                together([late, early], ())
                if early.at == early.stages:
                    *sums, out_sum = settle_pairs(early, 0, half, (), D)
                    sums, out_sum = together([late], (sums, out_sum))
        *sums, vectors = settle_pairs(late, half, other, sums, VECTORS)
        vectors = [vectors[index] for index in (16, 17, 18)] + [vectors[19:21]] + [
            vectors[index] for index in (0, 1, 4, 2, 3)
        ] + [vectors[8:12].reshape(-1)]
        finals = (final_out[None, :SEG], final_out[None, SEG:])
        grad_inputs = grad_residual + mm(grad_projected, w_query, nt)
        grad_content = (
            grad_inputs[:SEG] + mm(grad_keys[MEM:], w_key, nt) + mm(grad_values[MEM:], w_value, nt)
        )
        return low(grad_content), low(grad_inputs[SEG:]), sums, out_sum, vectors, finals

    operands = (
        probs, grad_mixture, mixture, inverse, query_content, query_position, query_segment, keys,
        values, relative, segment_ids, inputs, frame, positions, grad_attended, token_sums,
        inner_bias_sum, segment_embed, grad_residual, w_query, w_key, w_value, final_out,
    )
    shapes = jax.eval_shape(attention_part, operands)
    grad_content, grad_query, sums, out_sum, vectors, finals = lax.cond(
        sequence_lengths[0] > -1,
        attention_part,
        lambda operands: jax.tree.map(lambda item: jnp.zeros(item.shape, item.dtype), shapes),
        operands,
    )
    query_sum, key_sum, value_sum, rel_sum = sums
    outer_sum, inner_sum = widen(outer_sum, inner_sum)
    content_sum, position_sum, segment_sum, embed_sum, gain1, shift1, bias, gain2, shift2, hidden = vectors
    return (
        *finals, grad_content[None], grad_query[None],
        query_sum, key_sum, value_sum, out_sum, rel_sum,
        content_sum, position_sum, segment_sum, embed_sum, gain1, shift1, inner_sum, hidden,
        outer_sum, bias, gain2, shift2,
    )


def solution(mesh):
    both = ("batch", "mem")
    rows = P(both, None, None)
    return jax.shard_map(
        shards,
        mesh=mesh,
        in_specs=(rows, rows, P("batch", "mem", None), P(both), P(both, None), P(both, None))
        + (P(),) * 17
        + (rows, rows),
        out_specs=(rows,) * 4 + (P(),) * 17,
        check_vma=False,
    )
```

```python
import functools

import jax
import jax.numpy as jnp
from jax import lax
from jax.experimental import pallas as pl
from jax.experimental.pallas import tpu as pltpu
from jax.sharding import PartitionSpec as P

D = 768
HEADS = 12
HEAD = 64
SEG = 512
MEM = 384
KEYS = MEM + SEG
REL = MEM + 2 * SEG
PAIR = 2 * HEAD
PAIRS = HEADS // 2
ROWS = 256
SUB = 128
CHUNK = 32
WIN = KEYS + SUB
FAR = -1e30
LOG2E = 1.4426950408889634
SCALE = HEAD**-0.5
VMEM_BYTES = 60 * 1024 * 1024
nt = (((1,), (1,)), ((), ()))
nn = (((1,), (0,)), ((), ()))
tn = (((0,), (0,)), ((), ()))


def mm(left, right, dims):
    return lax.dot_general(left, right, dims, preferred_element_type=jnp.float32)


def lane_low(rows):
    return lax.broadcasted_iota(jnp.int32, (rows, PAIR), 1) < HEAD


def tile_spans(tile):
    start = pl.multiple_of(tile * SUB, SUB)
    return [start, start + SEG]


def both_rows(ref, spans):
    return jnp.concatenate([ref[pl.ds(start, SUB), :] for start in spans], axis=0)


def spread(row_ref, out_ref):
    for at in range(0, SEG, SUB):
        block = jnp.broadcast_to(row_ref[:, at : at + SUB], (SUB, SUB))
        out_ref[at : at + SUB, :] = block.T


def twice_rows(ref, tile):
    rows = ref[pl.ds(pl.multiple_of(tile * SUB, SUB), SUB), :]
    return jnp.concatenate([rows, rows], axis=0)


def key_segment_zero(seg_col):
    return jnp.concatenate([jnp.ones((MEM, PAIR), jnp.bool_), seg_col[...] == 0], axis=0)


def forward_kernel(
    length_ref, qc_ref, qp_ref, qs_ref, k_ref, v_ref, rel_ref, emb_ref, seg_ref, rank_ref,
    mix_ref, inv_ref, prob_ref, kcat, vcat, seg_col, rank_col,
):
    @pl.when(pl.program_id(0) == 0)
    def _():
        spread(seg_ref, seg_col)
        spread(rank_ref, rank_col)

    same = key_segment_zero(seg_col)
    live = lax.broadcasted_iota(jnp.int32, (1, SEG), 1) < length_ref[0]
    krank = jnp.where(live, rank_ref[...], 2 * SEG)
    zero_row = emb_ref[0:1, :].astype(jnp.float32)
    one_row = emb_ref[1:2, :].astype(jnp.float32)
    zero_roll = pltpu.roll(zero_row, HEAD, 1)
    one_roll = pltpu.roll(one_row, HEAD, 1)
    low_row = lane_low(1)
    for head in range(2):
        if head == 0:
            near = jnp.where(low_row, zero_row, one_roll)
            away = jnp.where(low_row, one_row, zero_roll)
        else:
            near = jnp.where(low_row, zero_roll, one_row)
            away = jnp.where(low_row, one_roll, zero_row)
        kcat[head, :, :PAIR] = k_ref[...]
        kcat[head, :, PAIR:] = jnp.where(same, near, away).astype(jnp.bfloat16)
    vcat[:, :PAIR] = v_ref[...]
    vcat[:, PAIR:] = jnp.ones((KEYS, PAIR), jnp.bfloat16)

    def block(tile, carry):
        spans = tile_spans(tile)
        low = lane_low(ROWS)
        zero = jnp.zeros((ROWS, PAIR), jnp.bfloat16)
        qc = both_rows(qc_ref, spans)
        qp = both_rows(qp_ref, spans)
        qs = both_rows(qs_ref, spans)
        qs_roll = pltpu.roll(qs.astype(jnp.float32), HEAD, 1).astype(jnp.bfloat16)
        seg_keep = (twice_rows(seg_col, tile) == 0) == low
        rank = twice_rows(rank_col, tile) - jnp.where(
            lax.broadcasted_iota(jnp.int32, (ROWS, PAIR), 0) < SUB, 0, 1
        )
        rank = jnp.concatenate([rank] * (SEG // PAIR), axis=1)
        factor = SCALE * LOG2E
        window = rel_ref[pl.ds(3 - tile, WIN // SUB)].reshape(WIN, PAIR)
        grid = mm(
            jnp.concatenate([jnp.where(low, qp, zero), jnp.where(low, zero, qp)], axis=0), window, nt
        )
        parts = []
        for head in range(2):
            mine = low if head == 0 else ~low
            twice = jnp.where(mine, qs, qs_roll)
            qcat = jnp.concatenate(
                [jnp.where(mine, qc, zero), jnp.where(seg_keep, twice, zero)], axis=1
            )
            score = mm(qcat, kcat[head], nt)
            for row in range(0, ROWS, CHUNK):
                at = row % SUB
                shifted = pltpu.roll(
                    grid[head * ROWS + row : head * ROWS + row + CHUNK],
                    WIN - SUB + 1 + at, 1, stride=1, stride_axis=0,
                )[:, :KEYS]
                logit = score[row : row + CHUNK] + shifted
                current = jnp.where(krank <= rank[row : row + CHUNK], logit[:, MEM:], FAR)
                logit = jnp.concatenate([logit[:, :MEM], current], axis=1)
                top = jnp.max(logit, axis=-1, keepdims=True)
                soft = jnp.exp2((logit - top) * factor).astype(jnp.bfloat16)
                prob_ref[head, pl.ds(spans[row // SUB] + at, CHUNK), :] = soft
                parts.append(soft)
        summed = mm(jnp.concatenate(parts, axis=0), vcat[...], nn)
        scale = 1.0 / summed[:, PAIR:]
        mixed = summed[:, :PAIR] * scale
        mixed = jnp.where(low, mixed[:ROWS], mixed[ROWS:]).astype(jnp.bfloat16)
        scale = jnp.where(low, scale[:ROWS], scale[ROWS:])
        for index, start in enumerate(spans):
            mix_ref[pl.ds(start, SUB), :] = mixed[index * SUB : (index + 1) * SUB]
            inv_ref[pl.ds(start, SUB), :] = scale[index * SUB : (index + 1) * SUB]
        return carry

    lax.fori_loop(0, SEG // SUB, block, 0)


def whole(rows, lanes):
    return pl.BlockSpec((rows, lanes), lambda p: (0, 0))


def attention_forward(length, qc, qp, qs, keys, values, rel, emb, seg, rank):
    pair = lambda rows: pl.BlockSpec((rows, PAIR), lambda p: (0, p))
    return pl.pallas_call(
        forward_kernel,
        grid=(PAIRS,),
        in_specs=[
            pl.BlockSpec(memory_space=pltpu.SMEM),
            pair(2 * SEG), pair(2 * SEG), pair(2 * SEG), pair(KEYS), pair(KEYS),
            pl.BlockSpec((REL // SUB, SUB, PAIR), lambda p: (0, 0, p)),
            pair(2), whole(1, SEG), whole(1, SEG),
        ],
        out_specs=[
            pair(2 * SEG), pair(2 * SEG),
            pl.BlockSpec((None, 2, 2 * SEG, KEYS), lambda p: (p, 0, 0, 0)),
        ],
        out_shape=[
            jax.ShapeDtypeStruct((2 * SEG, D), jnp.bfloat16),
            jax.ShapeDtypeStruct((2 * SEG, D), jnp.float32),
            jax.ShapeDtypeStruct((PAIRS, 2, 2 * SEG, KEYS), jnp.bfloat16),
        ],
        scratch_shapes=[
            pltpu.VMEM((2, KEYS, 2 * PAIR), jnp.bfloat16),
            pltpu.VMEM((KEYS, 2 * PAIR), jnp.bfloat16),
            pltpu.VMEM((SEG, PAIR), jnp.int32),
            pltpu.VMEM((SEG, PAIR), jnp.int32),
        ],
        compiler_params=pltpu.CompilerParams(
            dimension_semantics=("arbitrary",), vmem_limit_bytes=VMEM_BYTES
        ),
        cost_estimate=pl.CostEstimate(
            flops=30000000000, transcendentals=11000000, bytes_accessed=30000000
        ),
        name="attention_forward",
    )(length, qc, qp, qs, keys, values, rel.reshape(REL // SUB, SUB, D), emb, seg, rank)


def backward_kernel(
    prob_ref, dmix_ref, mix_ref, inv_ref, qc_ref, qp_ref, qs_ref, k_ref, v_ref, rel_ref, emb_ref,
    seg_ref, inputs_ref, frame_ref, positions_ref, *rest,
):
    dproj_ref, dk_ref, dv_ref, small_ref, bucket_ref, kcat, dk_acc, dv_acc, drel_acc, seg_col = rest[-10:]

    @pl.when(pl.program_id(0) == 0)
    def _():
        spread(seg_ref, seg_col)

    kcat[:, :PAIR] = k_ref[...]
    kcat[:, PAIR:] = jnp.where(key_segment_zero(seg_col) == lane_low(KEYS), 1.0, 0.0).astype(
        jnp.bfloat16
    )
    dk_acc[...] = jnp.zeros_like(dk_acc)
    dv_acc[...] = jnp.zeros_like(dv_acc)
    drel_acc[...] = jnp.zeros_like(drel_acc)
    small_ref[...] = jnp.zeros_like(small_ref)

    def block(tile, carry):
        spans = tile_spans(tile)
        low = lane_low(ROWS)
        zero = jnp.zeros((ROWS, PAIR), jnp.bfloat16)
        row_index = lax.broadcasted_iota(jnp.int32, (ROWS, ROWS), 0)
        column_index = lax.broadcasted_iota(jnp.int32, (ROWS, ROWS), 1)
        flip = jnp.where(
            (row_index // SUB == column_index // SUB)
            & (row_index % SUB + column_index % SUB == SUB - 1),
            1.0, 0.0,
        ).astype(jnp.bfloat16)
        dmix = (
            both_rows(dmix_ref, spans).astype(jnp.float32) * (both_rows(inv_ref, spans) * SCALE)
        ).astype(jnp.bfloat16)
        weighted = dmix.astype(jnp.float32) * both_rows(mix_ref, spans).astype(jnp.float32)
        qc = both_rows(qc_ref, spans)
        qp = both_rows(qp_ref, spans)
        qs = both_rows(qs_ref, spans).astype(jnp.float32)
        qp_turned = mm(flip, qp, nn).astype(jnp.bfloat16)
        first_rows = twice_rows(seg_col, tile) == 0
        emb = emb_ref[...].astype(jnp.float32)
        dm = jnp.concatenate([jnp.where(low, dmix, zero), jnp.where(low, zero, dmix)], axis=0)
        qc_both = jnp.concatenate([jnp.where(low, qc, zero), jnp.where(low, zero, qc)], axis=0)
        qp_both = jnp.concatenate(
            [jnp.where(low, qp_turned, zero), jnp.where(low, zero, qp_turned)], axis=0
        )
        row_sum = jnp.concatenate(
            [
                jnp.sum(jnp.where(low, weighted, 0.0), axis=-1, keepdims=True),
                jnp.sum(jnp.where(low, 0.0, weighted), axis=-1, keepdims=True),
            ],
            axis=0,
        )
        prob = jnp.concatenate([both_rows(prob_ref.at[head], spans) for head in range(2)], axis=0)
        dprob = mm(dm, v_ref[...], nt)
        total = jnp.concatenate(
            [
                (
                    prob[at : at + CHUNK].astype(jnp.float32)
                    * (dprob[at : at + CHUNK] - row_sum[at : at + CHUNK])
                ).astype(jnp.bfloat16)
                for at in range(0, 2 * ROWS, CHUNK)
            ],
            axis=0,
        )
        back = mm(total, kcat[...], nn)
        turned = [mm(flip, total[head * ROWS : (head + 1) * ROWS], nn) for head in range(2)]
        grid = jnp.concatenate(
            [
                pltpu.roll(
                    jnp.concatenate(
                        [turned[head][row : row + CHUNK], jnp.zeros((CHUNK, SUB), jnp.float32)],
                        axis=1,
                    ),
                    row % SUB, 1, stride=1, stride_axis=0,
                ).astype(jnp.bfloat16)
                for head in range(2)
                for row in range(0, ROWS, CHUNK)
            ],
            axis=0,
        )
        window = rel_ref[pl.ds(3 - tile, WIN // SUB)].reshape(WIN, PAIR)
        dqp = mm(grid, window, nn)
        dqp = jnp.where(low, dqp[:ROWS], dqp[ROWS:]).astype(jnp.bfloat16)
        dqp_wide = mm(flip, dqp, nn)
        dv_acc[...] += mm(dm, prob, tn)
        dk_acc[...] += mm(qc_both, total, tn)
        drel = mm(qp_both, grid, tn)
        for part in range(WIN // SUB):
            drel_acc[3 - tile + part] += drel[:, part * SUB : (part + 1) * SUB]
        dqc_wide = (
            jnp.where(low, back[:ROWS, :PAIR], back[ROWS:, :PAIR])
            .astype(jnp.bfloat16)
            .astype(jnp.float32)
        )
        sums = [back[head * ROWS : (head + 1) * ROWS, PAIR:] for head in range(2)]
        rolled = [pltpu.roll(part, HEAD, 1) for part in sums]
        key_zero = jnp.where(low, sums[0], rolled[1])
        key_one = jnp.where(low, rolled[0], sums[1])
        near = jnp.where(first_rows, key_zero, key_one)
        other = jnp.where(first_rows, key_one, key_zero)
        dqs_wide = (near * emb[0:1] + other * emb[1:2]).astype(jnp.bfloat16).astype(jnp.float32)
        dproj = (dqc_wide + dqp_wide + dqs_wide).astype(jnp.bfloat16)
        for index, start in enumerate(spans):
            dproj_ref[pl.ds(start, SUB), :] = dproj[index * SUB : (index + 1) * SUB]
        rows = [dqc_wide, dqp_wide, dqs_wide, near * qs, other * qs]
        for row, value in enumerate(rows):
            small_ref[row : row + 1, :] += jnp.sum(value, axis=0, keepdims=True)
        return carry

    lax.fori_loop(0, SEG // SUB, block, 0, unroll=True)
    dk_low = dk_acc[...].astype(jnp.bfloat16)
    dv_low = (dv_acc[...] * (1.0 / SCALE)).astype(jnp.bfloat16)
    dk_ref[...] = dk_low.T
    dv_ref[...] = dv_low.T
    drel_low = jnp.concatenate(
        [drel_acc[part] for part in range(REL // SUB)], axis=1
    ).astype(jnp.bfloat16)
    grads = (
        mm(dproj_ref[...], inputs_ref[...], tn), mm(dk_low, frame_ref[...], nn),
        mm(dv_low, frame_ref[...], nn), mm(drel_low, positions_ref[...], nn),
    )
    for index, grad in enumerate(grads):
        bucket_ref[index * PAIR : (index + 1) * PAIR, :] = grad.astype(jnp.bfloat16)


def attention_backward(
    first, count, bucket_block, chain, prob, dmix, mix, inv, qc, qp, qs, keys, values, rel, emb, seg,
    inputs, frame, positions,
):
    pair = lambda rows: pl.BlockSpec((rows, PAIR), lambda p: (0, first + p))
    rel_block = pl.BlockSpec((REL // SUB, SUB, PAIR), lambda p: (0, 0, first + p))
    bucket_rows = chain[4] if isinstance(chain[4], int) else chain[4].shape[0]
    passed = [item for item in chain if not isinstance(item, int) and item is not None]
    places = [at for at, item in enumerate(chain) if not isinstance(item, int) and item is not None]
    return pl.pallas_call(
        backward_kernel,
        grid=(count,),
        in_specs=[
            pl.BlockSpec((None, 2, 2 * SEG, KEYS), lambda p: (first + p, 0, 0, 0)),
            pair(2 * SEG), pair(2 * SEG), pair(2 * SEG), pair(2 * SEG), pair(2 * SEG), pair(2 * SEG),
            pair(KEYS), pair(KEYS), rel_block, pair(2), whole(1, SEG),
            whole(2 * SEG, D), whole(KEYS, D), whole(REL, D),
        ]
        + [pl.BlockSpec(memory_space=pl.ANY)] * len(passed),
        out_specs=[
            pair(2 * SEG), pair(KEYS), pair(KEYS), pair(8),
            pl.BlockSpec((4 * PAIR, D), lambda p: (bucket_block + p, 0)),
        ],
        out_shape=[
            jax.ShapeDtypeStruct((2 * SEG, D), jnp.bfloat16),
            jax.ShapeDtypeStruct((KEYS, D), jnp.bfloat16),
            jax.ShapeDtypeStruct((KEYS, D), jnp.bfloat16),
            jax.ShapeDtypeStruct((8, D), jnp.float32),
            jax.ShapeDtypeStruct((bucket_rows, D), jnp.bfloat16),
        ],
        scratch_shapes=[
            pltpu.VMEM((KEYS, 2 * PAIR), jnp.bfloat16),
            pltpu.VMEM((PAIR, KEYS), jnp.float32),
            pltpu.VMEM((PAIR, KEYS), jnp.float32),
            pltpu.VMEM((REL // SUB, PAIR, SUB), jnp.float32),
            pltpu.VMEM((SEG, PAIR), jnp.int32),
        ],
        input_output_aliases={15 + index: at for index, at in enumerate(places)},
        compiler_params=pltpu.CompilerParams(
            dimension_semantics=("arbitrary",), vmem_limit_bytes=VMEM_BYTES
        ),
        cost_estimate=pl.CostEstimate(
            flops=count * 8000000000, transcendentals=0, bytes_accessed=count * 8000000
        ),
        name="attention_backward",
    )(
        prob, dmix, mix, inv, qc, qp, qs, keys, values, rel.reshape(REL // SUB, SUB, D), emb, seg,
        inputs, frame, positions, *passed,
    )


norm_epsilon = 1e-06
TOKENS = 256
FF_CHUNK = 768
half_erfc = (0.5 * 0.254829592, 0.5 * -0.284496736, 0.5 * 1.421413741, 0.5 * -1.453152027, 0.5 * 1.061405429)


def gelu_pair(x):
    gauss = jnp.exp2(x * x * (-0.5 * LOG2E))
    t = 1.0 / (1.0 + (0.3275911 * 0.7071067811865476) * jnp.abs(x))
    a1, a2, a3, a4, a5 = half_erfc
    tail = t * (a1 + t * (a2 + t * (a3 + t * (a4 + t * a5)))) * gauss
    cdf = jnp.where(x >= 0.0, 1.0 - tail, tail)
    return x * cdf, cdf + x * gauss * 0.3989422804014327


def normalise(tensor):
    centred = tensor - jnp.mean(tensor, axis=-1, keepdims=True)
    inverse = lax.rsqrt(jnp.mean(centred * centred, axis=-1, keepdims=True) + norm_epsilon)
    return centred * inverse, inverse


def norm_back(grad, hat, inverse):
    return inverse * (
        grad
        - jnp.mean(grad, axis=-1, keepdims=True)
        - hat * jnp.mean(grad * hat, axis=-1, keepdims=True)
    )


def token_kernel(
    x_ref, mix_ref, cot_ref, wo_ref, wi_ref, wf_ref, bias_inner_ref, rows_ref,
    final_ref, active_ref, outer_ref, inner_ref, attended_ref, dmix_ref, low_ref, residual_ref,
    sums_ref, inner_sum_ref,
    slope,
):
    @pl.when(pl.program_id(0) == 0)
    def _():
        sums_ref[...] = jnp.zeros_like(sums_ref)
        inner_sum_ref[...] = jnp.zeros_like(inner_sum_ref)

    gain_one, shift_one = rows_ref[0:1, :], rows_ref[1:2, :]
    gain_two, shift_two = rows_ref[2:3, :], rows_ref[3:4, :]
    bias_outer = rows_ref[4:5, :]
    hat_one, inverse_one = normalise(
        x_ref[...].astype(jnp.float32) + mm(mix_ref[...], wo_ref[...], nn)
    )
    normed = hat_one * gain_one + shift_one
    normed_low = normed.astype(jnp.bfloat16)
    low_ref[...] = normed_low
    chunks = [slice(at, at + FF_CHUNK) for at in range(0, wi_ref.shape[1], FF_CHUNK)]
    pre = mm(normed_low, wi_ref[:, chunks[0]], nn)
    total = normed + bias_outer
    for index, chunk in enumerate(chunks):
        here = pre + bias_inner_ref[:, chunk]
        if index + 1 < len(chunks):
            pre = mm(normed_low, wi_ref[:, chunks[index + 1]], nn)
        value, derivative = gelu_pair(here)
        value = value.astype(jnp.bfloat16)
        active_ref[:, chunk] = value
        slope[:, chunk] = derivative
        total = total + mm(value, wf_ref[chunk, :], nn)
    hat_two, inverse_two = normalise(total)
    final_ref[...] = (hat_two * gain_two + shift_two).astype(jnp.bfloat16)
    cot = cot_ref[...].astype(jnp.float32)
    grad_total = norm_back(cot * gain_two, hat_two, inverse_two)
    grad_outer = grad_total.astype(jnp.bfloat16)
    outer_ref[...] = grad_outer
    sums_ref[2:3, :] += jnp.sum(cot * hat_two, axis=0, keepdims=True)
    sums_ref[3:4, :] += jnp.sum(cot, axis=0, keepdims=True)
    sums_ref[4:5, :] += jnp.sum(grad_outer.astype(jnp.float32), axis=0, keepdims=True)
    back = mm(grad_outer, wf_ref[chunks[0], :], nt)
    for index, chunk in enumerate(chunks):
        here = back
        if index + 1 < len(chunks):
            back = mm(grad_outer, wf_ref[chunks[index + 1], :], nt)
        grad_inner = (here * slope[:, chunk]).astype(jnp.bfloat16)
        inner_ref[:, chunk] = grad_inner
        inner_sum_ref[:, chunk] += jnp.sum(grad_inner.astype(jnp.float32), axis=0, keepdims=True)
        grad_total = grad_total + mm(grad_inner, wi_ref[:, chunk], nt)
    sums_ref[0:1, :] += jnp.sum(grad_total * hat_one, axis=0, keepdims=True)
    sums_ref[1:2, :] += jnp.sum(grad_total, axis=0, keepdims=True)
    residual = norm_back(grad_total * gain_one, hat_one, inverse_one)
    residual_ref[...] = residual
    attended = residual.astype(jnp.bfloat16)
    attended_ref[...] = attended
    dmix_ref[...] = mm(attended, wo_ref[...], nt).astype(jnp.bfloat16)


def token_layer(x, mix, cot, w_out, w_inner, w_outer, bias_inner, rows):
    count = x.shape[0]
    hidden = w_inner.shape[1]
    tile = lambda lanes: pl.BlockSpec((TOKENS, lanes), lambda i: (i, 0))
    once = lambda a, b: pl.BlockSpec((a, b), lambda i: (0, 0), pipeline_mode=pl.Buffered(1))
    sums = lambda a, b: pl.BlockSpec((a, b), lambda i: (0, 0))
    low = lambda lanes: jax.ShapeDtypeStruct((count, lanes), jnp.bfloat16)
    return pl.pallas_call(
        token_kernel,
        grid=(count // TOKENS,),
        in_specs=[
            tile(D), tile(D), tile(D), once(D, D), once(D, hidden), once(hidden, D),
            once(1, hidden), once(8, D),
        ],
        out_specs=[
            tile(D), tile(hidden), tile(D), tile(hidden), tile(D), tile(D), tile(D), tile(D),
            sums(8, D), sums(1, hidden),
        ],
        out_shape=[
            low(D), low(hidden), low(D), low(hidden), low(D), low(D), low(D),
            jax.ShapeDtypeStruct((count, D), jnp.float32),
            jax.ShapeDtypeStruct((8, D), jnp.float32),
            jax.ShapeDtypeStruct((1, hidden), jnp.float32),
        ],
        scratch_shapes=[pltpu.VMEM((TOKENS, hidden), jnp.float32)],
        compiler_params=pltpu.CompilerParams(
            dimension_semantics=("arbitrary",), vmem_limit_bytes=VMEM_BYTES
        ),
        cost_estimate=pl.CostEstimate(
            flops=22000000000, transcendentals=6000000, bytes_accessed=40000000
        ),
        name="token_layer",
    )(x, mix, cot, w_out, w_inner, w_outer, bias_inner, rows)


def chip_bits():
    bits = []
    bit = 2
    while bit < lax.axis_size("batch"):
        bits.append(bit)
        bit *= 2
    return bits


def digit(bit):
    return lax.axis_index("batch") // bit % 2


def across(tensor, bits):
    count = lax.axis_size("batch")
    return lax.ppermute(tensor, "batch", [(i, i ^ bits[i & 1]) for i in range(count)])


def own_digit(bits):
    return jnp.where(digit(1) == 1, digit(bits[1]), digit(bits[0]))


def along(tensor, shift):
    ring = lax.axis_size("mem")
    return lax.ppermute(tensor, "mem", [(i, (i + shift) % ring) for i in range(ring)])


def rows_of(tensor, start, count):
    return lax.dynamic_slice(tensor, (start, 0), (count, tensor.shape[1]))


class Sum:
    def __init__(self, tensor):
        bits = chip_bits()
        self.bits = [(1, 1)] + list(zip(bits, bits[::-1]))
        self.state = tensor
        self.at = 0
        self.stages = 2 * len(self.bits) + 2

    def step(self):
        count, tensor = len(self.bits), self.state
        ring, me = lax.axis_size("mem"), lax.axis_index("mem")
        if self.at < count:
            bit = self.bits[self.at]
            half = tensor.shape[0] // 2
            mine = own_digit(bit)
            got = across(rows_of(tensor, (1 - mine) * half, half), bit)
            kept = rows_of(tensor, mine * half, half)
            self.state = (kept.astype(jnp.float32) + got.astype(jnp.float32)).astype(jnp.bfloat16)
        elif self.at == count:
            block = tensor.shape[0] // ring
            total = rows_of(tensor, me * block, block).astype(jnp.float32)
            for shift in range(1, ring):
                sent = rows_of(tensor, (me + shift) % ring * block, block)
                total = total + along(sent, shift).astype(jnp.float32)
            self.state = total.astype(jnp.bfloat16)
        elif self.at == count + 1:
            parts = [tensor] + [along(tensor, shift) for shift in range(1, ring)]
            self.state = jnp.concatenate(parts, axis=0)
        else:
            bit = self.bits[2 * count + 1 - self.at]
            self.state = jnp.concatenate([tensor, across(tensor, bit)], axis=0)
        self.at += 1

    def places(self):
        ring = lax.axis_size("mem")
        weight = ring * lax.axis_size("batch") // 2
        index = jnp.arange(2 * weight, dtype=jnp.int32)
        place = (lax.axis_index("mem") - index % ring) % ring
        core = index // weight % 2
        for even, odd in self.bits:
            own = jnp.where(core == 1, digit(odd), digit(even))
            place = place + (index // weight % 2 + own) % 2 * weight
            weight //= 2
        return place


def together(active, tree):
    states, tree = lax.optimization_barrier(([item.state for item in active], tree))
    for item, state in zip(active, states):
        item.state = state
    return tree


def placed(item):
    tensor, place = item.state, item.places()
    blocks = place.shape[0]
    if tensor.shape[0] // blocks % 8:
        tensor = tensor.reshape(blocks, -1, tensor.shape[1])[place].reshape(tensor.shape)
        place = jnp.arange(8, dtype=jnp.int32)
    return tensor, place


def block_of(place_ref, in_ref, index):
    rows = in_ref.shape[0] // place_ref.shape[0]
    start = pl.multiple_of(place_ref[index] * rows, 8)
    return in_ref[pl.ds(start, rows), :].astype(jnp.float32)


def settle_pairs_kernel(count, place_ref, in_ref, *rest):
    outs, full = rest[-6:-1], rest[-1]
    rows = in_ref.shape[0] // place_ref.shape[0]

    @pl.when(pl.program_id(0) == 0)
    def _():
        for item in range(place_ref.shape[0]):
            full[item * rows : (item + 1) * rows, :] = block_of(place_ref, in_ref, item)
        grads = count * 4 * PAIR
        outs[4][...] = full[grads : grads + outs[4].shape[0], :]

    for index in range(4):
        start = pl.multiple_of((pl.program_id(0) * 4 + index) * PAIR, PAIR)
        outs[index][...] = full[pl.ds(start, PAIR), :].T


def settle_pairs(item, first, count, earlier, after):
    tensor, place = placed(item)
    rows, lanes = tensor.shape
    square = jax.ShapeDtypeStruct((D, D), jnp.float32)
    return pl.pallas_call(
        functools.partial(settle_pairs_kernel, count),
        grid_spec=pltpu.PrefetchScalarGridSpec(
            num_scalar_prefetch=1,
            grid=(count,),
            in_specs=[pl.BlockSpec((rows, lanes), lambda i, p: (0, 0))]
            + [pl.BlockSpec(memory_space=pl.ANY)] * len(earlier),
            out_specs=[pl.BlockSpec((lanes, PAIR), lambda i, p: (0, first + i))] * 4
            + [pl.BlockSpec((after, lanes), lambda i, p: (0, 0))],
            scratch_shapes=[pltpu.VMEM((rows, lanes), jnp.float32)],
        ),
        out_shape=[square] * 4 + [jax.ShapeDtypeStruct((after, lanes), jnp.float32)],
        input_output_aliases={2 + index: index for index in range(len(earlier))},
        compiler_params=pltpu.CompilerParams(vmem_limit_bytes=48 * 1024 * 1024),
        name="settle_pairs",
    )(place, tensor, *earlier)


def sinusoid():
    fine_count = 32
    frequency = 1.0 / 10000.0 ** (
        jnp.arange(0, D, 2, dtype=jnp.int32).astype(jnp.float32) / D
    )
    coarse = (KEYS - 1 - fine_count * jnp.arange(REL // fine_count, dtype=jnp.int32)).astype(
        jnp.float32
    )[:, None] * frequency[None]
    fine = jnp.arange(fine_count, dtype=jnp.int32).astype(jnp.float32)[:, None] * frequency[None]
    sin_coarse, cos_coarse = jnp.sin(coarse)[:, None], jnp.cos(coarse)[:, None]
    sin_fine, cos_fine = jnp.sin(fine)[None], jnp.cos(fine)[None]
    sine = sin_coarse * cos_fine - cos_coarse * sin_fine
    cosine = cos_coarse * cos_fine + sin_coarse * sin_fine
    return jnp.concatenate([sine, cosine], axis=-1).reshape(REL, D).astype(jnp.bfloat16)


EXTRA = 256
FIRST = 3
VECTORS = 24


WIDE = 1024


def widen_kernel(outer_ref, inner_ref, outer_out, inner_out):
    outer_out[...] = outer_ref[...].astype(jnp.float32).T
    inner_out[...] = inner_ref[...].astype(jnp.float32)


def widen(outer, inner):
    hidden = inner.shape[1]
    return pl.pallas_call(
        widen_kernel,
        grid=(hidden // WIDE,),
        in_specs=[
            pl.BlockSpec((D, WIDE), lambda i: (0, i)),
            pl.BlockSpec((D, WIDE), lambda i: (0, i)),
        ],
        out_specs=[
            pl.BlockSpec((WIDE, D), lambda i: (i, 0)),
            pl.BlockSpec((D, WIDE), lambda i: (0, i)),
        ],
        out_shape=[
            jax.ShapeDtypeStruct((hidden, D), jnp.float32),
            jax.ShapeDtypeStruct((D, hidden), jnp.float32),
        ],
        compiler_params=pltpu.CompilerParams(vmem_limit_bytes=VMEM_BYTES),
        name="widen",
    )(outer, inner)


def shards(
    content_in, query_in, memory, sequence_lengths, order_rank, segment_ids,
    w_query, w_key, w_value, w_out, w_rel,
    bias_content, bias_position, bias_segment, segment_embed,
    gain_one, shift_one, w_inner, bias_inner, w_outer, bias_outer, gain_two, shift_two,
    content_cotangent, query_cotangent,
):
    wide = lambda tensor: tensor.astype(jnp.float32)
    low = lambda tensor: tensor.astype(jnp.bfloat16)
    both = ("batch", "mem")
    past = lax.all_to_all(memory, "mem", split_axis=0, concat_axis=1, tiled=True)[0]
    content = content_in[0]
    inputs = jnp.concatenate([content, query_in[0]], axis=0)
    cotangent = jnp.concatenate([content_cotangent[0], query_cotangent[0]], axis=0)
    positions = sinusoid()
    relative = low(mm(positions, w_rel, nn))
    frame = jnp.concatenate([past, content], axis=0)
    keys = low(mm(frame, w_key, nn))
    values = low(mm(frame, w_value, nn))
    projected = mm(inputs, w_query, nn)
    query_content = low(projected + wide(bias_content))
    query_position = low(projected + wide(bias_position))
    query_segment = low(projected + wide(bias_segment))
    mixture, inverse, probs = attention_forward(
        sequence_lengths, query_content, query_position, query_segment, keys, values, relative,
        segment_embed, segment_ids, order_rank,
    )
    rows = jnp.stack(
        [wide(t) for t in (gain_one, shift_one, gain_two, shift_two, bias_outer)]
        + [jnp.zeros((D,), jnp.float32)] * 3
    )
    (
        final_out, active_low, grad_outer_low, grad_inner_low, grad_attended, grad_mixture,
        normed_low, grad_residual, token_sums, inner_bias_sum,
    ) = token_layer(
        inputs, mixture, cotangent, w_out, w_inner, w_outer, wide(bias_inner)[None], rows
    )
    low_mm = lambda left, right: low(mm(left, right, tn))
    grad_outer_w = low_mm(grad_outer_low, active_low)
    grad_inner_w = low_mm(normed_low, grad_inner_low)
    grad_outer_w, grad_inner_w, grad_mixture, grad_attended = lax.optimization_barrier(
        (grad_outer_w, grad_inner_w, grad_mixture, grad_attended)
    )
    outer_sum, inner_sum = lax.psum((grad_outer_w, grad_inner_w), both)

    def attention_part(operands):
        (
            probs, grad_mixture, mixture, inverse, query_content, query_position, query_segment,
            keys, values, relative, segment_ids, inputs, frame, positions, grad_attended,
            token_sums, inner_bias_sum, segment_embed, grad_residual, w_query, w_key, w_value, final_out,
        ) = operands
        common = (
            mixture, inverse, query_content, query_position, query_segment, keys, values, relative,
            segment_embed, segment_ids, inputs, frame, positions,
        )
        rows_of_pairs = lambda count: count * 4 * PAIR
        half, other = FIRST, PAIRS - FIRST
        chain = attention_backward(
            0, half, 0, [None] * 4 + [rows_of_pairs(half) + D], probs, grad_mixture, *common
        )
        early = Sum(lax.dynamic_update_slice(chain[4], low_mm(mixture, grad_attended), (rows_of_pairs(half), 0)))
        early.step()
        chain, grad_mixture = together([early], (list(chain[:4]), grad_mixture))
        early.step()
        chain = attention_backward(
            half, other, 0, chain + [rows_of_pairs(other) + EXTRA], probs, grad_mixture, *common
        )
        grad_projected, grad_keys, grad_values, small, bucket = together([early], list(chain))
        vectors = jnp.concatenate(
            [token_sums, inner_bias_sum.reshape(-1, D), jnp.zeros((4, D), jnp.float32), small], axis=0
        )
        vectors = jnp.pad(vectors, ((0, EXTRA - vectors.shape[0]), (0, 0)))
        late = Sum(lax.dynamic_update_slice(bucket, low(vectors), (rows_of_pairs(other), 0)))
        while late.at < late.stages:
            late.step()
            if early.at < early.stages:
                early.step()
                together([late, early], ())
                if early.at == early.stages:
                    *sums, out_sum = settle_pairs(early, 0, half, (), D)
                    sums, out_sum = together([late], (sums, out_sum))
        *sums, vectors = settle_pairs(late, half, other, sums, VECTORS)
        vectors = [vectors[index] for index in (16, 17, 18)] + [vectors[19:21]] + [
            vectors[index] for index in (0, 1, 4, 2, 3)
        ] + [vectors[8:12].reshape(-1)]
        finals = (final_out[None, :SEG], final_out[None, SEG:])
        grad_inputs = grad_residual + mm(grad_projected, w_query, nt)
        grad_content = (
            grad_inputs[:SEG] + mm(grad_keys[MEM:], w_key, nt) + mm(grad_values[MEM:], w_value, nt)
        )
        return low(grad_content), low(grad_inputs[SEG:]), sums, out_sum, vectors, finals

    operands = (
        probs, grad_mixture, mixture, inverse, query_content, query_position, query_segment, keys,
        values, relative, segment_ids, inputs, frame, positions, grad_attended, token_sums,
        inner_bias_sum, segment_embed, grad_residual, w_query, w_key, w_value, final_out,
    )
    shapes = jax.eval_shape(attention_part, operands)
    grad_content, grad_query, sums, out_sum, vectors, finals = lax.cond(
        sequence_lengths[0] > -1,
        attention_part,
        lambda operands: jax.tree.map(lambda item: jnp.zeros(item.shape, item.dtype), shapes),
        operands,
    )
    query_sum, key_sum, value_sum, rel_sum = sums
    outer_sum, inner_sum = widen(outer_sum, inner_sum)
    content_sum, position_sum, segment_sum, embed_sum, gain1, shift1, bias, gain2, shift2, hidden = vectors
    return (
        *finals, grad_content[None], grad_query[None],
        query_sum, key_sum, value_sum, out_sum, rel_sum,
        content_sum, position_sum, segment_sum, embed_sum, gain1, shift1, inner_sum, hidden,
        outer_sum, bias, gain2, shift2,
    )


def solution(mesh):
    both = ("batch", "mem")
    rows = P(both, None, None)
    return jax.shard_map(
        shards,
        mesh=mesh,
        in_specs=(rows, rows, P("batch", "mem", None), P(both), P(both, None), P(both, None))
        + (P(),) * 17
        + (rows, rows),
        out_specs=(rows,) * 4 + (P(),) * 17,
        check_vma=False,
    )
```
